32 devices in a mesh: qr: 4 (over z), qc: 4 (over x, core), grp: 2 (over y).
Axes of the slice: x: 2, y: 2, z: 4, core: 2. Of those that a mesh axis runs over, the one named last changes fastest.
Arguments:
- kohn_sham: bfloat16 [1536, 1536], P('qr', 'qc'), may hold values from -1 to 1, as said below
- pattern: int32 [24, 24], P('qr', 'qc'), may hold values from 0 to 1, as said below
- basis_centers: float32 [3, 1536], P(None, 'qr'), may hold values from 0 to 6.8
- occupations: float32 [1536], P('qr'), may hold values from 0.05 to 0.5
- atoms: float32 [4, 4, 4, 2, 1024], P(None, 'qr', 'qc', 'grp'), may hold values from -1.2 to 3.4, as said below
- neighbours: int32 [4, 4, 2, 2, 64, 1024], P('qr', 'qc', 'grp'), may hold values from 0 to 1023, as said below
- emb_atom: int32 [8192], P(('qr', 'qc', 'grp')), may hold values from 0 to 1023
- emb_dest: int32 [8192, 1], P(('qr', 'qc', 'grp')), may hold values from 0 to 3; in each aligned block of 256 rows (0 to 255, 256 to 511, ...) at most 96 rows name the same one
- emb_block: int32 [8192], P(('qr', 'qc', 'grp')), may hold values from 0 to 5
Outputs:
- sign_step: bfloat16 [1536, 1536], P(('qr', 'grp'), 'qc')
- forces: float32 [3, 4, 4, 2, 1024], P(None, 'qr', 'qc', 'grp')
The draws below stay inside these ranges and needn't reach their ends.
Inputs may be any that keep to these rules, and one draw needn't show every extreme that they name: `kohn_sham`: zero outside the blocks that pattern marks. `pattern`: 1 on every diagonal block. `atoms`: rows 0 to 2 lie in the domain's box of edge 3.4; row 3 holds charges. `neighbours`: entry 0 of the fourth dimension is a slot, 0 to 26; entry 1 an atom of that domain. `emb_dest`: among the 256 records of one domain at most 96 name the same tile row.
All inputs are finite; a program needn't handle non-finite values.
Results may differ from the reference program's by a relative error of at most 0.012.
Values may be sent and summed in bfloat16 or wider, within the bound.
No kernel may reach another device: no remote copies, remote signals or barrier semaphores. Data moves between devices by JAX's collectives and lax.ppermute only.
A program may use at most 128 MiB of HBM per device.

```python
import math
import jax
import jax.numpy as jnp
import numpy as np
from jax import lax

BLOCK = 64
TILE_BLOCKS = 6
ATOMS = 1024
NEIGH = 64
RECORDS = 256
CAPACITY = 96
TILE = 384
ORDER = 1536
BLOCKS = 24
N_QR = 4
N_QC = 4
N_GRP = 2
DEVICES = 32


domain_edge = 3.4


def pattern_bits(key):
    inner_key = jax.random.fold_in(key, 17)
    coins = jax.random.randint(inner_key, (BLOCKS, BLOCKS), 0, 5)
    rows = jnp.arange(BLOCKS)[:, None]
    columns = jnp.arange(BLOCKS)[None, :]
    near_band = jnp.abs(rows - columns) <= 1
    return jnp.where(near_band, 1, jnp.where(coins == 0, 1, 0)).astype(jnp.int32)


def draw_pattern(key, part):
    return pattern_bits(key)


def draw_kohn_sham(key, part):
    block_mask = pattern_bits(key)
    full_mask = jnp.repeat(jnp.repeat(block_mask, BLOCK, axis=0), BLOCK, axis=1).astype(jnp.float32)
    key_one, key_two, key_three = jax.random.split(jax.random.fold_in(key, 29), 3)
    spread_level = 0.7 * (ORDER * 0.22 + 2.0 * BLOCK) ** (-0.5)
    noise_part = jnp.clip(jax.random.normal(key_one, (ORDER, ORDER)), -5.0, 5.0)
    magnitude = jax.random.uniform(key_two, (ORDER,), minval=0.3, maxval=0.9)
    coin_flip = jax.random.uniform(jax.random.fold_in(key_two, 3), (ORDER,))
    diagonal_values = jnp.where(coin_flip < 0.5, -magnitude, magnitude)
    identity = jnp.eye(ORDER, dtype=jnp.float32)
    matrix = full_mask * (1.0 - identity) * noise_part * spread_level + identity * diagonal_values[None, :]
    return matrix.astype(jnp.bfloat16)


def draw_atoms(key, part):
    key_one, key_two = jax.random.split(jax.random.fold_in(key, 41), 2)
    layout = (N_QR, N_QC, N_GRP, ATOMS)
    located = jax.random.uniform(key_one, (3,) + layout, minval=0.0, maxval=domain_edge)
    charges = jnp.clip(0.3 * jax.random.normal(key_two, (1,) + layout), -1.2, 1.2)
    return jnp.concatenate([located, charges], axis=0).astype(jnp.float32)


def draw_neighbours(key, part):
    key_one, key_two = jax.random.split(jax.random.fold_in(key, 53), 2)
    layout = (N_QR, N_QC, N_GRP, 1, NEIGH, ATOMS)
    slots = jax.random.randint(key_one, layout, 0, 27)
    members = jax.random.randint(key_two, layout, 0, ATOMS)
    return jnp.concatenate([slots, members], axis=3).astype(jnp.int32)


def with_ends(values, stream_key, low, largest):
    longest = values.shape.index(max(values.shape))
    spots = []
    for shift in (0, 1):
        where = [jax.random.randint(jax.random.fold_in(stream_key, axis), (), 0, length) for axis, length in enumerate(values.shape)]
        where[longest] = (where[longest] + shift) % values.shape[longest]
        spots.append(tuple(where))
    return values.at[spots[0]].set(low).at[spots[1]].set(largest)


def shard_levels(own_key, dims, cuts, smallest, high):
    loudness, own = 1.0, jax.random.fold_in(own_key, 6)
    for dim, parts in cuts:
        heights = jnp.exp(jax.random.uniform(jax.random.fold_in(own, dim), (parts,), jnp.float32, smallest / len(cuts), high / len(cuts)))
        loudness = loudness * jnp.repeat(heights, dims[dim] // parts).reshape([-1 if axis == dim else 1 for axis in range(len(dims))])
    return loudness


def deal_out(stream_key, own, number, rows, amount, top, most, lean):
    sequence = jax.random.permutation(stream_key, amount)
    crowded, common = load_shares(amount, rows * top, most, lean, True), load_shares(amount, rows * top, most, lean, False)
    places = jnp.arange(amount)

    def named(lengths, rotation):
        used = int((lengths > 0).sum())
        fixed = max(1, used // 4)
        moved = fixed + (places - fixed + rotation * (used - fixed)) % max(1, amount - fixed)
        return jnp.zeros((amount,), jnp.int32).at[sequence[jnp.where(places < fixed, places, moved)]].set(jnp.asarray(lengths, jnp.int32))

    lengths = jnp.where(number % 4 == 0, named(crowded, number // 4), named(common, number - number // 4 - 1))
    mixed = jax.random.permutation(jax.random.fold_in(own, 3), amount)
    giver, receiver = mixed[0:amount // 2 * 2:2], mixed[1:amount // 2 * 2:2]
    slack = jnp.minimum(lengths[giver] - 1, most - lengths[receiver]) // 2
    slack = jnp.where((giver == sequence[0]) | (receiver == sequence[0]) | (lengths[receiver] == 0), 0, jnp.maximum(slack, 0))
    moved = jax.random.randint(jax.random.fold_in(own, 4), (amount // 2,), 0, 1 << 20) % (slack + 1)
    lengths = lengths.at[giver].add(-moved).at[receiver].add(moved)
    labels = jnp.searchsorted(jnp.cumsum(lengths), jnp.arange(rows * top), side="right").astype(jnp.int32)
    listing = labels.reshape(top, rows).T
    listing = listing[jax.random.permutation(jax.random.fold_in(own, 1), rows)]
    rotation = jax.random.randint(jax.random.fold_in(own, 2), (rows, 1), 0, top)
    return jnp.take_along_axis(listing, (jnp.arange(top)[None, :] + rotation) % top, axis=1)


def load_shares(count, total, reach, skew, full):
    portions = [(1 << 20) // math.isqrt(standing ** skew) + 1 for standing in range(1, count + 1)]
    largest = reach if full else min(reach, max(-(-total // count), total * portions[0] // sum(portions)))
    least = 1 if total - largest >= count - 1 else 0
    counts, surplus = [largest] + [least] * (count - 1), total - largest - least * (count - 1)
    while surplus > 0:
        candidates = [i for i in range(1, count) if counts[i] < largest] or [i for i in range(1, count) if counts[i] < reach]
        mass, left = sum([portions[i] for i in candidates]), surplus
        for i in candidates:
            addition = min(reach - counts[i], max(1, left * portions[i] // mass), surplus)
            counts[i] = counts[i] + addition
            surplus = surplus - addition
    return np.array(counts)


def setup_inputs(seed: int = 0) -> dict:
    splits = jax.random.split(jax.random.key(seed), 10)
    kohn_sham = draw_kohn_sham(jax.random.fold_in(splits[9], 71), 0)
    pattern = draw_pattern(jax.random.fold_in(splits[9], 71), 0)
    basis_centers = jnp.clip(6.8 * jax.random.uniform(splits[2], (3, ORDER), jnp.float32) ** shard_levels(splits[2], (3, ORDER), ((1, 4),), -0.2, 0.2), 0.0, 6.8)
    occupations = jnp.clip(0.05 + 0.45 * jax.random.uniform(splits[3], (ORDER,), jnp.float32) ** shard_levels(splits[3], (ORDER,), ((0, 4),), -0.2, 0.2), 0.05, 0.5)
    atoms = draw_atoms(jax.random.fold_in(splits[9], 71), 0)
    neighbours = draw_neighbours(jax.random.fold_in(splits[9], 71), 0)
    emb_atom = with_ends(jax.random.randint(splits[6], (RECORDS * DEVICES,), 0, ATOMS), jax.random.fold_in(splits[6], 1), 0, ATOMS - 1).astype(jnp.int32)
    emb_dest_keys = jax.random.split(jax.random.fold_in(splits[7], 1), (RECORDS * DEVICES) // RECORDS)
    emb_dest_turns = jax.random.permutation(jax.random.fold_in(splits[7], 3), (RECORDS * DEVICES) // RECORDS)
    emb_dest = jax.vmap(lambda own, number: deal_out(jax.random.fold_in(splits[7], 2), own, number, RECORDS, N_QR, 1, CAPACITY, 2))(emb_dest_keys, emb_dest_turns).reshape((RECORDS * DEVICES, 1))
    emb_block = with_ends(jax.random.randint(splits[8], (RECORDS * DEVICES,), 0, TILE_BLOCKS), jax.random.fold_in(splits[8], 1), 0, TILE_BLOCKS - 1).astype(jnp.int32)
    return dict(kohn_sham=kohn_sham, pattern=pattern, basis_centers=basis_centers, occupations=occupations, atoms=atoms, neighbours=neighbours, emb_atom=emb_atom, emb_dest=emb_dest, emb_block=emb_block)


coulomb = 138.935
hartree_nm = 0.0529177
soften = 0.01
domain_edge = 3.4

def pair_terms(own_atoms, nearby, index_list):
    taken = nearby[:, index_list]
    offset = own_atoms[:3, None, :] - taken[:3]
    distance = lax.optimization_barrier(jnp.sum(offset * offset, axis=0)) + soften
    strength = coulomb * own_atoms[3][None, :] * taken[3] / (distance * jnp.sqrt(distance))
    return lax.optimization_barrier(jnp.sum(offset * strength[None], axis=1))

def domain_coords(domain):
    plane_size = N_QC * N_GRP
    return (domain // plane_size, domain // N_GRP % N_QC, domain % N_GRP)

def neighbourhood(flat_atoms, domain):
    first_axis, second_axis, third_axis = domain_coords(domain)
    places = jnp.arange(27, dtype=jnp.int32)
    step_one = places // 9 - 1
    step_two = places // 3 % 3 - 1
    step_three = places % 3 - 1
    others = (first_axis + step_one) % N_QR * (N_QC * N_GRP) + (second_axis + step_two) % N_QC * N_GRP + (third_axis + step_three) % N_GRP
    gathered = flat_atoms[:, others, :]
    displace = jnp.stack([step_one, step_two, step_three]).astype(jnp.float32) * domain_edge
    located = gathered[:3] + displace[:, :, None]
    return jnp.concatenate([located, gathered[3:]], axis=0).reshape(4, 27 * ATOMS)

def reference(kohn_sham, pattern, basis_centers, occupations, atoms, neighbours, emb_atom, emb_dest, emb_block):
    flat_atoms = atoms.reshape(4, DEVICES, ATOMS)
    lists = neighbours.reshape(DEVICES, 2, NEIGH, ATOMS)

    def domain_force(domain):
        index_list = (lists[domain, 0] * ATOMS + lists[domain, 1]).astype(jnp.int32)
        return pair_terms(flat_atoms[:, domain, :], neighbourhood(flat_atoms, domain), index_list)
    pair_force = lax.map(domain_force, jnp.arange(DEVICES, dtype=jnp.int32))
    pair_force = jnp.transpose(pair_force, (1, 0, 2))
    owners = jnp.arange(RECORDS * DEVICES, dtype=jnp.int32) // RECORDS
    first_axis, second_axis, third_axis = domain_coords(owners)
    anchor = jnp.stack([first_axis, second_axis, third_axis]).astype(jnp.float32) * domain_edge
    atom_index = (owners * ATOMS + emb_atom).astype(jnp.int32)
    all_atoms = flat_atoms.reshape(4, DEVICES * ATOMS)
    record_place = all_atoms[:3, atom_index] + anchor
    record_charge = all_atoms[3, atom_index]
    block_index = (emb_dest[:, 0] * TILE_BLOCKS + emb_block).astype(jnp.int32)
    centers = basis_centers.reshape(3, BLOCKS, BLOCK)[:, block_index, :]
    weights = occupations.reshape(BLOCKS, BLOCK)[block_index]
    offset = record_place[:, :, None] - centers
    distance = lax.optimization_barrier(jnp.sum(offset * offset, axis=0)) + soften
    root_distance = jnp.sqrt(distance)
    potential_terms = hartree_nm * record_charge[:, None] / root_distance
    potential = jnp.zeros((BLOCKS, BLOCK), jnp.float32).at[block_index].add(potential_terms).reshape(ORDER)
    record_force = coulomb * record_charge[None, :] * lax.optimization_barrier(jnp.sum(weights[None] * offset / (distance * root_distance)[None], axis=2))
    embed_force = jnp.zeros((3, DEVICES * ATOMS), jnp.float32).at[:, atom_index].add(record_force)
    forces = (pair_force + embed_force.reshape(3, DEVICES, ATOMS)).reshape(3, N_QR, N_QC, N_GRP, ATOMS)
    shifted = (kohn_sham.astype(jnp.float32) + jnp.diag(potential)).astype(jnp.bfloat16)
    pattern_full = jnp.repeat(jnp.repeat(pattern, BLOCK, axis=0), BLOCK, axis=1) == 1
    slice_width = TILE // N_GRP

    def split_product(left_matrix, right_matrix):
        left_parts = left_matrix.reshape(ORDER, N_QR, N_GRP, slice_width)
        right_parts = right_matrix.reshape(N_QR, N_GRP, slice_width, ORDER)
        summed = jnp.zeros((ORDER, ORDER), jnp.float32)
        for layer_index in range(N_GRP):
            left_piece = left_parts[:, :, layer_index, :].reshape(ORDER, N_QR * slice_width)
            right_piece = right_parts[:, layer_index].reshape(N_QR * slice_width, ORDER)
            partial_value = jnp.where(pattern_full, jnp.dot(left_piece, right_piece, preferred_element_type=jnp.float32), 0.0)
            rounded = lax.optimization_barrier(partial_value.astype(jnp.bfloat16))
            summed = summed + rounded.astype(jnp.float32)
        return summed
    square = split_product(shifted, shifted).astype(jnp.bfloat16)
    cube = split_product(shifted, square)
    sign_step = (0.5 * (3.0 * shifted.astype(jnp.float32) - cube)).astype(jnp.bfloat16)
    return (sign_step, forces)
```

```python
import functools

import jax
import jax.numpy as jnp
from jax import lax
from jax.experimental import pallas as pl
from jax.experimental.pallas import tpu as pltpu
from jax.sharding import PartitionSpec as P

BLOCK = 64
SUB, LANES = 8, 128

coulomb = 138.935
hartree_nm = 0.0529177
soften = 0.01
domain_edge = 3.4

ALL = ("qr", "qc", "grp")
VMEM = pltpu.MemorySpace.VMEM
SMEM = pltpu.MemorySpace.SMEM

LANE_PICK = lax.GatherDimensionNumbers(
    offset_dims=(),
    collapsed_slice_dims=(1,),
    start_index_map=(1,),
    operand_batching_dims=(0,),
    start_indices_batching_dims=(0,),
)


def pick_lanes(row, lane):
    return lax.gather(
        row, lane[..., None], LANE_PICK, (1, 1), mode=lax.GatherScatterMode.PROMISE_IN_BOUNDS
    )


def everyone(value, axes):
    count = 1
    for axis in (axes,) if isinstance(axes, str) else axes:
        count *= lax.axis_size(axis)
    copies = jnp.broadcast_to(value[None], (count,) + value.shape)
    return lax.all_to_all(copies, axes, split_axis=0, concat_axis=0, tiled=True)


def rotated(value, axis):
    count = lax.axis_size(axis)
    return [value] + [
        lax.ppermute(value, axis, [(i, (i + k) % count) for i in range(count)])
        for k in range(1, count)
    ]


def thirds(value):
    high = value.astype(jnp.bfloat16)
    rest = value - high.astype(jnp.float32)
    middle = rest.astype(jnp.bfloat16)
    low = (rest - middle.astype(jnp.float32)).astype(jnp.bfloat16)
    return high, middle, low


def records_kernel(
    anchor_ref, atoms_ref, pick_ref, block_ref, centers_ref, field_ref, force_ref
):
    atom_count = atoms_ref.shape[1]
    count = pick_ref.shape[1]
    blocks = centers_ref.shape[1]
    one_atom = (
        lax.broadcasted_iota(jnp.int32, (atom_count, count), 0) == pick_ref[...]
    ).astype(jnp.bfloat16)
    one_block = (
        lax.broadcasted_iota(jnp.int32, (blocks, count), 0) == block_ref[...]
    ).astype(jnp.bfloat16)

    def chosen_atoms(rows):
        pieces = [
            jnp.dot(piece, one_atom, preferred_element_type=jnp.float32) for piece in thirds(rows)
        ]
        return pieces[0] + pieces[1] + pieces[2]

    def chosen_centers(rows):
        pieces = [
            lax.dot_general(
                piece, one_block, (((0,), (0,)), ((), ())), preferred_element_type=jnp.float32
            )
            for piece in thirds(rows)
        ]
        return pieces[0] + pieces[1] + pieces[2]

    taken = chosen_atoms(atoms_ref[...])
    charge = taken[3:4]
    offset = [taken[c : c + 1] + anchor_ref[0, c] - chosen_centers(centers_ref[c]) for c in range(3)]
    weight = chosen_centers(centers_ref[3])
    distance = offset[0] * offset[0] + offset[1] * offset[1] + offset[2] * offset[2] + soften
    inverse = lax.rsqrt(distance)
    terms = hartree_nm * charge * inverse
    partial = jnp.zeros((blocks, BLOCK), jnp.float32)
    for piece in thirds(terms):
        partial = partial + lax.dot_general(
            one_block, piece, (((1,), (1,)), ((), ())), preferred_element_type=jnp.float32
        )
    field_ref[...] = partial
    strength = weight * (inverse * inverse * inverse)
    pushes = [
        coulomb * charge * jnp.sum(strength * offset[c], axis=0, keepdims=True) for c in range(3)
    ]
    pushes = jnp.concatenate(pushes + [jnp.zeros((5, count), jnp.float32)], axis=0)
    total = jnp.zeros((8, atom_count), jnp.float32)
    for piece in thirds(pushes):
        total = total + lax.dot_general(
            piece, one_atom, (((1,), (1,)), ((), ())), preferred_element_type=jnp.float32
        )
    force_ref[...] = total


def embedding(anchor, own, pick, block, centers):
    atom_count, count, blocks = own.shape[1], pick.shape[1], centers.shape[1]
    return pl.pallas_call(
        records_kernel,
        out_shape=(
            jax.ShapeDtypeStruct((blocks, BLOCK), jnp.float32),
            jax.ShapeDtypeStruct((8, atom_count), jnp.float32),
        ),
        in_specs=[pl.BlockSpec(memory_space=SMEM)] + [pl.BlockSpec(memory_space=VMEM)] * 4,
        out_specs=(pl.BlockSpec(memory_space=VMEM),) * 2,
        cost_estimate=pl.CostEstimate(flops=10**9, bytes_accessed=10**6, transcendentals=0),
        name="embedding",
    )(anchor, own, pick, block, centers)


def packing_kernel(ids_ref, near_ref, packed_ref, scale_ref):
    domains = packed_ref.shape[1] // SUB
    low = [near_ref[ids_ref[0], c] for c in range(4)]
    high = list(low)
    for d in range(1, domains):
        for c in range(4):
            value = near_ref[ids_ref[d], c]
            low[c] = jnp.minimum(low[c], value)
            high[c] = jnp.maximum(high[c], value)
    steps = 65535.0
    base, back, step = [], [], []
    for c in range(4):
        least = jnp.min(low[c], axis=(0, 1), keepdims=True)
        width = jnp.maximum(jnp.max(high[c], axis=(0, 1), keepdims=True) - least, 1e-30)
        base.append(jnp.broadcast_to(least, (SUB, LANES)))
        back.append(jnp.broadcast_to(steps / width, (SUB, LANES)))
        step.append(jnp.broadcast_to(width * (1.0 / steps), (SUB, LANES)))
        scale_ref[c] = base[c]
        scale_ref[4 + c] = step[c]
    for d in range(domains):
        code = [
            jnp.clip((near_ref[ids_ref[d], c] - base[c]) * back[c] + 0.5, 0.0, steps).astype(
                jnp.int32
            )
            for c in range(4)
        ]
        packed_ref[0, d * SUB : (d + 1) * SUB, :] = code[0] | (code[1] << 16)
        packed_ref[1, d * SUB : (d + 1) * SUB, :] = code[2] | (code[3] << 16)


def packing(ids, near):
    domains = ids.shape[0]
    return pl.pallas_call(
        packing_kernel,
        out_shape=(
            jax.ShapeDtypeStruct((2, domains * SUB, LANES), jnp.int32),
            jax.ShapeDtypeStruct((8, SUB, LANES), jnp.float32),
        ),
        in_specs=[pl.BlockSpec(memory_space=SMEM), pl.BlockSpec(memory_space=VMEM)],
        out_specs=(pl.BlockSpec(memory_space=VMEM),) * 2,
        cost_estimate=pl.CostEstimate(flops=10**7, bytes_accessed=10**6, transcendentals=0),
        name="packing",
    )(ids, near)


def compact(place, count):
    if count >= 3:
        return place
    if count == 2:
        return jnp.where(place == 1, 0, 1)
    return jnp.zeros_like(place)


def pair_kernel(counts, first, groups, lists_ref, own_ref, packed_ref, scale_ref, force_ref):
    rows = packed_ref.shape[1]
    parts = lists_ref.shape[1] // SUB
    distinct = [min(3, count) for count in counts]

    def group(a, _):
        column = pl.multiple_of((first + a) * LANES, LANES)
        mine = [
            jnp.broadcast_to(own_ref[c, pl.ds(first + a, 1), :], (SUB, LANES)) for c in range(4)
        ]

        def part(b, sums):
            start = pl.multiple_of(b * SUB, SUB)
            slot = lists_ref[0, pl.ds(start, SUB), pl.ds(column, LANES)]
            member = lists_ref[1, pl.ds(start, SUB), pl.ds(column, LANES)]
            p = (slot * 57) >> 9
            rest = slot - 9 * p
            q = (rest * 11) >> 5
            r = rest - 3 * q
            domain = (
                compact(p, counts[0]) * distinct[1] + compact(q, counts[1])
            ) * distinct[2] + compact(r, counts[2])
            row = domain * SUB + (member >> 7)
            lane = member & (LANES - 1)
            words = [jnp.zeros((SUB, LANES), jnp.int32) for _ in range(2)]
            for k in range(rows):
                here = row == k
                for w in range(2):
                    line = jnp.broadcast_to(packed_ref[w, k : k + 1, :], (SUB, LANES))
                    words[w] = jnp.where(here, pick_lanes(line, lane), words[w])
            code = [
                words[0] & 0xFFFF,
                (words[0] >> 16) & 0xFFFF,
                words[1] & 0xFFFF,
                (words[1] >> 16) & 0xFFFF,
            ]
            value = [code[c].astype(jnp.float32) * scale_ref[4 + c] + scale_ref[c] for c in range(4)]
            shift = [(place - 1).astype(jnp.float32) * domain_edge for place in (p, q, r)]
            offset = [mine[c] - (value[c] + shift[c]) for c in range(3)]
            distance = (
                offset[0] * offset[0] + offset[1] * offset[1] + offset[2] * offset[2] + soften
            )
            inverse = lax.rsqrt(distance)
            strength = value[3] * (inverse * inverse * inverse)
            return tuple(sums[c] + offset[c] * strength for c in range(3))

        zero = jnp.zeros((SUB, LANES), jnp.float32)
        sums = lax.fori_loop(0, parts, part, (zero, zero, zero))
        for c in range(3):
            force_ref[c, pl.ds(a, 1), :] = (
                coulomb * mine[3][:1] * jnp.sum(sums[c], axis=0, keepdims=True)
            )
        return 0

    lax.fori_loop(0, groups, group, 0)


def pair_forces(counts, first, groups, lists, own, packed, scale):
    return pl.pallas_call(
        functools.partial(pair_kernel, counts, first, groups),
        out_shape=jax.ShapeDtypeStruct((3, groups, LANES), jnp.float32),
        in_specs=[pl.BlockSpec(memory_space=VMEM)] * 4,
        out_specs=pl.BlockSpec(memory_space=VMEM),
        cost_estimate=pl.CostEstimate(
            flops=10**8 * groups, bytes_accessed=10**6, transcendentals=0
        ),
        name="pairs",
    )(lists, own, packed, scale)


def neighbourhood(block):
    counts = tuple(lax.axis_size(axis) for axis in ALL)
    here = [lax.axis_index(axis) for axis in ALL]
    reach = []
    for count in counts:
        reach.append((-1, 0, 1) if count >= 3 else (0, 1) if count == 2 else (0,))
    total = counts[0] * counts[1] * counts[2]
    if total <= 64:
        near = everyone(block, ALL)
        ids = [
            (((here[0] + i) % counts[0]) * counts[1] + (here[1] + j) % counts[1]) * counts[2]
            + (here[2] + k) % counts[2]
            for i in reach[0]
            for j in reach[1]
            for k in reach[2]
        ]
        return near, jnp.stack(ids).astype(jnp.int32)
    near = block[None]
    for axis, count in reversed(tuple(zip(ALL, counts))):
        ahead = [((i + 1) % count, i) for i in range(count)]
        behind = [(i, (i + 1) % count) for i in range(count)]
        if count >= 3:
            near = jnp.concatenate(
                [lax.ppermute(near, axis, behind), near, lax.ppermute(near, axis, ahead)], axis=0
            )
        elif count == 2:
            near = jnp.concatenate([near, lax.ppermute(near, axis, ahead)], axis=0)
    return near, jnp.arange(near.shape[0], dtype=jnp.int32)


def per_device(
    kohn_sham, pattern, basis_centers, occupations, atoms, neighbours, emb_atom, emb_dest, emb_block
):
    counts = tuple(lax.axis_size(axis) for axis in ALL)
    extent, layers = counts[0], counts[2]
    grid_row = lax.axis_index("qr")
    grid_column = lax.axis_index("qc")
    layer = lax.axis_index("grp")
    order = kohn_sham.shape[0]
    width = order // layers
    tile_blocks = order // BLOCK
    atom_count = atoms.shape[4]
    record_count = emb_atom.shape[0]

    basis = jnp.concatenate([basis_centers, occupations[None]], axis=0)
    basis_all = everyone(basis, "qr")
    centers = (
        jnp.transpose(basis_all.reshape(extent, 4, tile_blocks, BLOCK), (1, 0, 2, 3))
    ).reshape(4, extent * tile_blocks, BLOCK)

    first = layer * width
    left_own = lax.dynamic_slice_in_dim(kohn_sham, first, width, 1)
    right_own = lax.dynamic_slice_in_dim(kohn_sham, first, width, 0)
    left = everyone(left_own, "qc")
    rights = rotated(right_own, "qr")

    near, ids = neighbourhood(atoms.reshape(4, SUB, atom_count // SUB))

    anchor = (
        jnp.stack([grid_row, grid_column, layer]).astype(jnp.float32)[None] * domain_edge
    )
    field, embed_force = embedding(
        anchor,
        atoms.reshape(4, atom_count),
        emb_atom[None],
        (emb_dest[:, 0] * tile_blocks + emb_block)[None],
        centers,
    )
    field_all = everyone(field.reshape(extent * order), ALL)
    potential = jnp.sum(field_all, axis=0).reshape(extent, order)

    keep = jnp.repeat(jnp.repeat(pattern, BLOCK, axis=0), BLOCK, axis=1) == 1
    behind = [(grid_row - k) % extent for k in range(extent)]
    lefts = [lax.dynamic_index_in_dim(left, tile, 0, keepdims=False) for tile in behind]

    def swap_layers(part):
        wide = part.reshape(layers, width, order)
        mine = lax.dynamic_index_in_dim(wide, layer, 0, keepdims=False)
        got = lax.all_to_all(
            wide.astype(jnp.bfloat16), "grp", split_axis=0, concat_axis=0, tiled=True
        )
        other = jnp.arange(layers)[:, None, None] != layer
        return mine + jnp.sum(jnp.where(other, got.astype(jnp.float32), 0.0), axis=0)

    product = jnp.zeros((order, order), jnp.float32)
    for k in range(extent):
        product = product + jnp.dot(lefts[k], rights[k], preferred_element_type=jnp.float32)
    product = jnp.where(keep, product, 0.0)
    product_rows = swap_layers(product).astype(jnp.bfloat16)
    products = rotated(product_rows, "qr")

    own_column = lax.dynamic_index_in_dim(potential, grid_column, 0, keepdims=False)
    rows_at = jnp.arange(width)[:, None] + first
    columns_at = jnp.arange(order)[None, :]
    cube = jnp.zeros((order, order), jnp.float32)
    for k in range(extent):
        tile = behind[k]
        row_field = lax.dynamic_slice_in_dim(
            lax.dynamic_index_in_dim(potential, tile, 0, keepdims=False), first, width, 0
        )
        matrix = rights[k].astype(jnp.float32)
        diagonal = (rows_at == columns_at) & (tile == grid_column)
        square = (
            products[k].astype(jnp.float32)
            + matrix * (row_field[:, None] + own_column[None, :])
            + jnp.where(diagonal, row_field[:, None] * row_field[:, None], 0.0)
        ).astype(jnp.bfloat16)
        operand = lefts[k]
        if k == 0:
            on_diagonal = jnp.arange(order)[:, None] == jnp.arange(width)[None, :] + first
            operand = (
                operand.astype(jnp.float32) + jnp.where(on_diagonal, row_field[None, :], 0.0)
            ).astype(jnp.bfloat16)
        cube = cube + jnp.dot(operand, square, preferred_element_type=jnp.float32)
    cube = jnp.where(keep, cube, 0.0)
    cube_rows = swap_layers(cube)
    row_field = lax.dynamic_slice_in_dim(
        lax.dynamic_index_in_dim(potential, grid_row, 0, keepdims=False), first, width, 0
    )
    diagonal = (rows_at == columns_at) & (grid_row == grid_column)
    shifted = (
        right_own.astype(jnp.float32) + jnp.where(diagonal, row_field[:, None], 0.0)
    ).astype(jnp.bfloat16)
    sign_step = (0.5 * (3.0 * shifted.astype(jnp.float32) - cube_rows)).astype(jnp.bfloat16)

    own = atoms.reshape(4, SUB, atom_count // SUB)
    packed, scale = packing(ids, near)
    lists = neighbours[0, 0, 0]
    pieces = 4
    groups = SUB // pieces
    pair_force = jnp.concatenate(
        [
            pair_forces(counts, i * groups, groups, lists, own, packed, scale)
            for i in range(pieces)
        ],
        axis=1,
    )
    forces = pair_force.reshape(3, atom_count) + embed_force[:3]
    return (sign_step, forces.reshape(3, 1, 1, 1, atom_count))


def solution(mesh):
    in_specs = (
        P("qr", "qc"),
        P("qr", "qc"),
        P(None, "qr"),
        P("qr"),
        P(None, "qr", "qc", "grp", None),
        P("qr", "qc", "grp", None, None, None),
        P(("qr", "qc", "grp")),
        P(("qr", "qc", "grp"), None),
        P(("qr", "qc", "grp")),
    )
    out_specs = (P(("qr", "grp"), "qc"), P(None, "qr", "qc", "grp", None))
    return jax.shard_map(
        per_device, mesh=mesh, in_specs=in_specs, out_specs=out_specs, check_vma=False
    )
```

```python
import functools

import jax
import jax.numpy as jnp
from jax import lax
from jax.experimental import pallas as pl
from jax.experimental.pallas import tpu as pltpu
from jax.sharding import PartitionSpec as P

BLOCK = 64
SUB, LANES = 8, 128

coulomb = 138.935
hartree_nm = 0.0529177
soften = 0.01
domain_edge = 3.4

ALL = ("qr", "qc", "grp")
VMEM = pltpu.MemorySpace.VMEM
SMEM = pltpu.MemorySpace.SMEM

LANE_PICK = lax.GatherDimensionNumbers(
    offset_dims=(),
    collapsed_slice_dims=(1,),
    start_index_map=(1,),
    operand_batching_dims=(0,),
    start_indices_batching_dims=(0,),
)


def pick_lanes(row, lane):
    return lax.gather(
        row, lane[..., None], LANE_PICK, (1, 1), mode=lax.GatherScatterMode.PROMISE_IN_BOUNDS
    )


def everyone(value, axes):
    count = 1
    for axis in (axes,) if isinstance(axes, str) else axes:
        count *= lax.axis_size(axis)
    copies = jnp.broadcast_to(value[None], (count,) + value.shape)
    return lax.all_to_all(copies, axes, split_axis=0, concat_axis=0, tiled=True)


def rotated(value, axis):
    count = lax.axis_size(axis)
    return [value] + [
        lax.ppermute(value, axis, [(i, (i + k) % count) for i in range(count)])
        for k in range(1, count)
    ]


def thirds(value):
    high = value.astype(jnp.bfloat16)
    rest = value - high.astype(jnp.float32)
    middle = rest.astype(jnp.bfloat16)
    low = (rest - middle.astype(jnp.float32)).astype(jnp.bfloat16)
    return high, middle, low


def records_kernel(
    anchor_ref, atoms_ref, pick_ref, block_ref, centers_ref, field_ref, force_ref
):
    atom_count = atoms_ref.shape[1]
    count = pick_ref.shape[1]
    blocks = centers_ref.shape[1]
    one_atom = (
        lax.broadcasted_iota(jnp.int32, (atom_count, count), 0) == pick_ref[...]
    ).astype(jnp.bfloat16)
    one_block = (
        lax.broadcasted_iota(jnp.int32, (blocks, count), 0) == block_ref[...]
    ).astype(jnp.bfloat16)

    def chosen_atoms(rows):
        pieces = [
            jnp.dot(piece, one_atom, preferred_element_type=jnp.float32) for piece in thirds(rows)
        ]
        return pieces[0] + pieces[1] + pieces[2]

    def chosen_centers(rows):
        pieces = [
            lax.dot_general(
                piece, one_block, (((0,), (0,)), ((), ())), preferred_element_type=jnp.float32
            )
            for piece in thirds(rows)
        ]
        return pieces[0] + pieces[1] + pieces[2]

    taken = chosen_atoms(atoms_ref[...])
    charge = taken[3:4]
    offset = [taken[c : c + 1] + anchor_ref[0, c] - chosen_centers(centers_ref[c]) for c in range(3)]
    weight = chosen_centers(centers_ref[3])
    distance = offset[0] * offset[0] + offset[1] * offset[1] + offset[2] * offset[2] + soften
    inverse = lax.rsqrt(distance)
    terms = hartree_nm * charge * inverse
    partial = jnp.zeros((blocks, BLOCK), jnp.float32)
    for piece in thirds(terms):
        partial = partial + lax.dot_general(
            one_block, piece, (((1,), (1,)), ((), ())), preferred_element_type=jnp.float32
        )
    field_ref[...] = partial
    strength = weight * (inverse * inverse * inverse)
    pushes = [
        coulomb * charge * jnp.sum(strength * offset[c], axis=0, keepdims=True) for c in range(3)
    ]
    pushes = jnp.concatenate(pushes + [jnp.zeros((5, count), jnp.float32)], axis=0)
    total = jnp.zeros((8, atom_count), jnp.float32)
    for piece in thirds(pushes):
        total = total + lax.dot_general(
            piece, one_atom, (((1,), (1,)), ((), ())), preferred_element_type=jnp.float32
        )
    force_ref[...] = total


def embedding(anchor, own, pick, block, centers):
    atom_count, count, blocks = own.shape[1], pick.shape[1], centers.shape[1]
    return pl.pallas_call(
        records_kernel,
        out_shape=(
            jax.ShapeDtypeStruct((blocks, BLOCK), jnp.float32),
            jax.ShapeDtypeStruct((8, atom_count), jnp.float32),
        ),
        in_specs=[pl.BlockSpec(memory_space=SMEM)] + [pl.BlockSpec(memory_space=VMEM)] * 4,
        out_specs=(pl.BlockSpec(memory_space=VMEM),) * 2,
        cost_estimate=pl.CostEstimate(flops=10**9, bytes_accessed=10**6, transcendentals=0),
        name="embedding",
    )(anchor, own, pick, block, centers)


SLOT_BITS = 5
BATCH = 2
CHUNK = 32


def packing_kernel(picks, near_ref, packed_ref, scale_ref):
    domains = len(picks)

    def entry(d, c):
        outer, inner = picks[d](near_ref)
        return near_ref[outer, inner, c]

    low = [entry(0, c) for c in range(4)]
    high = list(low)
    for d in range(1, domains):
        for c in range(4):
            value = entry(d, c)
            low[c] = jnp.minimum(low[c], value)
            high[c] = jnp.maximum(high[c], value)
    steps = 65535.0
    base, back = [], []
    for c in range(4):
        least = jnp.min(low[c], axis=(0, 1), keepdims=True)
        width = jnp.maximum(jnp.max(high[c], axis=(0, 1), keepdims=True) - least, 1e-30)
        base.append(jnp.broadcast_to(least, (SUB, LANES)))
        back.append(jnp.broadcast_to(steps / width, (SUB, LANES)))
        scale_ref[c] = base[c]
        scale_ref[4 + c] = jnp.broadcast_to(width * (1.0 / steps), (SUB, LANES))
    for d in range(domains):
        code = [
            jnp.clip((entry(d, c) - base[c]) * back[c] + 0.5, 0.0, steps).astype(jnp.int32)
            for c in range(4)
        ]
        packed_ref[0, d * SUB : (d + 1) * SUB, :] = code[0] | (code[1] << 16)
        packed_ref[1, d * SUB : (d + 1) * SUB, :] = code[2] | (code[3] << 16)
    for w in range(2):
        packed_ref[w, domains * SUB :, :] = jnp.zeros((CHUNK, LANES), jnp.int32)


def packing(ids, near):
    domains = ids.shape[1]

    def kernel(ids_ref, near_ref, packed_ref, scale_ref):
        picks = [lambda _, d=d: (ids_ref[0, d], ids_ref[1, d]) for d in range(domains)]
        packing_kernel(picks, near_ref, packed_ref, scale_ref)

    return pl.pallas_call(
        kernel,
        out_shape=(
            jax.ShapeDtypeStruct((2, domains * SUB + CHUNK, LANES), jnp.int32),
            jax.ShapeDtypeStruct((8, SUB, LANES), jnp.float32),
        ),
        in_specs=[pl.BlockSpec(memory_space=SMEM), pl.BlockSpec(memory_space=VMEM)],
        out_specs=(pl.BlockSpec(memory_space=VMEM),) * 2,
        cost_estimate=pl.CostEstimate(flops=10**7, bytes_accessed=5 * 10**6, transcendentals=0),
        name="packing",
    )(ids, near)


def compact(place, count):
    if count >= 3:
        return place
    if count == 2:
        return jnp.where(place == 1, 0, 1)
    return jnp.zeros_like(place)


def places_of(slot):
    p = (slot * 57) >> 9
    rest = slot - 9 * p
    q = (rest * 11) >> 5
    return p, q, rest - 3 * q


def network(count):
    pairs = []
    p = 1
    while p < count:
        k = p
        while k >= 1:
            for j in range(k % p, count - k, 2 * k):
                for i in range(min(k, count - j - k)):
                    if (i + j) // (2 * p) == (i + j + k) // (2 * p):
                        pairs.append((i + j, i + j + k))
            k //= 2
        p *= 2
    return pairs


def sorting_kernel(counts, lists_ref, keys_ref, range_ref, spread_ref):
    entries = lists_ref.shape[1]
    distinct = [min(3, count) for count in counts]
    for b in range(entries // SUB):
        for a in range(SUB):
            slot = lists_ref[0, b * SUB : (b + 1) * SUB, a * LANES : (a + 1) * LANES]
            member = lists_ref[1, b * SUB : (b + 1) * SUB, a * LANES : (a + 1) * LANES]
            p, q, r = places_of(slot)
            domain = (
                compact(p, counts[0]) * distinct[1] + compact(q, counts[1])
            ) * distinct[2] + compact(r, counts[2])
            key = ((domain * (SUB * LANES) + member) << SLOT_BITS) + slot
            spread_ref[pl.ds(b * SUB * SUB + a, SUB, stride=SUB), :] = key.astype(jnp.float32)
    keys = [spread_ref[n * SUB : (n + 1) * SUB, :] for n in range(entries)]
    for i, j in network(entries):
        keys[i], keys[j] = jnp.minimum(keys[i], keys[j]), jnp.maximum(keys[i], keys[j])
    for n in range(entries):
        keys_ref[n] = keys[n].astype(jnp.int32)
    least = [jnp.min(keys[n], axis=0, keepdims=True) for n in range(0, entries, BATCH)]
    most = [
        jnp.max(keys[n + BATCH - 1], axis=0, keepdims=True) for n in range(0, entries, BATCH)
    ]
    least = jnp.min(jnp.concatenate(least, axis=0), axis=1, keepdims=True)
    most = jnp.max(jnp.concatenate(most, axis=0), axis=1, keepdims=True)
    both = jnp.concatenate([least, most], axis=0).astype(jnp.int32) >> (SLOT_BITS + 7)
    range_ref[...] = jnp.broadcast_to(both, range_ref.shape)


def sorting(counts, lists):
    entries = lists.shape[1]
    return pl.pallas_call(
        functools.partial(sorting_kernel, counts),
        out_shape=(
            jax.ShapeDtypeStruct((entries, SUB, LANES), jnp.int32),
            jax.ShapeDtypeStruct((2 * entries // BATCH, LANES), jnp.int32),
        ),
        in_specs=[pl.BlockSpec(memory_space=VMEM)],
        out_specs=(pl.BlockSpec(memory_space=VMEM),) * 2,
        scratch_shapes=[pltpu.VMEM((entries * SUB, LANES), jnp.float32)],
        cost_estimate=pl.CostEstimate(flops=10**7, bytes_accessed=7 * 10**6, transcendentals=0),
        name="sorting",
    )(lists)


def pair_kernel(first, last, range_ref, keys_ref, own_ref, packed_ref, scale_ref, force_ref):
    blocks = keys_ref.shape[0] // BATCH
    mine = [own_ref[c] for c in range(4)]

    def step(j, sums):
        keys = [keys_ref[j * BATCH + i] for i in range(BATCH)]
        rows = [key >> (SLOT_BITS + 7) for key in keys]
        lanes = [(key >> SLOT_BITS) & (LANES - 1) for key in keys]
        low = range_ref[j, 0]
        rounds = (range_ref[blocks + j, 0] - low) // CHUNK + 1

        def scan(i, words):
            words = list(words)
            base = low + i * CHUNK
            for m in range(BATCH):
                for u in range(CHUNK):
                    here = rows[m] == base + u
                    for w in range(2):
                        line = jnp.broadcast_to(packed_ref[w, pl.ds(base + u, 1), :], (SUB, LANES))
                        k = 2 * m + w
                        words[k] = jnp.where(here, pick_lanes(line, lanes[m]), words[k])
            return tuple(words)

        zero = jnp.zeros((SUB, LANES), jnp.int32)
        words = lax.fori_loop(0, rounds, scan, (zero,) * (2 * BATCH))
        sums = list(sums)
        for m in range(BATCH):
            places = places_of(keys[m] & ((1 << SLOT_BITS) - 1))
            code = [
                words[2 * m] & 0xFFFF,
                (words[2 * m] >> 16) & 0xFFFF,
                words[2 * m + 1] & 0xFFFF,
                (words[2 * m + 1] >> 16) & 0xFFFF,
            ]
            value = [code[c].astype(jnp.float32) * scale_ref[4 + c] + scale_ref[c] for c in range(4)]
            shift = [(place - 1).astype(jnp.float32) * domain_edge for place in places]
            offset = [mine[c] - (value[c] + shift[c]) for c in range(3)]
            distance = (
                offset[0] * offset[0] + offset[1] * offset[1] + offset[2] * offset[2] + soften
            )
            inverse = lax.rsqrt(distance)
            strength = value[3] * (inverse * inverse * inverse)
            for c in range(3):
                sums[c] = sums[c] + offset[c] * strength
        return tuple(sums)

    zero = jnp.zeros((SUB, LANES), jnp.float32)
    sums = lax.fori_loop(first, last, step, (zero, zero, zero))
    for c in range(3):
        force_ref[c] = coulomb * mine[3] * sums[c]


def pair_forces(first, last, ranges, keys, own, packed, scale):
    return pl.pallas_call(
        functools.partial(pair_kernel, first, last),
        out_shape=jax.ShapeDtypeStruct((3, SUB, LANES), jnp.float32),
        in_specs=[pl.BlockSpec(memory_space=SMEM)] + [pl.BlockSpec(memory_space=VMEM)] * 4,
        out_specs=pl.BlockSpec(memory_space=VMEM),
        cost_estimate=pl.CostEstimate(
            flops=10**7, bytes_accessed=(last - first) * 10**6, transcendentals=0
        ),
        name="pairs",
    )(ranges, keys, own, packed, scale)


def neighbourhood(counts, along_rows):
    here = [lax.axis_index(axis) for axis in ALL]
    reach = [(-1, 0, 1) if n >= 3 else (0, 1) if n == 2 else (0,) for n in counts]
    if counts[1] * counts[2] <= 16:
        near = everyone(along_rows, ("qc", "grp"))
        outer = [
            ((here[1] + j) % counts[1]) * counts[2] + (here[2] + k) % counts[2]
            for j in reach[1]
            for k in reach[2]
        ]
    else:
        near = along_rows[None]
        for axis, count in (("grp", counts[2]), ("qc", counts[1])):
            ahead = [((i + 1) % count, i) for i in range(count)]
            behind = [(i, (i + 1) % count) for i in range(count)]
            if count >= 3:
                near = jnp.concatenate(
                    [lax.ppermute(near, axis, behind), near, lax.ppermute(near, axis, ahead)]
                )
            elif count == 2:
                near = jnp.concatenate([near, lax.ppermute(near, axis, ahead)])
        outer = [jnp.int32(k) for k in range(near.shape[0])]
    inner = [(here[0] + i) % counts[0] for i in reach[0]]
    ids = jnp.stack(
        [jnp.stack([o for _ in inner for o in outer]), jnp.stack([i for i in inner for _ in outer])]
    )
    return near, ids.astype(jnp.int32)


def per_device(
    kohn_sham, pattern, basis_centers, occupations, atoms, neighbours, emb_atom, emb_dest, emb_block
):
    counts = tuple(lax.axis_size(axis) for axis in ALL)
    extent, layers = counts[0], counts[2]
    grid_row = lax.axis_index("qr")
    grid_column = lax.axis_index("qc")
    layer = lax.axis_index("grp")
    order = kohn_sham.shape[0]
    width = order // layers
    tile_blocks = order // BLOCK
    atom_count = atoms.shape[4]
    record_count = emb_atom.shape[0]

    own = atoms.reshape(4, SUB, atom_count // SUB)
    after = lax.optimization_barrier

    basis = jnp.concatenate([basis_centers, occupations[None]], axis=0)
    plane = SUB * LANES
    planes = -(-basis.size // plane)
    packet = jnp.concatenate(
        [own, jnp.pad(basis.reshape(-1), (0, planes * plane - basis.size)).reshape(planes, SUB, LANES)]
    )
    packets = everyone(packet, "qr")
    basis_all = packets[:, 4:].reshape(extent, planes * plane)[:, : basis.size]
    centers = (
        jnp.transpose(basis_all.reshape(extent, 4, tile_blocks, BLOCK), (1, 0, 2, 3))
    ).reshape(4, extent * tile_blocks, BLOCK)

    first = layer * width
    left_own = lax.dynamic_slice_in_dim(kohn_sham, first, width, 1)
    right_own = lax.dynamic_slice_in_dim(kohn_sham, first, width, 0)
    left = everyone(left_own, "qc")
    rights = rotated(right_own, "qr")
    near, ids = neighbourhood(counts, packets[:, :4])
    keys, ranges = sorting(counts, neighbours[0, 0, 0])

    anchor = (
        jnp.stack([grid_row, grid_column, layer]).astype(jnp.float32)[None] * domain_edge
    )
    field, embed_force = embedding(
        anchor,
        atoms.reshape(4, atom_count),
        emb_atom[None],
        (emb_dest[:, 0] * tile_blocks + emb_block)[None],
        centers,
    )
    field_all = everyone(field.reshape(extent * order), ALL)

    keep = jnp.repeat(jnp.repeat(pattern, BLOCK, axis=0), BLOCK, axis=1) == 1
    behind = [(grid_row - k) % extent for k in range(extent)]
    lefts = [lax.dynamic_index_in_dim(left, tile, 0, keepdims=False) for tile in behind]

    def swap_layers(part):
        wide = part.reshape(layers, width, order)
        mine = lax.dynamic_index_in_dim(wide, layer, 0, keepdims=False)
        if layers == 2:
            theirs = lax.dynamic_index_in_dim(wide, 1 - layer, 0, keepdims=False)
            got = lax.ppermute(theirs.astype(jnp.bfloat16), "grp", [(0, 1), (1, 0)])[None]
            return mine, got
        got = lax.all_to_all(
            wide.astype(jnp.bfloat16), "grp", split_axis=0, concat_axis=0, tiled=True
        )
        other = jnp.arange(layers)[:, None, None] != layer
        return mine, jnp.where(other, got, 0)

    def added(mine, got):
        return mine + jnp.sum(got.astype(jnp.float32), axis=0)

    blocks = keys.shape[0] // BATCH
    cuts = (0, blocks // 4, 3 * blocks // 4, blocks)

    product = jnp.zeros((order, order), jnp.float32)
    for k in range(extent):
        product = product + jnp.dot(lefts[k], rights[k], preferred_element_type=jnp.float32)
    product = jnp.where(keep, product, 0.0)

    packed, scale = packing(ids, near)

    mine, got = swap_layers(product)
    mine, packed = after((mine, packed))
    pair_one = pair_forces(cuts[0], cuts[1], ranges, keys, own, packed, scale)
    got, pair_one = after((got, pair_one))
    product_rows = added(mine, got).astype(jnp.bfloat16)
    product_rows, packed = after((product_rows, packed))
    products = rotated(product_rows, "qr")
    pair_two = pair_forces(cuts[1], cuts[2], ranges, keys, own, packed, scale)
    *received, pair_two = after((*products[1:], pair_two))
    products = [products[0]] + received
    potential = jnp.sum(field_all, axis=0).reshape(extent, order)

    own_column = lax.dynamic_index_in_dim(potential, grid_column, 0, keepdims=False)
    rows_at = jnp.arange(width)[:, None] + first
    columns_at = jnp.arange(order)[None, :]
    cube = jnp.zeros((order, order), jnp.float32)
    for k in range(extent):
        tile = behind[k]
        row_field = lax.dynamic_slice_in_dim(
            lax.dynamic_index_in_dim(potential, tile, 0, keepdims=False), first, width, 0
        )
        matrix = rights[k].astype(jnp.float32)
        diagonal = (rows_at == columns_at) & (tile == grid_column)
        square = (
            products[k].astype(jnp.float32)
            + matrix * (row_field[:, None] + own_column[None, :])
            + jnp.where(diagonal, row_field[:, None] * row_field[:, None], 0.0)
        ).astype(jnp.bfloat16)
        operand = lefts[k]
        if k == 0:
            on_diagonal = jnp.arange(order)[:, None] == jnp.arange(width)[None, :] + first
            operand = (
                operand.astype(jnp.float32) + jnp.where(on_diagonal, row_field[None, :], 0.0)
            ).astype(jnp.bfloat16)
        cube = cube + jnp.dot(operand, square, preferred_element_type=jnp.float32)
    cube = jnp.where(keep, cube, 0.0)
    mine, got = swap_layers(cube)
    mine, packed = after((mine, packed))
    pair_three = pair_forces(cuts[2], cuts[3], ranges, keys, own, packed, scale)
    got, pair_three = after((got, pair_three))
    cube_rows = added(mine, got)
    row_field = lax.dynamic_slice_in_dim(
        lax.dynamic_index_in_dim(potential, grid_row, 0, keepdims=False), first, width, 0
    )
    diagonal = (rows_at == columns_at) & (grid_row == grid_column)
    shifted = (
        right_own.astype(jnp.float32) + jnp.where(diagonal, row_field[:, None], 0.0)
    ).astype(jnp.bfloat16)
    sign_step = (0.5 * (3.0 * shifted.astype(jnp.float32) - cube_rows)).astype(jnp.bfloat16)

    pair_force = pair_one + pair_two + pair_three
    forces = pair_force.reshape(3, atom_count) + embed_force[:3]
    return (sign_step, forces.reshape(3, 1, 1, 1, atom_count))


def solution(mesh):
    in_specs = (
        P("qr", "qc"),
        P("qr", "qc"),
        P(None, "qr"),
        P("qr"),
        P(None, "qr", "qc", "grp", None),
        P("qr", "qc", "grp", None, None, None),
        P(("qr", "qc", "grp")),
        P(("qr", "qc", "grp"), None),
        P(("qr", "qc", "grp")),
    )
    out_specs = (P(("qr", "grp"), "qc"), P(None, "qr", "qc", "grp", None))
    return jax.shard_map(
        per_device, mesh=mesh, in_specs=in_specs, out_specs=out_specs, check_vma=False
    )
```

```python
import functools

import jax
import jax.numpy as jnp
from jax import lax
from jax.experimental import pallas as pl
from jax.experimental.pallas import tpu as pltpu
from jax.sharding import PartitionSpec as P

BLOCK = 64
SUB, LANES = 8, 128

coulomb = 138.935
hartree_nm = 0.0529177
soften = 0.01
domain_edge = 3.4

ALL = ("qr", "qc", "grp")
VMEM = pltpu.MemorySpace.VMEM
GRANT = 16 << 20
SMEM = pltpu.MemorySpace.SMEM

LANE_PICK = lax.GatherDimensionNumbers(
    offset_dims=(),
    collapsed_slice_dims=(1,),
    start_index_map=(1,),
    operand_batching_dims=(0,),
    start_indices_batching_dims=(0,),
)


def pick_lanes(row, lane):
    return lax.gather(
        row, lane[..., None], LANE_PICK, (1, 1), mode=lax.GatherScatterMode.PROMISE_IN_BOUNDS
    )


def everyone(value, axes):
    count = 1
    for axis in (axes,) if isinstance(axes, str) else axes:
        count *= lax.axis_size(axis)
    copies = jnp.broadcast_to(value[None], (count,) + value.shape)
    return lax.all_to_all(copies, axes, split_axis=0, concat_axis=0, tiled=True)


def rotated(value, axis):
    count = lax.axis_size(axis)
    return [value] + [
        lax.ppermute(value, axis, [(i, (i + k) % count) for i in range(count)])
        for k in range(1, count)
    ]


def thirds(value):
    high = value.astype(jnp.bfloat16)
    rest = value - high.astype(jnp.float32)
    middle = rest.astype(jnp.bfloat16)
    low = (rest - middle.astype(jnp.float32)).astype(jnp.bfloat16)
    return high, middle, low


def prepare_kernel(matrix_ref, atoms_ref, centers_ref, weights_ref, left_ref, right_ref, packet_ref):
    order, width = left_ref.shape
    layer = lax.axis_index("grp")
    right_ref[...] = matrix_ref[pl.ds(pl.multiple_of(layer * width, width), width), :]
    for i in range(order // width):

        @pl.when(layer == i)
        def _():
            left_ref[...] = matrix_ref[:, i * width : (i + 1) * width]

    packet_ref[0:4] = atoms_ref[...]
    lines = order // LANES
    rows = [
        (centers_ref[c : c + 1] if c < 3 else weights_ref[...])[:, n * LANES : (n + 1) * LANES]
        for c in range(4)
        for n in range(lines)
    ]
    planes = packet_ref.shape[0] - 4
    rows = rows + [jnp.zeros((1, LANES), jnp.float32)] * (planes * SUB - len(rows))
    for n in range(planes):
        packet_ref[4 + n] = jnp.concatenate(rows[n * SUB : (n + 1) * SUB], axis=0)


def prepare(width, matrix, atoms, centers, weights):
    order = matrix.shape[0]
    planes = -(-4 * (order // LANES) // SUB)
    return pl.pallas_call(
        prepare_kernel,
        out_shape=(
            jax.ShapeDtypeStruct((order, width), matrix.dtype),
            jax.ShapeDtypeStruct((width, order), matrix.dtype),
            jax.ShapeDtypeStruct((4 + planes, SUB, LANES), jnp.float32),
        ),
        in_specs=[pl.BlockSpec(memory_space=VMEM)] * 4,
        out_specs=(pl.BlockSpec(memory_space=VMEM),) * 3,
        cost_estimate=pl.CostEstimate(flops=10**6, bytes_accessed=10**6, transcendentals=0),
        compiler_params=pltpu.CompilerParams(vmem_limit_bytes=GRANT),
        name="prepare",
    )(matrix, atoms, centers, weights)


def records_kernel(extent, lines, *refs):
    packet_refs = refs[:extent]
    pick_ref, dest_ref, block_ref, field_ref, force_ref = refs[extent:]
    count = pick_ref.shape[1]
    here = [lax.axis_index(axis) for axis in ALL]
    anchor = [place.astype(jnp.float32) * domain_edge for place in here]
    pick, dest, block = pick_ref[...], dest_ref[...], block_ref[...]
    lane, group = pick & (LANES - 1), pick >> 7
    behind = here[0] - dest
    behind = jnp.where(behind < 0, behind + extent, behind)
    iota = functools.partial(lax.broadcasted_iota, jnp.int32)
    one_lane = (iota((LANES, count), 0) == lane).astype(jnp.bfloat16)
    in_group = iota((SUB, count), 0) == group
    half = block >> 1
    odd = (block & 1) == 1
    one_line = (iota((extent * lines, count), 0) == behind * lines + half).astype(jnp.bfloat16)
    one_out = (iota((extent * lines, count), 0) == dest * lines + half).astype(jnp.bfloat16)

    def exact(product, value):
        high, middle, low = thirds(value)
        return product(high) + product(middle) + product(low)

    def dot(contract):
        return lambda other: lambda value: lax.dot_general(
            value, other, (contract, ((), ())), preferred_element_type=jnp.float32
        )

    own = packet_refs[0]
    atoms = jnp.concatenate([own[c] for c in range(4)], axis=0)
    spread = exact(dot(((1,), (0,)))(one_lane), atoms)
    taken = [
        jnp.sum(jnp.where(in_group, spread[c * SUB : (c + 1) * SUB], 0.0), axis=0, keepdims=True)
        for c in range(4)
    ]

    def line(k, n):
        return packet_refs[k][4 + n // SUB, n % SUB : n % SUB + 1, :]

    def chosen(c):
        table = jnp.concatenate(
            [line(k, c * lines + n) for k in range(extent) for n in range(lines)], axis=0
        )
        both = exact(dot(((0,), (0,)))(one_line), table)
        return jnp.where(odd, both[BLOCK:], both[:BLOCK])

    charge = taken[3]
    offset = [taken[c] + anchor[c] - chosen(c) for c in range(3)]
    weight = chosen(3)
    distance = offset[0] * offset[0] + offset[1] * offset[1] + offset[2] * offset[2] + soften
    inverse = lax.rsqrt(distance)
    terms = hartree_nm * charge * inverse
    terms = jnp.concatenate([jnp.where(odd, 0.0, terms), jnp.where(odd, terms, 0.0)], axis=0)
    high, middle, low = thirds(terms)
    field_ref[...] = sum(
        lax.dot_general(one_out, piece, (((1,), (1,)), ((), ())), preferred_element_type=jnp.float32)
        for piece in (high, middle, low)
    )
    strength = weight * (inverse * inverse * inverse)
    pushes = [
        coulomb * charge * jnp.sum(strength * offset[c], axis=0, keepdims=True) for c in range(3)
    ]
    pushes = jnp.concatenate([jnp.where(in_group, push, 0.0) for push in pushes], axis=0)
    total = exact(dot(((1,), (1,)))(one_lane), pushes)
    for c in range(3):
        force_ref[c] = total[c * SUB : (c + 1) * SUB]


def embedding(order, packets, pick, dest, block):
    extent, lines = len(packets), order // LANES
    return pl.pallas_call(
        functools.partial(records_kernel, extent, lines),
        out_shape=(
            jax.ShapeDtypeStruct((extent * lines, LANES), jnp.float32),
            jax.ShapeDtypeStruct((3, SUB, LANES), jnp.float32),
        ),
        in_specs=[pl.BlockSpec(memory_space=VMEM)] * (extent + 3),
        out_specs=(pl.BlockSpec(memory_space=VMEM),) * 2,
        cost_estimate=pl.CostEstimate(flops=10**7, bytes_accessed=5 * 10**6, transcendentals=0),
        compiler_params=pltpu.CompilerParams(vmem_limit_bytes=GRANT),
        name="embedding",
    )(*packets, pick, dest, block)


def field_kernel(parts_ref, rows_ref, columns_ref):
    total = parts_ref[0]
    for k in range(1, parts_ref.shape[0]):
        total = total + parts_ref[k]
    rows_ref[...] = total
    for n in range(total.shape[0]):
        columns_ref[n * LANES : (n + 1) * LANES, :] = jnp.broadcast_to(
            total[n : n + 1], (LANES, LANES)
        ).T


def whole_field(parts):
    lines = parts.shape[1]
    return pl.pallas_call(
        field_kernel,
        out_shape=(
            jax.ShapeDtypeStruct((lines, LANES), jnp.float32),
            jax.ShapeDtypeStruct((lines * LANES, LANES), jnp.float32),
        ),
        in_specs=[pl.BlockSpec(memory_space=VMEM)],
        out_specs=(pl.BlockSpec(memory_space=VMEM),) * 2,
        cost_estimate=pl.CostEstimate(flops=10**6, bytes_accessed=3 * 10**6, transcendentals=0),
        compiler_params=pltpu.CompilerParams(vmem_limit_bytes=GRANT),
        name="field",
    )(parts)


def modulo(value, count):
    return jnp.where(value < 0, value + count, value)


def keep_pattern(pattern_ref, value):
    blocks = pattern_ref.shape[0]
    which = lax.broadcasted_iota(jnp.int32, (1, value.shape[1]), 1) // BLOCK
    out = []
    for a in range(blocks):
        marks = jnp.zeros((1, value.shape[1]), jnp.int32)
        for b in range(blocks):
            marks = jnp.where(which == b, pattern_ref[a, b], marks)
        out.append(jnp.where(marks == 1, value[a * BLOCK : (a + 1) * BLOCK], 0.0))
    return jnp.concatenate(out, axis=0)


def part_outputs(layers, value, hold_ref, mine_ref, send_ref):
    width = mine_ref.shape[0]
    layer = lax.axis_index("grp")
    hold_ref[...] = value
    mine_ref[...] = hold_ref[pl.ds(pl.multiple_of(layer * width, width), width), :]
    if layers == 2:
        send_ref[...] = hold_ref[
            pl.ds(pl.multiple_of((1 - layer) * width, width), width), :
        ].astype(send_ref.dtype)
    else:
        send_ref[...] = value.astype(send_ref.dtype)


def product_kernel(places, pattern_ref, *refs):
    extent = len(refs) - 4 - len(places)
    left_refs, right_refs = refs[: len(places)], refs[len(places) : len(places) + extent]
    mine_ref, send_ref, table_ref, hold_ref = refs[len(places) + extent :]
    row, column = lax.axis_index("qr"), lax.axis_index("qc")
    for left_ref, place in zip(left_refs, places):
        table_ref[place(column)] = left_ref[...]
    total = jnp.zeros(hold_ref.shape, jnp.float32)
    for k in range(extent):
        total = total + jnp.dot(
            table_ref[modulo(row - k, extent)],
            right_refs[k][...],
            preferred_element_type=jnp.float32,
        )
    part_outputs(
        hold_ref.shape[0] // mine_ref.shape[0],
        keep_pattern(pattern_ref, total),
        hold_ref,
        mine_ref,
        send_ref,
    )


def part_shapes(order, width):
    rows = width if order == 2 * width else order
    return (
        jax.ShapeDtypeStruct((width, order), jnp.float32),
        jax.ShapeDtypeStruct((rows, order), jnp.bfloat16),
    )


def product_part(pattern, lefts, places, rights):
    order, width = lefts[0].shape
    inputs = len(lefts) + len(rights)
    return pl.pallas_call(
        functools.partial(product_kernel, places),
        out_shape=part_shapes(order, width)
        + (jax.ShapeDtypeStruct((len(lefts), order, width), jnp.bfloat16),),
        in_specs=[pl.BlockSpec(memory_space=SMEM)] + [pl.BlockSpec(memory_space=VMEM)] * inputs,
        out_specs=(pl.BlockSpec(memory_space=VMEM),) * 3,
        scratch_shapes=[pltpu.VMEM((order, order), jnp.float32)],
        cost_estimate=pl.CostEstimate(
            flops=2 * order * order * width * len(rights),
            bytes_accessed=3 * 10**6,
            transcendentals=0,
        ),
        compiler_params=pltpu.CompilerParams(vmem_limit_bytes=GRANT),
        name="product",
    )(pattern, *lefts, *rights)


def cube_kernel(pattern_ref, table_ref, rows_ref, columns_ref, *refs):
    extent = (len(refs) - 3) // 2
    product_refs, right_refs = refs[:extent], refs[extent : 2 * extent]
    mine_ref, send_ref, hold_ref = refs[2 * extent :]
    width, order = mine_ref.shape
    lines = order // LANES
    row, column, layer = (lax.axis_index(axis) for axis in ALL)
    first = layer * width
    iota = functools.partial(lax.broadcasted_iota, jnp.int32)
    total = jnp.zeros((order, order), jnp.float32)
    for k in range(extent):
        tile = modulo(row - k, extent)
        down = columns_ref[pl.ds(pl.multiple_of(tile * order + first, width), width), :]
        pieces = []
        for n in range(lines):
            spot = slice(n * LANES, (n + 1) * LANES)
            across = rows_ref[pl.ds(column * lines + n, 1), :]
            matrix = right_refs[k][:, spot].astype(jnp.float32)
            on_diagonal = iota((width, LANES), 0) + first == iota((width, LANES), 1) + n * LANES
            corner = jnp.where(on_diagonal & (tile == column), down * down, 0.0)
            piece = product_refs[k][:, spot].astype(jnp.float32) + matrix * (down + across) + corner
            pieces.append(piece.astype(jnp.bfloat16))
        square = jnp.concatenate(pieces, axis=1)
        operand = table_ref[tile]
        if k == 0:
            own = columns_ref[pl.ds(pl.multiple_of(row * order, order), order), :]
            parts = []
            for start in range(0, width, LANES):
                size = min(LANES, width - start)
                shape = (order, size)
                on_diagonal = iota(shape, 0) == iota(shape, 1) + (first + start)
                parts.append(jnp.where(on_diagonal, own[:, :size], 0.0))
            added = parts[0] if len(parts) == 1 else jnp.concatenate(parts, axis=1)
            operand = (operand.astype(jnp.float32) + added).astype(jnp.bfloat16)
        total = total + jnp.dot(operand, square, preferred_element_type=jnp.float32)
    part_outputs(
        order // width, keep_pattern(pattern_ref, total), hold_ref, mine_ref, send_ref
    )


def cube_part(pattern, table, rows, columns, products, rights):
    _, order, width = table.shape
    inputs = 3 + len(products) + len(rights)
    return pl.pallas_call(
        cube_kernel,
        out_shape=part_shapes(order, width),
        in_specs=[pl.BlockSpec(memory_space=SMEM)] + [pl.BlockSpec(memory_space=VMEM)] * inputs,
        out_specs=(pl.BlockSpec(memory_space=VMEM),) * 2,
        scratch_shapes=[pltpu.VMEM((order, order), jnp.float32)],
        cost_estimate=pl.CostEstimate(
            flops=2 * order * order * width * len(rights),
            bytes_accessed=3 * 10**6,
            transcendentals=0,
        ),
        compiler_params=pltpu.CompilerParams(vmem_limit_bytes=GRANT),
        name="cube",
    )(pattern, table, rows, columns, *products, *rights)


def final_kernel(mine_ref, got_ref, right_ref, columns_ref, out_ref):
    width, order = mine_ref.shape
    row, column, layer = (lax.axis_index(axis) for axis in ALL)
    first = layer * width
    down = columns_ref[pl.ds(pl.multiple_of(row * order + first, width), width), :]
    iota = functools.partial(lax.broadcasted_iota, jnp.int32)
    for n in range(order // LANES):
        spot = slice(n * LANES, (n + 1) * LANES)
        on_diagonal = iota((width, LANES), 0) + first == iota((width, LANES), 1) + n * LANES
        added = jnp.where(on_diagonal & (row == column), down, 0.0)
        shifted = (right_ref[:, spot].astype(jnp.float32) + added).astype(jnp.bfloat16)
        cube = mine_ref[:, spot] + got_ref[:, spot].astype(jnp.float32)
        out_ref[:, spot] = (0.5 * (3.0 * shifted.astype(jnp.float32) - cube)).astype(jnp.bfloat16)


def final_step(mine, got, right, columns):
    return pl.pallas_call(
        final_kernel,
        out_shape=jax.ShapeDtypeStruct(mine.shape, jnp.bfloat16),
        in_specs=[pl.BlockSpec(memory_space=VMEM)] * 4,
        out_specs=pl.BlockSpec(memory_space=VMEM),
        cost_estimate=pl.CostEstimate(flops=10**6, bytes_accessed=10**6, transcendentals=0),
        compiler_params=pltpu.CompilerParams(vmem_limit_bytes=GRANT),
        name="final",
    )(mine, got, right, columns)


SLOT_BITS = 5
BATCH = 2
CHUNK = 32


def packing_kernel(pick, domains, near_ref, packed_ref, scale_ref):
    picks = pick()

    def entry(d, c):
        outer, inner = picks[d]
        return near_ref[outer, inner, c]

    low = [entry(0, c) for c in range(4)]
    high = list(low)
    for d in range(1, domains):
        for c in range(4):
            value = entry(d, c)
            low[c] = jnp.minimum(low[c], value)
            high[c] = jnp.maximum(high[c], value)
    steps = 65535.0
    base, back = [], []
    for c in range(4):
        least = jnp.min(low[c], axis=(0, 1), keepdims=True)
        width = jnp.maximum(jnp.max(high[c], axis=(0, 1), keepdims=True) - least, 1e-30)
        base.append(jnp.broadcast_to(least, (SUB, LANES)))
        back.append(jnp.broadcast_to(steps / width, (SUB, LANES)))
        scale_ref[c] = base[c]
        scale_ref[4 + c] = jnp.broadcast_to(width * (1.0 / steps), (SUB, LANES))
    for d in range(domains):
        code = [
            jnp.clip((entry(d, c) - base[c]) * back[c] + 0.5, 0.0, steps).astype(jnp.int32)
            for c in range(4)
        ]
        packed_ref[0, d * SUB : (d + 1) * SUB, :] = code[0] | (code[1] << 16)
        packed_ref[1, d * SUB : (d + 1) * SUB, :] = code[2] | (code[3] << 16)
    for w in range(2):
        packed_ref[w, domains * SUB :, :] = jnp.zeros((CHUNK, LANES), jnp.int32)


def packing(pick, domains, near):
    return pl.pallas_call(
        functools.partial(packing_kernel, pick, domains),
        out_shape=(
            jax.ShapeDtypeStruct((2, domains * SUB + CHUNK, LANES), jnp.int32),
            jax.ShapeDtypeStruct((8, SUB, LANES), jnp.float32),
        ),
        in_specs=[pl.BlockSpec(memory_space=VMEM)],
        out_specs=(pl.BlockSpec(memory_space=VMEM),) * 2,
        cost_estimate=pl.CostEstimate(flops=10**7, bytes_accessed=5 * 10**6, transcendentals=0),
        compiler_params=pltpu.CompilerParams(vmem_limit_bytes=GRANT),
        name="packing",
    )(near)


def compact(place, count):
    if count >= 3:
        return place
    if count == 2:
        return jnp.where(place == 1, 0, 1)
    return jnp.zeros_like(place)


def places_of(slot):
    p = (slot * 57) >> 9
    rest = slot - 9 * p
    q = (rest * 11) >> 5
    return p, q, rest - 3 * q


def network(count):
    pairs = []
    p = 1
    while p < count:
        k = p
        while k >= 1:
            for j in range(k % p, count - k, 2 * k):
                for i in range(min(k, count - j - k)):
                    if (i + j) // (2 * p) == (i + j + k) // (2 * p):
                        pairs.append((i + j, i + j + k))
            k //= 2
        p *= 2
    return pairs


def sorting_kernel(counts, lists_ref, keys_ref, range_ref, spread_ref):
    entries = lists_ref.shape[1]
    distinct = [min(3, count) for count in counts]
    for b in range(entries // SUB):
        for a in range(SUB):
            slot = lists_ref[0, b * SUB : (b + 1) * SUB, a * LANES : (a + 1) * LANES]
            member = lists_ref[1, b * SUB : (b + 1) * SUB, a * LANES : (a + 1) * LANES]
            p, q, r = places_of(slot)
            domain = (
                compact(p, counts[0]) * distinct[1] + compact(q, counts[1])
            ) * distinct[2] + compact(r, counts[2])
            key = ((domain * (SUB * LANES) + member) << SLOT_BITS) + slot
            spread_ref[pl.ds(b * SUB * SUB + a, SUB, stride=SUB), :] = key.astype(jnp.float32)
    keys = [spread_ref[n * SUB : (n + 1) * SUB, :] for n in range(entries)]
    for i, j in network(entries):
        keys[i], keys[j] = jnp.minimum(keys[i], keys[j]), jnp.maximum(keys[i], keys[j])
    for n in range(entries):
        keys_ref[n] = keys[n].astype(jnp.int32)
    least = [jnp.min(keys[n], axis=0, keepdims=True) for n in range(0, entries, BATCH)]
    most = [
        jnp.max(keys[n + BATCH - 1], axis=0, keepdims=True) for n in range(0, entries, BATCH)
    ]
    least = jnp.min(jnp.concatenate(least, axis=0), axis=1, keepdims=True)
    most = jnp.max(jnp.concatenate(most, axis=0), axis=1, keepdims=True)
    both = jnp.concatenate([least, most], axis=0).astype(jnp.int32) >> (SLOT_BITS + 7)
    range_ref[...] = jnp.broadcast_to(both, range_ref.shape)


def sorting(counts, lists):
    entries = lists.shape[1]
    return pl.pallas_call(
        functools.partial(sorting_kernel, counts),
        out_shape=(
            jax.ShapeDtypeStruct((entries, SUB, LANES), jnp.int32),
            jax.ShapeDtypeStruct((2 * entries // BATCH, LANES), jnp.int32),
        ),
        in_specs=[pl.BlockSpec(memory_space=VMEM)],
        out_specs=(pl.BlockSpec(memory_space=VMEM),) * 2,
        scratch_shapes=[pltpu.VMEM((entries * SUB, LANES), jnp.float32)],
        cost_estimate=pl.CostEstimate(flops=10**7, bytes_accessed=7 * 10**6, transcendentals=0),
        compiler_params=pltpu.CompilerParams(vmem_limit_bytes=GRANT),
        name="sorting",
    )(lists)


def pair_kernel(
    first, last, range_ref, keys_ref, own_ref, packed_ref, scale_ref, start_ref, force_ref
):
    blocks = keys_ref.shape[0] // BATCH
    mine = [own_ref[c] for c in range(4)]

    def step(j, sums):
        keys = [keys_ref[j * BATCH + i] for i in range(BATCH)]
        rows = [key >> (SLOT_BITS + 7) for key in keys]
        lanes = [(key >> SLOT_BITS) & (LANES - 1) for key in keys]
        low = range_ref[j, 0]
        rounds = (range_ref[blocks + j, 0] - low) // CHUNK + 1

        def scan(i, words):
            words = list(words)
            base = low + i * CHUNK
            for m in range(BATCH):
                for u in range(CHUNK):
                    here = rows[m] == base + u
                    for w in range(2):
                        line = jnp.broadcast_to(packed_ref[w, pl.ds(base + u, 1), :], (SUB, LANES))
                        k = 2 * m + w
                        words[k] = jnp.where(here, pick_lanes(line, lanes[m]), words[k])
            return tuple(words)

        zero = jnp.zeros((SUB, LANES), jnp.int32)
        words = lax.fori_loop(0, rounds, scan, (zero,) * (2 * BATCH))
        sums = list(sums)
        for m in range(BATCH):
            places = places_of(keys[m] & ((1 << SLOT_BITS) - 1))
            code = [
                words[2 * m] & 0xFFFF,
                (words[2 * m] >> 16) & 0xFFFF,
                words[2 * m + 1] & 0xFFFF,
                (words[2 * m + 1] >> 16) & 0xFFFF,
            ]
            value = [code[c].astype(jnp.float32) * scale_ref[4 + c] + scale_ref[c] for c in range(4)]
            shift = [(place - 1).astype(jnp.float32) * domain_edge for place in places]
            offset = [mine[c] - (value[c] + shift[c]) for c in range(3)]
            distance = (
                offset[0] * offset[0] + offset[1] * offset[1] + offset[2] * offset[2] + soften
            )
            inverse = lax.rsqrt(distance)
            strength = value[3] * (inverse * inverse * inverse)
            for c in range(3):
                sums[c] = sums[c] + offset[c] * strength
        return tuple(sums)

    zero = jnp.zeros((SUB, LANES), jnp.float32)
    sums = lax.fori_loop(first, last, step, (zero, zero, zero))
    for c in range(3):
        force_ref[c] = start_ref[c] + coulomb * mine[3] * sums[c]


def pair_forces(first, last, ranges, keys, own, packed, scale, start):
    return pl.pallas_call(
        functools.partial(pair_kernel, first, last),
        out_shape=jax.ShapeDtypeStruct((3, SUB, LANES), jnp.float32),
        in_specs=[pl.BlockSpec(memory_space=SMEM)] + [pl.BlockSpec(memory_space=VMEM)] * 5,
        out_specs=pl.BlockSpec(memory_space=VMEM),
        cost_estimate=pl.CostEstimate(
            flops=10**7, bytes_accessed=(last - first) * 10**6, transcendentals=0
        ),
        compiler_params=pltpu.CompilerParams(vmem_limit_bytes=GRANT),
        name="pairs",
    )(ranges, keys, own, packed, scale, start)


def neighbourhood(counts, along_rows):
    reach = [(-1, 0, 1) if n >= 3 else (0, 1) if n == 2 else (0,) for n in counts]
    inner = [(-i) % counts[0] for i in reach[0]]
    stacked = jnp.stack(along_rows)
    if counts[1] * counts[2] <= 16:
        near = everyone(stacked, ("qc", "grp"))

        def pick():
            column, layer = lax.axis_index("qc"), lax.axis_index("grp")
            outer = [
                lax.rem(column + (j % counts[1]), counts[1]) * counts[2]
                + lax.rem(layer + k, counts[2])
                for j in reach[1]
                for k in ((k % counts[2]) for k in reach[2])
            ]
            return [(o, i) for i in inner for o in outer]

        return near, pick
    near = stacked[None]
    for axis, count in (("grp", counts[2]), ("qc", counts[1])):
        ahead = [((i + 1) % count, i) for i in range(count)]
        behind = [(i, (i + 1) % count) for i in range(count)]
        if count >= 3:
            near = jnp.concatenate(
                [lax.ppermute(near, axis, behind), near, lax.ppermute(near, axis, ahead)]
            )
        elif count == 2:
            near = jnp.concatenate([near, lax.ppermute(near, axis, ahead)])
    outer = range(near.shape[0])
    return near, lambda: [(o, i) for i in inner for o in outer]


def crossed(value, axis):
    count = lax.axis_size(axis)
    if count & (count - 1):
        return rotated(value, axis), [lambda me, k=k: modulo(me - k, count) for k in range(count)]
    return (
        [value]
        + [lax.ppermute(value, axis, [(i, i ^ k) for i in range(count)]) for k in range(1, count)],
        [lambda me, k=k: me ^ k for k in range(count)],
    )


def per_device(
    kohn_sham, pattern, basis_centers, occupations, atoms, neighbours, emb_atom, emb_dest, emb_block
):
    counts = tuple(lax.axis_size(axis) for axis in ALL)
    layers = counts[2]
    order = kohn_sham.shape[0]
    width = order // layers
    record_count = emb_atom.shape[0]
    own = atoms.reshape(4, SUB, LANES)
    after = lax.optimization_barrier

    left_own, right_own, packet = prepare(width, kohn_sham, own, basis_centers, occupations[None])
    packets = rotated(packet, "qr")
    rights = rotated(right_own, "qr")
    lefts, places = crossed(left_own, "qc")
    keys, ranges = sorting(counts, neighbours[0, 0, 0])
    near, pick = neighbourhood(counts, [piece[:4] for piece in packets])
    domains = min(3, counts[0]) * min(3, counts[1]) * min(3, counts[2])

    field, embed_force = embedding(
        order,
        packets,
        emb_atom.reshape(1, record_count),
        emb_dest.reshape(1, record_count),
        emb_block.reshape(1, record_count),
    )

    def from_layers(send):
        if layers == 2:
            return lax.ppermute(send, "grp", [(0, 1), (1, 0)])
        got = lax.all_to_all(
            send.reshape(layers, width, order), "grp", split_axis=0, concat_axis=0, tiled=True
        )
        other = jnp.arange(layers)[:, None, None] != lax.axis_index("grp")
        return jnp.sum(jnp.where(other, got.astype(jnp.float32), 0.0), axis=0)

    blocks = keys.shape[0] // BATCH
    cuts = (0, blocks // 4, 3 * blocks // 4, blocks)

    mine, send, table = product_part(pattern, lefts, places, rights)
    got = from_layers(send)
    field_all = everyone(field, ALL)

    packed, scale = packing(pick, domains, near)
    mine, packed = after((mine, packed))
    force = pair_forces(cuts[0], cuts[1], ranges, keys, own, packed, scale, embed_force)
    got, force = after((got, force))
    product_rows = (mine + got.astype(jnp.float32)).astype(jnp.bfloat16)
    product_rows, force = after((product_rows, force))
    products = rotated(product_rows, "qr")
    force = pair_forces(cuts[1], cuts[2], ranges, keys, own, packed, scale, force)
    rows, columns = whole_field(field_all)
    *received, force = after((*products[1:], force))
    products = [products[0]] + received

    mine, send = cube_part(pattern, table, rows, columns, products, rights)
    got = from_layers(send)
    mine, force = after((mine, force))
    force = pair_forces(cuts[2], cuts[3], ranges, keys, own, packed, scale, force)
    got, force = after((got, force))
    sign_step = final_step(mine, got, right_own, columns)
    return (sign_step, force.reshape(3, 1, 1, 1, SUB * LANES))


def solution(mesh):
    in_specs = (
        P("qr", "qc"),
        P("qr", "qc"),
        P(None, "qr"),
        P("qr"),
        P(None, "qr", "qc", "grp", None),
        P("qr", "qc", "grp", None, None, None),
        P(("qr", "qc", "grp")),
        P(("qr", "qc", "grp"), None),
        P(("qr", "qc", "grp")),
    )
    out_specs = (P(("qr", "grp"), "qc"), P(None, "qr", "qc", "grp", None))
    return jax.shard_map(
        per_device, mesh=mesh, in_specs=in_specs, out_specs=out_specs, check_vma=False
    )
```

```python
import functools

import jax
import jax.numpy as jnp
from jax import lax
from jax.experimental import pallas as pl
from jax.experimental.pallas import tpu as pltpu
from jax.sharding import PartitionSpec as P

BLOCK = 64
SUB, LANES = 8, 128

coulomb = 138.935
hartree_nm = 0.0529177
soften = 0.01
domain_edge = 3.4

ALL = ("qr", "qc", "grp")
VMEM = pltpu.MemorySpace.VMEM
GRANT = 16 << 20
SMEM = pltpu.MemorySpace.SMEM

LANE_PICK = lax.GatherDimensionNumbers(
    offset_dims=(),
    collapsed_slice_dims=(1,),
    start_index_map=(1,),
    operand_batching_dims=(0,),
    start_indices_batching_dims=(0,),
)


def pick_lanes(row, lane):
    return lax.gather(
        row, lane[..., None], LANE_PICK, (1, 1), mode=lax.GatherScatterMode.PROMISE_IN_BOUNDS
    )


def everyone(value, axes):
    count = 1
    for axis in (axes,) if isinstance(axes, str) else axes:
        count *= lax.axis_size(axis)
    copies = jnp.broadcast_to(value[None], (count,) + value.shape)
    return lax.all_to_all(copies, axes, split_axis=0, concat_axis=0, tiled=True)


def rotated(value, axis):
    count = lax.axis_size(axis)
    return [value] + [
        lax.ppermute(value, axis, [(i, (i + k) % count) for i in range(count)])
        for k in range(1, count)
    ]


def thirds(value):
    high = value.astype(jnp.bfloat16)
    rest = value - high.astype(jnp.float32)
    middle = rest.astype(jnp.bfloat16)
    low = (rest - middle.astype(jnp.float32)).astype(jnp.bfloat16)
    return high, middle, low


def prepare_kernel(
    matrix_ref,
    atoms_ref,
    centers_ref,
    weights_ref,
    left_ref,
    right_ref,
    packet_ref,
    matrix_buf,
    centers_buf,
    weights_buf,
    sems,
):
    order, width = left_ref.shape
    layer = lax.axis_index("grp")
    copies = [
        pltpu.make_async_copy(matrix_ref, matrix_buf, sems.at[0]),
        pltpu.make_async_copy(atoms_ref, packet_ref.at[0:4], sems.at[1]),
        pltpu.make_async_copy(centers_ref, centers_buf, sems.at[2]),
        pltpu.make_async_copy(weights_ref, weights_buf, sems.at[3]),
    ]
    for copy in copies:
        copy.start()
    copies[2].wait()
    copies[3].wait()
    lines = order // LANES
    rows = [
        centers_buf[c : c + 1, n * LANES : (n + 1) * LANES] for c in range(3) for n in range(lines)
    ]
    rows = rows + [weights_buf[n * LANES : (n + 1) * LANES].reshape(1, LANES) for n in range(lines)]
    planes = packet_ref.shape[0] - 4
    rows = rows + [jnp.zeros((1, LANES), jnp.float32)] * (planes * SUB - len(rows))
    for n in range(planes):
        packet_ref[4 + n] = jnp.concatenate(rows[n * SUB : (n + 1) * SUB], axis=0)
    copies[0].wait()
    right_ref[...] = matrix_buf[pl.ds(pl.multiple_of(layer * width, width), width), :]
    for i in range(order // width):

        @pl.when(layer == i)
        def _():
            left_ref[...] = matrix_buf[:, i * width : (i + 1) * width]

    copies[1].wait()


def prepare(width, matrix, atoms, centers, weights):
    order = matrix.shape[0]
    planes = -(-4 * (order // LANES) // SUB)
    return pl.pallas_call(
        prepare_kernel,
        out_shape=(
            jax.ShapeDtypeStruct((order, width), matrix.dtype),
            jax.ShapeDtypeStruct((width, order), matrix.dtype),
            jax.ShapeDtypeStruct((4 + planes, SUB, LANES), jnp.float32),
        ),
        in_specs=[pl.BlockSpec(memory_space=pltpu.MemorySpace.HBM)] * 4,
        out_specs=(pl.BlockSpec(memory_space=VMEM),) * 3,
        scratch_shapes=[
            pltpu.VMEM(matrix.shape, matrix.dtype),
            pltpu.VMEM(centers.shape, centers.dtype),
            pltpu.VMEM(weights.shape, weights.dtype),
            pltpu.SemaphoreType.DMA((4,)),
        ],
        cost_estimate=pl.CostEstimate(flops=10**6, bytes_accessed=10**6, transcendentals=0),
        compiler_params=pltpu.CompilerParams(vmem_limit_bytes=GRANT),
        name="prepare",
    )(matrix, atoms, centers, weights)


def records_kernel(extent, lines, *refs):
    packet_refs = refs[:extent]
    pick_ref, dest_ref, block_ref, field_ref, force_ref = refs[extent:]
    count = pick_ref.shape[1]
    here = [lax.axis_index(axis) for axis in ALL]
    anchor = [place.astype(jnp.float32) * domain_edge for place in here]
    pick, dest, block = pick_ref[...], dest_ref[...], block_ref[...]
    lane, group = pick & (LANES - 1), pick >> 7
    behind = here[0] - dest
    behind = jnp.where(behind < 0, behind + extent, behind)
    iota = functools.partial(lax.broadcasted_iota, jnp.int32)
    one_lane = (iota((LANES, count), 0) == lane).astype(jnp.bfloat16)
    in_group = iota((SUB, count), 0) == group
    half = block >> 1
    odd = (block & 1) == 1
    one_line = (iota((extent * lines, count), 0) == behind * lines + half).astype(jnp.bfloat16)
    one_out = (iota((extent * lines, count), 0) == dest * lines + half).astype(jnp.bfloat16)

    def exact(product, value):
        high, middle, low = thirds(value)
        return product(high) + product(middle) + product(low)

    def dot(contract):
        return lambda other: lambda value: lax.dot_general(
            value, other, (contract, ((), ())), preferred_element_type=jnp.float32
        )

    own = packet_refs[0]
    atoms = jnp.concatenate([own[c] for c in range(4)], axis=0)
    spread = exact(dot(((1,), (0,)))(one_lane), atoms)
    taken = [
        jnp.sum(jnp.where(in_group, spread[c * SUB : (c + 1) * SUB], 0.0), axis=0, keepdims=True)
        for c in range(4)
    ]

    def line(k, n):
        return packet_refs[k][4 + n // SUB, n % SUB : n % SUB + 1, :]

    def chosen(c):
        table = jnp.concatenate(
            [line(k, c * lines + n) for k in range(extent) for n in range(lines)], axis=0
        )
        both = exact(dot(((0,), (0,)))(one_line), table)
        return jnp.where(odd, both[BLOCK:], both[:BLOCK])

    charge = taken[3]
    offset = [taken[c] + anchor[c] - chosen(c) for c in range(3)]
    weight = chosen(3)
    distance = offset[0] * offset[0] + offset[1] * offset[1] + offset[2] * offset[2] + soften
    inverse = lax.rsqrt(distance)
    terms = hartree_nm * charge * inverse
    terms = jnp.concatenate([jnp.where(odd, 0.0, terms), jnp.where(odd, terms, 0.0)], axis=0)
    high, middle, low = thirds(terms)
    field_ref[...] = sum(
        lax.dot_general(one_out, piece, (((1,), (1,)), ((), ())), preferred_element_type=jnp.float32)
        for piece in (high, middle, low)
    )
    strength = weight * (inverse * inverse * inverse)
    pushes = [
        coulomb * charge * jnp.sum(strength * offset[c], axis=0, keepdims=True) for c in range(3)
    ]
    pushes = jnp.concatenate([jnp.where(in_group, push, 0.0) for push in pushes], axis=0)
    total = exact(dot(((1,), (1,)))(one_lane), pushes)
    for c in range(3):
        force_ref[c] = total[c * SUB : (c + 1) * SUB]


def embedding(order, packets, pick, dest, block):
    extent, lines = len(packets), order // LANES
    return pl.pallas_call(
        functools.partial(records_kernel, extent, lines),
        out_shape=(
            jax.ShapeDtypeStruct((extent * lines, LANES), jnp.float32),
            jax.ShapeDtypeStruct((3, SUB, LANES), jnp.float32),
        ),
        in_specs=[pl.BlockSpec(memory_space=VMEM)] * (extent + 3),
        out_specs=(pl.BlockSpec(memory_space=VMEM),) * 2,
        cost_estimate=pl.CostEstimate(flops=10**7, bytes_accessed=5 * 10**6, transcendentals=0),
        compiler_params=pltpu.CompilerParams(vmem_limit_bytes=GRANT),
        name="embedding",
    )(*packets, pick, dest, block)


def field_kernel(parts_ref, rows_ref, columns_ref):
    total = parts_ref[0]
    for k in range(1, parts_ref.shape[0]):
        total = total + parts_ref[k]
    rows_ref[...] = total
    for n in range(total.shape[0]):
        columns_ref[n * LANES : (n + 1) * LANES, :] = jnp.broadcast_to(
            total[n : n + 1], (LANES, LANES)
        ).T


def whole_field(parts):
    lines = parts.shape[1]
    return pl.pallas_call(
        field_kernel,
        out_shape=(
            jax.ShapeDtypeStruct((lines, LANES), jnp.float32),
            jax.ShapeDtypeStruct((lines * LANES, LANES), jnp.float32),
        ),
        in_specs=[pl.BlockSpec(memory_space=VMEM)],
        out_specs=(pl.BlockSpec(memory_space=VMEM),) * 2,
        cost_estimate=pl.CostEstimate(flops=10**6, bytes_accessed=3 * 10**6, transcendentals=0),
        compiler_params=pltpu.CompilerParams(vmem_limit_bytes=GRANT),
        name="field",
    )(parts)


def modulo(value, count):
    return jnp.where(value < 0, value + count, value)


def keep_pattern(pattern_ref, value):
    blocks = pattern_ref.shape[0]
    which = lax.broadcasted_iota(jnp.int32, (1, value.shape[1]), 1) // BLOCK
    out = []
    for a in range(blocks):
        marks = jnp.zeros((1, value.shape[1]), jnp.int32)
        for b in range(blocks):
            marks = jnp.where(which == b, pattern_ref[a, b], marks)
        out.append(jnp.where(marks == 1, value[a * BLOCK : (a + 1) * BLOCK], 0.0))
    return jnp.concatenate(out, axis=0)


def part_outputs(layers, value, hold_ref, mine_ref, send_ref):
    width = mine_ref.shape[0]
    layer = lax.axis_index("grp")
    hold_ref[...] = value
    mine_ref[...] = hold_ref[pl.ds(pl.multiple_of(layer * width, width), width), :]
    if layers == 2:
        send_ref[...] = hold_ref[
            pl.ds(pl.multiple_of((1 - layer) * width, width), width), :
        ].astype(send_ref.dtype)
    else:
        send_ref[...] = value.astype(send_ref.dtype)


def product_kernel(places, pattern_ref, *refs):
    extent = len(refs) - 4 - len(places)
    left_refs, right_refs = refs[: len(places)], refs[len(places) : len(places) + extent]
    mine_ref, send_ref, table_ref, hold_ref = refs[len(places) + extent :]
    row, column = lax.axis_index("qr"), lax.axis_index("qc")
    for left_ref, place in zip(left_refs, places):
        table_ref[place(column)] = left_ref[...]
    total = jnp.zeros(hold_ref.shape, jnp.float32)
    for k in range(extent):
        total = total + jnp.dot(
            table_ref[modulo(row - k, extent)],
            right_refs[k][...],
            preferred_element_type=jnp.float32,
        )
    part_outputs(
        hold_ref.shape[0] // mine_ref.shape[0],
        keep_pattern(pattern_ref, total),
        hold_ref,
        mine_ref,
        send_ref,
    )


def part_shapes(order, width):
    rows = width if order == 2 * width else order
    return (
        jax.ShapeDtypeStruct((width, order), jnp.float32),
        jax.ShapeDtypeStruct((rows, order), jnp.bfloat16),
    )


def product_part(pattern, lefts, places, rights):
    order, width = lefts[0].shape
    inputs = len(lefts) + len(rights)
    return pl.pallas_call(
        functools.partial(product_kernel, places),
        out_shape=part_shapes(order, width)
        + (jax.ShapeDtypeStruct((len(lefts), order, width), jnp.bfloat16),),
        in_specs=[pl.BlockSpec(memory_space=SMEM)] + [pl.BlockSpec(memory_space=VMEM)] * inputs,
        out_specs=(pl.BlockSpec(memory_space=VMEM),) * 3,
        scratch_shapes=[pltpu.VMEM((order, order), jnp.float32)],
        cost_estimate=pl.CostEstimate(
            flops=2 * order * order * width * len(rights),
            bytes_accessed=3 * 10**6,
            transcendentals=0,
        ),
        compiler_params=pltpu.CompilerParams(vmem_limit_bytes=GRANT),
        name="product",
    )(pattern, *lefts, *rights)


def cube_kernel(pattern_ref, table_ref, rows_ref, columns_ref, *refs):
    extent = (len(refs) - 3) // 2
    product_refs, right_refs = refs[:extent], refs[extent : 2 * extent]
    mine_ref, send_ref, hold_ref = refs[2 * extent :]
    width, order = mine_ref.shape
    lines = order // LANES
    row, column, layer = (lax.axis_index(axis) for axis in ALL)
    first = layer * width
    iota = functools.partial(lax.broadcasted_iota, jnp.int32)
    total = jnp.zeros((order, order), jnp.float32)
    for k in range(extent):
        tile = modulo(row - k, extent)
        down = columns_ref[pl.ds(pl.multiple_of(tile * order + first, width), width), :]
        pieces = []
        for n in range(lines):
            spot = slice(n * LANES, (n + 1) * LANES)
            across = rows_ref[pl.ds(column * lines + n, 1), :]
            matrix = right_refs[k][:, spot].astype(jnp.float32)
            on_diagonal = iota((width, LANES), 0) + first == iota((width, LANES), 1) + n * LANES
            corner = jnp.where(on_diagonal & (tile == column), down * down, 0.0)
            piece = product_refs[k][:, spot].astype(jnp.float32) + matrix * (down + across) + corner
            pieces.append(piece.astype(jnp.bfloat16))
        square = jnp.concatenate(pieces, axis=1)
        operand = table_ref[tile]
        if k == 0:
            own = columns_ref[pl.ds(pl.multiple_of(row * order, order), order), :]
            parts = []
            for start in range(0, width, LANES):
                size = min(LANES, width - start)
                shape = (order, size)
                on_diagonal = iota(shape, 0) == iota(shape, 1) + (first + start)
                parts.append(jnp.where(on_diagonal, own[:, :size], 0.0))
            added = parts[0] if len(parts) == 1 else jnp.concatenate(parts, axis=1)
            operand = (operand.astype(jnp.float32) + added).astype(jnp.bfloat16)
        total = total + jnp.dot(operand, square, preferred_element_type=jnp.float32)
    part_outputs(
        order // width, keep_pattern(pattern_ref, total), hold_ref, mine_ref, send_ref
    )


def cube_part(pattern, table, rows, columns, products, rights):
    _, order, width = table.shape
    inputs = 3 + len(products) + len(rights)
    return pl.pallas_call(
        cube_kernel,
        out_shape=part_shapes(order, width),
        in_specs=[pl.BlockSpec(memory_space=SMEM)] + [pl.BlockSpec(memory_space=VMEM)] * inputs,
        out_specs=(pl.BlockSpec(memory_space=VMEM),) * 2,
        scratch_shapes=[pltpu.VMEM((order, order), jnp.float32)],
        cost_estimate=pl.CostEstimate(
            flops=2 * order * order * width * len(rights),
            bytes_accessed=3 * 10**6,
            transcendentals=0,
        ),
        compiler_params=pltpu.CompilerParams(vmem_limit_bytes=GRANT),
        name="cube",
    )(pattern, table, rows, columns, *products, *rights)


def final_kernel(mine_ref, got_ref, right_ref, columns_ref, out_ref):
    width, order = mine_ref.shape
    row, column, layer = (lax.axis_index(axis) for axis in ALL)
    first = layer * width
    down = columns_ref[pl.ds(pl.multiple_of(row * order + first, width), width), :]
    iota = functools.partial(lax.broadcasted_iota, jnp.int32)
    for n in range(order // LANES):
        spot = slice(n * LANES, (n + 1) * LANES)
        on_diagonal = iota((width, LANES), 0) + first == iota((width, LANES), 1) + n * LANES
        added = jnp.where(on_diagonal & (row == column), down, 0.0)
        shifted = (right_ref[:, spot].astype(jnp.float32) + added).astype(jnp.bfloat16)
        cube = mine_ref[:, spot] + got_ref[:, spot].astype(jnp.float32)
        out_ref[:, spot] = (0.5 * (3.0 * shifted.astype(jnp.float32) - cube)).astype(jnp.bfloat16)


def final_step(mine, got, right, columns):
    return pl.pallas_call(
        final_kernel,
        out_shape=jax.ShapeDtypeStruct(mine.shape, jnp.bfloat16),
        in_specs=[pl.BlockSpec(memory_space=VMEM)] * 4,
        out_specs=pl.BlockSpec(memory_space=VMEM),
        cost_estimate=pl.CostEstimate(flops=10**6, bytes_accessed=10**6, transcendentals=0),
        compiler_params=pltpu.CompilerParams(vmem_limit_bytes=GRANT),
        name="final",
    )(mine, got, right, columns)


KEY_BITS = 8
GROUP_BITS = 3
BATCH = 8
CHUNK = 24


def packing_kernel(pick, domains, near_ref, packed_ref, scale_ref):
    picks = pick()

    def entry(d, c):
        outer, inner = picks[d]
        return near_ref[outer, inner, c]

    low = [entry(0, c) for c in range(4)]
    high = list(low)
    for d in range(1, domains):
        for c in range(4):
            value = entry(d, c)
            low[c] = jnp.minimum(low[c], value)
            high[c] = jnp.maximum(high[c], value)
    steps = 65535.0
    base, back = [], []
    for c in range(4):
        least = jnp.min(low[c], axis=(0, 1), keepdims=True)
        width = jnp.maximum(jnp.max(high[c], axis=(0, 1), keepdims=True) - least, 1e-30)
        base.append(jnp.broadcast_to(least, (SUB, LANES)))
        back.append(jnp.broadcast_to(steps / width, (SUB, LANES)))
        scale_ref[c] = base[c]
        scale_ref[4 + c] = jnp.broadcast_to(width * (1.0 / steps), (SUB, LANES))
    for d in range(domains):
        code = [
            jnp.clip((entry(d, c) - base[c]) * back[c] + 0.5, 0.0, steps).astype(jnp.int32)
            for c in range(4)
        ]
        start = (SUB - 1) * domains + d * SUB
        packed_ref[0, start : start + SUB, :] = code[0] | (code[1] << 16)
        packed_ref[1, start : start + SUB, :] = code[2] | (code[3] << 16)
    front, size = (SUB - 1) * domains, domains * SUB
    for w in range(2):
        packed_ref[w, :front, :] = jnp.zeros((front, LANES), jnp.int32)
        packed_ref[w, front + size :, :] = jnp.zeros((front + CHUNK, LANES), jnp.int32)


def packing(pick, domains, near):
    return pl.pallas_call(
        functools.partial(packing_kernel, pick, domains),
        out_shape=(
            jax.ShapeDtypeStruct(
                (2, domains * SUB + 2 * (SUB - 1) * domains + CHUNK, LANES), jnp.int32
            ),
            jax.ShapeDtypeStruct((8, SUB, LANES), jnp.float32),
        ),
        in_specs=[pl.BlockSpec(memory_space=VMEM)],
        out_specs=(pl.BlockSpec(memory_space=VMEM),) * 2,
        cost_estimate=pl.CostEstimate(flops=10**7, bytes_accessed=5 * 10**6, transcendentals=0),
        compiler_params=pltpu.CompilerParams(vmem_limit_bytes=GRANT),
        name="packing",
    )(near)


def compact(place, count):
    if count >= 3:
        return place
    if count == 2:
        return jnp.where(place == 1, 0, 1)
    return jnp.zeros_like(place)


def places_of(slot):
    p = (slot * 57) >> 9
    rest = slot - 9 * p
    q = (rest * 11) >> 5
    return p, q, rest - 3 * q


def network(count):
    pairs = []
    p = 1
    while p < count:
        k = p
        while k >= 1:
            for j in range(k % p, count - k, 2 * k):
                for i in range(min(k, count - j - k)):
                    if (i + j) // (2 * p) == (i + j + k) // (2 * p):
                        pairs.append((i + j, i + j + k))
            k //= 2
        p *= 2
    return pairs


def sorting_kernel(counts, lists_ref, keys_ref, range_ref, spread_ref):
    entries = lists_ref.shape[1]
    distinct = [min(3, count) for count in counts]
    domains = distinct[0] * distinct[1] * distinct[2]
    keys = []
    for b in range(entries // SUB):
        for a in range(SUB):
            slot = lists_ref[0, b * SUB : (b + 1) * SUB, a * LANES : (a + 1) * LANES]
            member = lists_ref[1, b * SUB : (b + 1) * SUB, a * LANES : (a + 1) * LANES]
            p, q, r = places_of(slot)
            domain = (
                compact(p, counts[0]) * distinct[1] + compact(q, counts[1])
            ) * distinct[2] + compact(r, counts[2])
            key = ((domain * (SUB * LANES) + member) << KEY_BITS) + (slot << GROUP_BITS) + a
            keys.append(key.astype(jnp.float32))
    size = len(keys)
    sublane = lax.broadcasted_iota(jnp.int32, (SUB, LANES), 0)

    def turned(values, bit):
        sign = jnp.where((sublane >> bit) & 1 == 1, -1.0, 1.0)
        return [value * sign for value in values]

    def by_sublane(values):
        for v in range(size):
            spread_ref[pl.ds(v, SUB, stride=size), :] = values[v]
        return [spread_ref[n * SUB : (n + 1) * SUB, :] for n in range(size)]

    def by_register(values):
        for n in range(size):
            spread_ref[n * SUB : (n + 1) * SUB, :] = values[n]
        return [spread_ref[pl.ds(v, SUB, stride=size), :] for v in range(size)]

    def exchange(values, i, j, up=True):
        low, high = jnp.minimum(values[i], values[j]), jnp.maximum(values[i], values[j])
        values[i], values[j] = (low, high) if up else (high, low)

    keys = turned(keys, 0)
    for i, j in network(size):
        exchange(keys, i, j)
    keys = turned(keys, 0)
    run = size // SUB
    for level in range(1, 4):
        keys = by_sublane(keys)
        for step in reversed(range(level)):
            for s in range(SUB):
                if not s >> step & 1:
                    for n in range(run):
                        exchange(
                            keys,
                            s * run + n,
                            (s | 1 << step) * run + n,
                            level == 3 or not s >> level & 1,
                        )
        keys = by_register(keys)
        if level < 3:
            keys = turned(keys, level)
        stride = size // 2
        while stride:
            for v in range(size):
                if not v & stride:
                    exchange(keys, v, v | stride)
            stride //= 2
        if level < 3:
            keys = turned(keys, level)

    whole = [key.astype(jnp.int32) for key in keys]
    for v in range(size):
        keys_ref[v] = whole[v]
    base = sublane * domains
    lows = [(whole[v] >> (KEY_BITS + 7)) - base for v in range(0, size, BATCH)]
    highs = [(whole[v + BATCH - 1] >> (KEY_BITS + 7)) - base for v in range(0, size, BATCH)]
    least = jnp.concatenate(
        [jnp.min(low.astype(jnp.float32), axis=0, keepdims=True) for low in lows], axis=0
    )
    most = jnp.concatenate(
        [jnp.max(high.astype(jnp.float32), axis=0, keepdims=True) for high in highs], axis=0
    )
    least = jnp.min(least, axis=1, keepdims=True)
    most = jnp.max(most, axis=1, keepdims=True)
    both = jnp.concatenate([least, most], axis=0).astype(jnp.int32)
    range_ref[...] = jnp.broadcast_to(both, range_ref.shape)


def sorting(counts, lists):
    entries = lists.shape[1]
    return pl.pallas_call(
        functools.partial(sorting_kernel, counts),
        out_shape=(
            jax.ShapeDtypeStruct((entries, SUB, LANES), jnp.int32),
            jax.ShapeDtypeStruct((2 * entries // BATCH, LANES), jnp.int32),
        ),
        in_specs=[pl.BlockSpec(memory_space=VMEM)],
        out_specs=(pl.BlockSpec(memory_space=VMEM),) * 2,
        scratch_shapes=[pltpu.VMEM((entries * SUB, LANES), jnp.float32)],
        cost_estimate=pl.CostEstimate(flops=10**7, bytes_accessed=5 * 10**6, transcendentals=0),
        compiler_params=pltpu.CompilerParams(vmem_limit_bytes=GRANT),
        name="sorting",
    )(lists)


def pair_kernel(
    domains, first, last, range_ref, keys_ref, own_ref, packed_ref, scale_ref, start_ref, force_ref
):
    blocks = keys_ref.shape[0] // BATCH
    front = (SUB - 1) * domains
    base = lax.broadcasted_iota(jnp.int32, (SUB, LANES), 0) * domains

    def step(j, sums):
        keys = [keys_ref[j * BATCH + i] for i in range(BATCH)]
        rows = [(key >> (KEY_BITS + 7)) - base for key in keys]
        lanes = [(key >> KEY_BITS) & (LANES - 1) for key in keys]
        low = range_ref[j, 0]
        rounds = (range_ref[blocks + j, 0] - low) // CHUNK + 1

        def scan(i, words):
            words = list(words)
            start = low + i * CHUNK
            for m in range(BATCH):
                for u in range(CHUNK):
                    here = rows[m] == start + u
                    for w in range(2):
                        lines = packed_ref[w, pl.ds(front + start + u, SUB, stride=domains), :]
                        k = 2 * m + w
                        words[k] = jnp.where(here, pick_lanes(lines, lanes[m]), words[k])
            return tuple(words)

        zero = jnp.zeros((SUB, LANES), jnp.int32)
        words = lax.fori_loop(0, rounds, scan, (zero,) * (2 * BATCH))
        sums = list(sums)
        for m in range(BATCH):
            group = keys[m] & ((1 << GROUP_BITS) - 1)
            places = places_of((keys[m] >> GROUP_BITS) & 31)
            mine = [group == g for g in range(SUB)]
            one, two = words[2 * m], words[2 * m + 1]
            code = [one & 0xFFFF, (one >> 16) & 0xFFFF, two & 0xFFFF, (two >> 16) & 0xFFFF]
            value = [code[c].astype(jnp.float32) * scale_ref[4 + c] + scale_ref[c] for c in range(4)]
            offset = []
            for c in range(3):
                place = own_ref[c, 0:1, :]
                for g in range(1, SUB):
                    place = jnp.where(mine[g], own_ref[c, g : g + 1, :], place)
                shift = (places[c] - 1).astype(jnp.float32) * domain_edge
                offset.append(place - (value[c] + shift))
            distance = (
                offset[0] * offset[0] + offset[1] * offset[1] + offset[2] * offset[2] + soften
            )
            inverse = lax.rsqrt(distance)
            strength = value[3] * (inverse * inverse * inverse)
            for c in range(3):
                push = offset[c] * strength
                for g in range(SUB):
                    k = c * SUB + g
                    sums[k] = sums[k] + jnp.where(mine[g], push, 0.0)
        return tuple(sums)

    zero = jnp.zeros((SUB, LANES), jnp.float32)
    sums = lax.fori_loop(first, last, step, (zero,) * (3 * SUB))
    for c in range(3):
        total = jnp.concatenate(
            [jnp.sum(sums[c * SUB + g], axis=0, keepdims=True) for g in range(SUB)], axis=0
        )
        force_ref[c] = start_ref[c] + coulomb * own_ref[3] * total


def pair_forces(domains, first, last, ranges, keys, own, packed, scale, start):
    return pl.pallas_call(
        functools.partial(pair_kernel, domains, first, last),
        out_shape=jax.ShapeDtypeStruct((3, SUB, LANES), jnp.float32),
        in_specs=[pl.BlockSpec(memory_space=SMEM)] + [pl.BlockSpec(memory_space=VMEM)] * 5,
        out_specs=pl.BlockSpec(memory_space=VMEM),
        cost_estimate=pl.CostEstimate(
            flops=10**7, bytes_accessed=(last - first) * BATCH * 10**5 * 3, transcendentals=0
        ),
        compiler_params=pltpu.CompilerParams(vmem_limit_bytes=GRANT),
        name="pairs",
    )(ranges, keys, own, packed, scale, start)


def neighbourhood(counts, along_rows, earlier):
    reach = [(-1, 0, 1) if n >= 3 else (0, 1) if n == 2 else (0,) for n in counts]
    inner = [(-i) % counts[0] for i in reach[0]]
    stacked, _ = lax.optimization_barrier((jnp.stack(along_rows), earlier))
    if counts[1] * counts[2] <= 16:
        near = everyone(stacked, ("qc", "grp"))

        def pick():
            column, layer = lax.axis_index("qc"), lax.axis_index("grp")
            outer = [
                lax.rem(column + (j % counts[1]), counts[1]) * counts[2]
                + lax.rem(layer + k, counts[2])
                for j in reach[1]
                for k in ((k % counts[2]) for k in reach[2])
            ]
            return [(o, i) for i in inner for o in outer]

        return near, pick
    near = stacked[None]
    for axis, count in (("grp", counts[2]), ("qc", counts[1])):
        ahead = [((i + 1) % count, i) for i in range(count)]
        behind = [(i, (i + 1) % count) for i in range(count)]
        if count >= 3:
            near = jnp.concatenate(
                [lax.ppermute(near, axis, behind), near, lax.ppermute(near, axis, ahead)]
            )
        elif count == 2:
            near = jnp.concatenate([near, lax.ppermute(near, axis, ahead)])
    outer = range(near.shape[0])
    return near, lambda: [(o, i) for i in inner for o in outer]


def crossed(value, axis):
    count = lax.axis_size(axis)
    if count & (count - 1):
        return rotated(value, axis), [lambda me, k=k: modulo(me - k, count) for k in range(count)]
    return (
        [value]
        + [lax.ppermute(value, axis, [(i, i ^ k) for i in range(count)]) for k in range(1, count)],
        [lambda me, k=k: me ^ k for k in range(count)],
    )


def per_device(
    kohn_sham, pattern, basis_centers, occupations, atoms, neighbours, emb_atom, emb_dest, emb_block
):
    counts = tuple(lax.axis_size(axis) for axis in ALL)
    layers = counts[2]
    order = kohn_sham.shape[0]
    width = order // layers
    record_count = emb_atom.shape[0]
    own = atoms.reshape(4, SUB, LANES)
    after = lax.optimization_barrier

    left_own, right_own, packet = prepare(width, kohn_sham, own, basis_centers, occupations)
    rights = rotated(right_own, "qr")
    packets = rotated(packet, "qr")
    lefts, places = crossed(left_own, "qc")
    keys, ranges = sorting(counts, neighbours[0, 0, 0])
    domains = min(3, counts[0]) * min(3, counts[1]) * min(3, counts[2])

    field, embed_force = embedding(
        order,
        packets,
        emb_atom.reshape(1, record_count),
        emb_dest.reshape(1, record_count),
        emb_block.reshape(1, record_count),
    )
    field_all = everyone(field, ALL)

    def from_layers(send):
        if layers == 2:
            return lax.ppermute(send, "grp", [(0, 1), (1, 0)])
        got = lax.all_to_all(
            send.reshape(layers, width, order), "grp", split_axis=0, concat_axis=0, tiled=True
        )
        other = jnp.arange(layers)[:, None, None] != lax.axis_index("grp")
        return jnp.sum(jnp.where(other, got.astype(jnp.float32), 0.0), axis=0)

    blocks = keys.shape[0] // BATCH

    *arrived, keys, field = after((*rights[1:], keys, field))
    mine, send, table = product_part(pattern, lefts, places, [right_own] + arrived)
    near, pick = neighbourhood(counts, [piece[:4] for piece in packets], field_all)
    got = from_layers(send)
    rows, columns = whole_field(field_all)
    product_rows = (mine + got.astype(jnp.float32)).astype(jnp.bfloat16)
    products = rotated(product_rows, "qr")
    packed, scale = packing(pick, domains, near)
    force = pair_forces(domains, 0, blocks, ranges, keys, own, packed, scale, embed_force)
    *received, force = after((*products[1:], force))
    products = [products[0]] + received

    mine, send = cube_part(pattern, table, rows, columns, products, rights)
    got = from_layers(send)
    sign_step = final_step(mine, got, right_own, columns)
    return (sign_step, force.reshape(3, 1, 1, 1, SUB * LANES))


def solution(mesh):
    in_specs = (
        P("qr", "qc"),
        P("qr", "qc"),
        P(None, "qr"),
        P("qr"),
        P(None, "qr", "qc", "grp", None),
        P("qr", "qc", "grp", None, None, None),
        P(("qr", "qc", "grp")),
        P(("qr", "qc", "grp"), None),
        P(("qr", "qc", "grp")),
    )
    out_specs = (P(("qr", "grp"), "qc"), P(None, "qr", "qc", "grp", None))
    return jax.shard_map(
        per_device, mesh=mesh, in_specs=in_specs, out_specs=out_specs, check_vma=False
    )
```

```python
import functools

import jax
import jax.numpy as jnp
from jax import lax
from jax.experimental import pallas as pl
from jax.experimental.pallas import tpu as pltpu
from jax.sharding import PartitionSpec as P


BLOCK = 64
SUB, LANES = 8, 128

coulomb = 138.935
hartree_nm = 0.0529177
soften = 0.01
domain_edge = 3.4

ALL = ("qr", "qc", "grp")
VMEM = pltpu.MemorySpace.VMEM
GRANT = 16 << 20
SMEM = pltpu.MemorySpace.SMEM

LANE_PICK = lax.GatherDimensionNumbers(
    offset_dims=(),
    collapsed_slice_dims=(1,),
    start_index_map=(1,),
    operand_batching_dims=(0,),
    start_indices_batching_dims=(0,),
)


def pick_lanes(row, lane):
    return lax.gather(
        row, lane[..., None], LANE_PICK, (1, 1), mode=lax.GatherScatterMode.PROMISE_IN_BOUNDS
    )


def everyone(value, axes):
    count = 1
    for axis in (axes,) if isinstance(axes, str) else axes:
        count *= lax.axis_size(axis)
    copies = jnp.broadcast_to(value[None], (count,) + value.shape)
    return lax.all_to_all(copies, axes, split_axis=0, concat_axis=0, tiled=True)


def rotated(value, axis):
    count = lax.axis_size(axis)
    return [value] + [
        lax.ppermute(value, axis, [(i, (i + k) % count) for i in range(count)])
        for k in range(1, count)
    ]


def in_place(*values):
    return [pltpu.with_memory_space_constraint(value, pltpu.MemorySpace.HBM) for value in values]


def thirds(value):
    high = value.astype(jnp.bfloat16)
    rest = value - high.astype(jnp.float32)
    middle = rest.astype(jnp.bfloat16)
    low = (rest - middle.astype(jnp.float32)).astype(jnp.bfloat16)
    return high, middle, low


def prepare_kernel(
    matrix_ref,
    atoms_ref,
    centers_ref,
    weights_ref,
    left_ref,
    right_ref,
    packet_ref,
    matrix_buf,
    centers_buf,
    weights_buf,
    sems,
):
    order, width = left_ref.shape
    layer = lax.axis_index("grp")
    copies = [
        pltpu.make_async_copy(matrix_ref, matrix_buf, sems.at[0]),
        pltpu.make_async_copy(atoms_ref, packet_ref.at[0:4], sems.at[1]),
        pltpu.make_async_copy(centers_ref, centers_buf, sems.at[2]),
        pltpu.make_async_copy(weights_ref, weights_buf, sems.at[3]),
    ]
    for copy in copies:
        copy.start()
    copies[2].wait()
    copies[3].wait()
    lines = order // LANES
    rows = [
        centers_buf[c : c + 1, n * LANES : (n + 1) * LANES] for c in range(3) for n in range(lines)
    ]
    rows = rows + [weights_buf[n * LANES : (n + 1) * LANES].reshape(1, LANES) for n in range(lines)]
    planes = packet_ref.shape[0] - 4
    rows = rows + [jnp.zeros((1, LANES), jnp.float32)] * (planes * SUB - len(rows))
    for n in range(planes):
        packet_ref[4 + n] = jnp.concatenate(rows[n * SUB : (n + 1) * SUB], axis=0)
    copies[0].wait()
    right_ref[...] = matrix_buf[pl.ds(pl.multiple_of(layer * width, width), width), :]
    for i in range(order // width):

        @pl.when(layer == i)
        def _():
            left_ref[...] = matrix_buf[:, i * width : (i + 1) * width]

    copies[1].wait()


def prepare(width, matrix, atoms, centers, weights):
    order = matrix.shape[0]
    planes = -(-4 * (order // LANES) // SUB)
    return pl.pallas_call(
        prepare_kernel,
        out_shape=(
            jax.ShapeDtypeStruct((order, width), matrix.dtype),
            jax.ShapeDtypeStruct((width, order), matrix.dtype),
            jax.ShapeDtypeStruct((4 + planes, SUB, LANES), jnp.float32),
        ),
        in_specs=[pl.BlockSpec(memory_space=pltpu.MemorySpace.HBM)] * 4,
        out_specs=(pl.BlockSpec(memory_space=VMEM),) * 3,
        scratch_shapes=[
            pltpu.VMEM(matrix.shape, matrix.dtype),
            pltpu.VMEM(centers.shape, centers.dtype),
            pltpu.VMEM(weights.shape, weights.dtype),
            pltpu.SemaphoreType.DMA((4,)),
        ],
        cost_estimate=pl.CostEstimate(flops=10**6, bytes_accessed=10**6, transcendentals=0),
        compiler_params=pltpu.CompilerParams(vmem_limit_bytes=GRANT),
        name="prepare",
    )(*in_place(matrix, atoms, centers, weights))


def records_kernel(extent, lines, *refs):
    packet_refs = refs[:extent]
    pick_ref, dest_ref, block_ref, field_ref, force_ref = refs[extent:]
    count = pick_ref.shape[1]
    here = [lax.axis_index(axis) for axis in ALL]
    anchor = [place.astype(jnp.float32) * domain_edge for place in here]
    pick, dest, block = pick_ref[...], dest_ref[...], block_ref[...]
    lane, group = pick & (LANES - 1), pick >> 7
    behind = here[0] - dest
    behind = jnp.where(behind < 0, behind + extent, behind)
    iota = functools.partial(lax.broadcasted_iota, jnp.int32)
    one_lane = (iota((LANES, count), 0) == lane).astype(jnp.bfloat16)
    in_group = iota((SUB, count), 0) == group
    half = block >> 1
    odd = (block & 1) == 1
    one_line = (iota((extent * lines, count), 0) == behind * lines + half).astype(jnp.bfloat16)
    one_out = (iota((extent * lines, count), 0) == dest * lines + half).astype(jnp.bfloat16)

    def exact(product, value):
        high, middle, low = thirds(value)
        return product(high) + product(middle) + product(low)

    def dot(contract):
        return lambda other: lambda value: lax.dot_general(
            value, other, (contract, ((), ())), preferred_element_type=jnp.float32
        )

    own = packet_refs[0]
    atoms = jnp.concatenate([own[c] for c in range(4)], axis=0)
    spread = exact(dot(((1,), (0,)))(one_lane), atoms)
    taken = [
        jnp.sum(jnp.where(in_group, spread[c * SUB : (c + 1) * SUB], 0.0), axis=0, keepdims=True)
        for c in range(4)
    ]

    def line(k, n):
        return packet_refs[k][4 + n // SUB, n % SUB : n % SUB + 1, :]

    def chosen(c):
        table = jnp.concatenate(
            [line(k, c * lines + n) for k in range(extent) for n in range(lines)], axis=0
        )
        both = exact(dot(((0,), (0,)))(one_line), table)
        return jnp.where(odd, both[BLOCK:], both[:BLOCK])

    charge = taken[3]
    offset = [taken[c] + anchor[c] - chosen(c) for c in range(3)]
    weight = chosen(3)
    distance = offset[0] * offset[0] + offset[1] * offset[1] + offset[2] * offset[2] + soften
    inverse = lax.rsqrt(distance)
    terms = hartree_nm * charge * inverse
    terms = jnp.concatenate([jnp.where(odd, 0.0, terms), jnp.where(odd, terms, 0.0)], axis=0)
    high, middle, low = thirds(terms)
    field_ref[...] = sum(
        lax.dot_general(one_out, piece, (((1,), (1,)), ((), ())), preferred_element_type=jnp.float32)
        for piece in (high, middle, low)
    )
    strength = weight * (inverse * inverse * inverse)
    pushes = [
        coulomb * charge * jnp.sum(strength * offset[c], axis=0, keepdims=True) for c in range(3)
    ]
    pushes = jnp.concatenate([jnp.where(in_group, push, 0.0) for push in pushes], axis=0)
    total = exact(dot(((1,), (1,)))(one_lane), pushes)
    for c in range(3):
        force_ref[c] = total[c * SUB : (c + 1) * SUB]


def embedding(order, packets, pick, dest, block):
    extent, lines = len(packets), order // LANES
    return pl.pallas_call(
        functools.partial(records_kernel, extent, lines),
        out_shape=(
            jax.ShapeDtypeStruct((extent * lines, LANES), jnp.float32),
            jax.ShapeDtypeStruct((3, SUB, LANES), jnp.float32),
        ),
        in_specs=[pl.BlockSpec(memory_space=VMEM)] * (extent + 3),
        out_specs=(pl.BlockSpec(memory_space=VMEM),) * 2,
        cost_estimate=pl.CostEstimate(flops=10**7, bytes_accessed=5 * 10**6, transcendentals=0),
        compiler_params=pltpu.CompilerParams(vmem_limit_bytes=GRANT),
        name="embedding",
    )(*packets, pick, dest, block)


def field_kernel(parts_ref, rows_ref, columns_ref):
    total = parts_ref[0]
    for k in range(1, parts_ref.shape[0]):
        total = total + parts_ref[k]
    rows_ref[...] = total
    for n in range(total.shape[0]):
        columns_ref[n * LANES : (n + 1) * LANES, :] = jnp.broadcast_to(
            total[n : n + 1], (LANES, LANES)
        ).T


def whole_field(parts):
    lines = parts.shape[1]
    return pl.pallas_call(
        field_kernel,
        out_shape=(
            jax.ShapeDtypeStruct((lines, LANES), jnp.float32),
            jax.ShapeDtypeStruct((lines * LANES, LANES), jnp.float32),
        ),
        in_specs=[pl.BlockSpec(memory_space=VMEM)],
        out_specs=(pl.BlockSpec(memory_space=VMEM),) * 2,
        cost_estimate=pl.CostEstimate(flops=10**6, bytes_accessed=3 * 10**6, transcendentals=0),
        compiler_params=pltpu.CompilerParams(vmem_limit_bytes=GRANT),
        name="field",
    )(parts)


def modulo(value, count):
    return jnp.where(value < 0, value + count, value)


def keep_pattern(keep_ref, value):
    return jnp.where(keep_ref[...].astype(jnp.float32) > 0.5, value, 0.0)


def part_outputs(layers, value, hold_ref, mine_ref, send_ref):
    width = mine_ref.shape[0]
    layer = lax.axis_index("grp")
    hold_ref[...] = value
    mine_ref[...] = hold_ref[pl.ds(pl.multiple_of(layer * width, width), width), :]
    if layers == 2:
        send_ref[...] = hold_ref[
            pl.ds(pl.multiple_of((1 - layer) * width, width), width), :
        ].astype(send_ref.dtype)
    else:
        send_ref[...] = value.astype(send_ref.dtype)


def product_kernel(places, keep_ref, *refs):
    extent = len(refs) - 4 - len(places)
    left_refs, right_refs = refs[: len(places)], refs[len(places) : len(places) + extent]
    mine_ref, send_ref, table_ref, hold_ref = refs[len(places) + extent :]
    row, column = lax.axis_index("qr"), lax.axis_index("qc")
    for left_ref, place in zip(left_refs, places):
        table_ref[place(column)] = left_ref[...]
    total = jnp.zeros(hold_ref.shape, jnp.float32)
    for k in range(extent):
        total = total + jnp.dot(
            table_ref[modulo(row - k, extent)],
            right_refs[k][...],
            preferred_element_type=jnp.float32,
        )
    part_outputs(
        hold_ref.shape[0] // mine_ref.shape[0],
        keep_pattern(keep_ref, total),
        hold_ref,
        mine_ref,
        send_ref,
    )


def part_shapes(order, width):
    rows = width if order == 2 * width else order
    return (
        jax.ShapeDtypeStruct((width, order), jnp.float32),
        jax.ShapeDtypeStruct((rows, order), jnp.bfloat16),
    )


def product_part(keep, lefts, places, rights):
    order, width = lefts[0].shape
    inputs = len(lefts) + len(rights)
    return pl.pallas_call(
        functools.partial(product_kernel, places),
        out_shape=part_shapes(order, width)
        + (jax.ShapeDtypeStruct((len(lefts), order, width), jnp.bfloat16),),
        in_specs=[pl.BlockSpec(memory_space=VMEM)] * (inputs + 1),
        out_specs=(pl.BlockSpec(memory_space=VMEM),) * 3,
        scratch_shapes=[pltpu.VMEM((order, order), jnp.float32)],
        cost_estimate=pl.CostEstimate(
            flops=2 * order * order * width * len(rights),
            bytes_accessed=3 * 10**6,
            transcendentals=0,
        ),
        compiler_params=pltpu.CompilerParams(vmem_limit_bytes=GRANT),
        name="product",
    )(keep, *lefts, *rights)


def cube_kernel(keep_ref, table_ref, rows_ref, columns_ref, *refs):
    extent = (len(refs) - 3) // 2
    product_refs, right_refs = refs[:extent], refs[extent : 2 * extent]
    mine_ref, send_ref, hold_ref = refs[2 * extent :]
    width, order = mine_ref.shape
    lines = order // LANES
    row, column, layer = (lax.axis_index(axis) for axis in ALL)
    first = layer * width
    iota = functools.partial(lax.broadcasted_iota, jnp.int32)
    total = jnp.zeros((order, order), jnp.float32)
    for k in range(extent):
        tile = modulo(row - k, extent)
        down = columns_ref[pl.ds(pl.multiple_of(tile * order + first, width), width), :]
        pieces = []
        for n in range(lines):
            spot = slice(n * LANES, (n + 1) * LANES)
            across = rows_ref[pl.ds(column * lines + n, 1), :]
            matrix = right_refs[k][:, spot].astype(jnp.float32)
            on_diagonal = iota((width, LANES), 0) + first == iota((width, LANES), 1) + n * LANES
            corner = jnp.where(on_diagonal & (tile == column), down * down, 0.0)
            piece = product_refs[k][:, spot].astype(jnp.float32) + matrix * (down + across) + corner
            pieces.append(piece.astype(jnp.bfloat16))
        square = jnp.concatenate(pieces, axis=1)
        operand = table_ref[tile]
        if k == 0:
            own = columns_ref[pl.ds(pl.multiple_of(row * order, order), order), :]
            parts = []
            for start in range(0, width, LANES):
                size = min(LANES, width - start)
                shape = (order, size)
                on_diagonal = iota(shape, 0) == iota(shape, 1) + (first + start)
                parts.append(jnp.where(on_diagonal, own[:, :size], 0.0))
            added = parts[0] if len(parts) == 1 else jnp.concatenate(parts, axis=1)
            operand = (operand.astype(jnp.float32) + added).astype(jnp.bfloat16)
        total = total + jnp.dot(operand, square, preferred_element_type=jnp.float32)
    part_outputs(
        order // width, keep_pattern(keep_ref, total), hold_ref, mine_ref, send_ref
    )


def cube_part(keep, table, rows, columns, products, rights):
    _, order, width = table.shape
    inputs = 3 + len(products) + len(rights)
    return pl.pallas_call(
        cube_kernel,
        out_shape=part_shapes(order, width),
        in_specs=[pl.BlockSpec(memory_space=VMEM)] * (inputs + 1),
        out_specs=(pl.BlockSpec(memory_space=VMEM),) * 2,
        scratch_shapes=[pltpu.VMEM((order, order), jnp.float32)],
        cost_estimate=pl.CostEstimate(
            flops=2 * order * order * width * len(rights),
            bytes_accessed=3 * 10**6,
            transcendentals=0,
        ),
        compiler_params=pltpu.CompilerParams(vmem_limit_bytes=GRANT),
        name="cube",
    )(keep, table, rows, columns, *products, *rights)


def final_kernel(mine_ref, got_ref, right_ref, columns_ref, out_ref):
    width, order = mine_ref.shape
    row, column, layer = (lax.axis_index(axis) for axis in ALL)
    first = layer * width
    down = columns_ref[pl.ds(pl.multiple_of(row * order + first, width), width), :]
    iota = functools.partial(lax.broadcasted_iota, jnp.int32)
    for n in range(order // LANES):
        spot = slice(n * LANES, (n + 1) * LANES)
        on_diagonal = iota((width, LANES), 0) + first == iota((width, LANES), 1) + n * LANES
        added = jnp.where(on_diagonal & (row == column), down, 0.0)
        shifted = (right_ref[:, spot].astype(jnp.float32) + added).astype(jnp.bfloat16)
        cube = mine_ref[:, spot] + got_ref[:, spot].astype(jnp.float32)
        out_ref[:, spot] = (0.5 * (3.0 * shifted.astype(jnp.float32) - cube)).astype(jnp.bfloat16)


def final_step(mine, got, right, columns):
    return pl.pallas_call(
        final_kernel,
        out_shape=jax.ShapeDtypeStruct(mine.shape, jnp.bfloat16),
        in_specs=[pl.BlockSpec(memory_space=VMEM)] * 4,
        out_specs=pl.BlockSpec(memory_space=VMEM),
        cost_estimate=pl.CostEstimate(flops=10**6, bytes_accessed=10**6, transcendentals=0),
        compiler_params=pltpu.CompilerParams(vmem_limit_bytes=GRANT),
        name="final",
    )(mine, got, right, columns)


KEY_BITS = 8
GROUP_BITS = 3
BATCH = 8
CHUNK = 24


def packing_kernel(inner, *refs):
    *near_refs, packed_ref, scale_ref = refs
    picks = [(near_ref, i) for i in range(inner) for near_ref in near_refs]
    domains = len(picks)

    def entry(d, c):
        near_ref, i = picks[d]
        return near_ref[i, c]

    low = [entry(0, c) for c in range(4)]
    high = list(low)
    for d in range(1, domains):
        for c in range(4):
            value = entry(d, c)
            low[c] = jnp.minimum(low[c], value)
            high[c] = jnp.maximum(high[c], value)
    steps = 65535.0
    base, back = [], []
    for c in range(4):
        least = jnp.min(low[c], axis=(0, 1), keepdims=True)
        width = jnp.maximum(jnp.max(high[c], axis=(0, 1), keepdims=True) - least, 1e-30)
        base.append(jnp.broadcast_to(least, (SUB, LANES)))
        back.append(jnp.broadcast_to(steps / width, (SUB, LANES)))
        scale_ref[c] = base[c]
        scale_ref[4 + c] = jnp.broadcast_to(width * (1.0 / steps), (SUB, LANES))
    for d in range(domains):
        code = [
            jnp.clip((entry(d, c) - base[c]) * back[c] + 0.5, 0.0, steps).astype(jnp.int32)
            for c in range(4)
        ]
        start = (SUB - 1) * domains + d * SUB
        packed_ref[0, start : start + SUB, :] = code[0] | (code[1] << 16)
        packed_ref[1, start : start + SUB, :] = code[2] | (code[3] << 16)
    front, size = (SUB - 1) * domains, domains * SUB
    for w in range(2):
        packed_ref[w, :front, :] = jnp.zeros((front, LANES), jnp.int32)
        packed_ref[w, front + size :, :] = jnp.zeros((front + CHUNK, LANES), jnp.int32)


def packing(near):
    domains = len(near) * near[0].shape[0]
    rows = domains * SUB + 2 * (SUB - 1) * domains + CHUNK
    return pl.pallas_call(
        functools.partial(packing_kernel, near[0].shape[0]),
        out_shape=(
            jax.ShapeDtypeStruct((2, rows, LANES), jnp.int32),
            jax.ShapeDtypeStruct((8, SUB, LANES), jnp.float32),
        ),
        in_specs=[pl.BlockSpec(memory_space=VMEM)] * len(near),
        out_specs=(pl.BlockSpec(memory_space=VMEM),) * 2,
        cost_estimate=pl.CostEstimate(flops=10**7, bytes_accessed=5 * 10**6, transcendentals=0),
        compiler_params=pltpu.CompilerParams(vmem_limit_bytes=GRANT),
        name="packing",
    )(*near)


def compact(place, count):
    if count >= 3:
        return place
    if count == 2:
        return jnp.where(place == 1, 0, 1)
    return jnp.zeros_like(place)


def places_of(slot):
    p = (slot * 57) >> 9
    rest = slot - 9 * p
    q = (rest * 11) >> 5
    return p, q, rest - 3 * q


def network(count):
    pairs = []
    p = 1
    while p < count:
        k = p
        while k >= 1:
            for j in range(k % p, count - k, 2 * k):
                for i in range(min(k, count - j - k)):
                    if (i + j) // (2 * p) == (i + j + k) // (2 * p):
                        pairs.append((i + j, i + j + k))
            k //= 2
        p *= 2
    return pairs


def sorting_kernel(
    counts,
    lists_hbm,
    pattern_hbm,
    pick_hbm,
    dest_hbm,
    block_hbm,
    keys_ref,
    range_ref,
    keep_ref,
    pick_ref,
    dest_ref,
    block_ref,
    spread_ref,
    lists_ref,
    pattern_ref,
    sems,
):
    moves = [
        (lists_hbm, lists_ref),
        (pattern_hbm, pattern_ref),
        (pick_hbm, pick_ref),
        (dest_hbm, dest_ref),
        (block_hbm, block_ref),
    ]
    copies = [
        pltpu.make_async_copy(source, target, sems.at[i]) for i, (source, target) in enumerate(moves)
    ]
    for copy in copies:
        copy.start()
    for copy in copies:
        copy.wait()
    order, blocks = keep_ref.shape[0], pattern_ref.shape[0]
    member_of = (
        lax.broadcasted_iota(jnp.int32, (order, blocks), 0) // BLOCK
        == lax.broadcasted_iota(jnp.int32, (order, blocks), 1)
    ).astype(jnp.bfloat16)
    marks = (pattern_ref[...] == 1).astype(jnp.float32).astype(jnp.bfloat16)
    wide = jnp.dot(member_of, marks, preferred_element_type=jnp.float32).astype(jnp.bfloat16)
    keep_ref[...] = lax.dot_general(
        wide, member_of, (((1,), (1,)), ((), ())), preferred_element_type=jnp.float32
    ).astype(jnp.bfloat16)

    entries = lists_ref.shape[1]
    distinct = [min(3, count) for count in counts]
    domains = distinct[0] * distinct[1] * distinct[2]
    keys = []
    for b in range(entries // SUB):
        for a in range(SUB):
            slot = lists_ref[0, b * SUB : (b + 1) * SUB, a * LANES : (a + 1) * LANES]
            member = lists_ref[1, b * SUB : (b + 1) * SUB, a * LANES : (a + 1) * LANES]
            p, q, r = places_of(slot)
            domain = (
                compact(p, counts[0]) * distinct[1] + compact(q, counts[1])
            ) * distinct[2] + compact(r, counts[2])
            key = ((domain * (SUB * LANES) + member) << KEY_BITS) + (slot << GROUP_BITS) + a
            keys.append(key.astype(jnp.float32))
    size = len(keys)
    sublane = lax.broadcasted_iota(jnp.int32, (SUB, LANES), 0)

    def turned(values, bit):
        sign = jnp.where((sublane >> bit) & 1 == 1, -1.0, 1.0)
        return [value * sign for value in values]

    def by_sublane(values):
        for v in range(size):
            spread_ref[pl.ds(v, SUB, stride=size), :] = values[v]
        return [spread_ref[n * SUB : (n + 1) * SUB, :] for n in range(size)]

    def by_register(values):
        for n in range(size):
            spread_ref[n * SUB : (n + 1) * SUB, :] = values[n]
        return [spread_ref[pl.ds(v, SUB, stride=size), :] for v in range(size)]

    def exchange(values, i, j, up=True):
        low, high = jnp.minimum(values[i], values[j]), jnp.maximum(values[i], values[j])
        values[i], values[j] = (low, high) if up else (high, low)

    keys = turned(keys, 0)
    for i, j in network(size):
        exchange(keys, i, j)
    keys = turned(keys, 0)
    run = size // SUB
    for level in range(1, 4):
        keys = by_sublane(keys)
        for step in reversed(range(level)):
            for s in range(SUB):
                if not s >> step & 1:
                    for n in range(run):
                        exchange(
                            keys,
                            s * run + n,
                            (s | 1 << step) * run + n,
                            level == 3 or not s >> level & 1,
                        )
        keys = by_register(keys)
        if level < 3:
            keys = turned(keys, level)
        stride = size // 2
        while stride:
            for v in range(size):
                if not v & stride:
                    exchange(keys, v, v | stride)
            stride //= 2
        if level < 3:
            keys = turned(keys, level)

    whole = [key.astype(jnp.int32) for key in keys]
    for v in range(size):
        keys_ref[v] = whole[v]
    base = sublane * domains
    lows = [(whole[v] >> (KEY_BITS + 7)) - base for v in range(0, size, BATCH)]
    highs = [(whole[v + BATCH - 1] >> (KEY_BITS + 7)) - base for v in range(0, size, BATCH)]
    least = jnp.concatenate(
        [jnp.min(low.astype(jnp.float32), axis=0, keepdims=True) for low in lows], axis=0
    )
    most = jnp.concatenate(
        [jnp.max(high.astype(jnp.float32), axis=0, keepdims=True) for high in highs], axis=0
    )
    least = jnp.min(least, axis=1, keepdims=True)
    most = jnp.max(most, axis=1, keepdims=True)
    both = jnp.concatenate([least, most], axis=0).astype(jnp.int32)
    range_ref[...] = jnp.broadcast_to(both, range_ref.shape)


def sorting(counts, order, lists, pattern, pick, dest, block):
    entries = lists.shape[1]
    records = jax.ShapeDtypeStruct(pick.shape, jnp.int32)
    return pl.pallas_call(
        functools.partial(sorting_kernel, counts),
        out_shape=(
            jax.ShapeDtypeStruct((entries, SUB, LANES), jnp.int32),
            jax.ShapeDtypeStruct((2 * entries // BATCH, LANES), jnp.int32),
            jax.ShapeDtypeStruct((order, order), jnp.bfloat16),
            records,
            records,
            records,
        ),
        in_specs=[pl.BlockSpec(memory_space=pltpu.MemorySpace.HBM)] * 5,
        out_specs=(pl.BlockSpec(memory_space=VMEM),) * 6,
        scratch_shapes=[
            pltpu.VMEM((entries * SUB, LANES), jnp.float32),
            pltpu.VMEM(lists.shape, jnp.int32),
            pltpu.VMEM(pattern.shape, jnp.int32),
            pltpu.SemaphoreType.DMA((5,)),
        ],
        cost_estimate=pl.CostEstimate(flops=10**7, bytes_accessed=5 * 10**6, transcendentals=0),
        compiler_params=pltpu.CompilerParams(vmem_limit_bytes=GRANT),
        name="sorting",
    )(*in_place(lists, pattern, pick, dest, block))


def pair_kernel(
    domains, first, last, range_ref, keys_ref, own_ref, packed_ref, scale_ref, start_ref, force_ref
):
    blocks = keys_ref.shape[0] // BATCH
    front = (SUB - 1) * domains
    base = lax.broadcasted_iota(jnp.int32, (SUB, LANES), 0) * domains

    def step(j, sums):
        keys = [keys_ref[j * BATCH + i] for i in range(BATCH)]
        rows = [(key >> (KEY_BITS + 7)) - base for key in keys]
        lanes = [(key >> KEY_BITS) & (LANES - 1) for key in keys]
        low = range_ref[j, 0]
        rounds = (range_ref[blocks + j, 0] - low) // CHUNK + 1

        def scan(i, words):
            words = list(words)
            start = low + i * CHUNK
            for m in range(BATCH):
                for u in range(CHUNK):
                    here = rows[m] == start + u
                    for w in range(2):
                        lines = packed_ref[w, pl.ds(front + start + u, SUB, stride=domains), :]
                        k = 2 * m + w
                        words[k] = jnp.where(here, pick_lanes(lines, lanes[m]), words[k])
            return tuple(words)

        zero = jnp.zeros((SUB, LANES), jnp.int32)
        words = lax.fori_loop(0, rounds, scan, (zero,) * (2 * BATCH))
        sums = list(sums)
        for m in range(BATCH):
            group = keys[m] & ((1 << GROUP_BITS) - 1)
            places = places_of((keys[m] >> GROUP_BITS) & 31)
            mine = [group == g for g in range(SUB)]
            one, two = words[2 * m], words[2 * m + 1]
            code = [one & 0xFFFF, (one >> 16) & 0xFFFF, two & 0xFFFF, (two >> 16) & 0xFFFF]
            value = [code[c].astype(jnp.float32) * scale_ref[4 + c] + scale_ref[c] for c in range(4)]
            offset = []
            for c in range(3):
                place = own_ref[c, 0:1, :]
                for g in range(1, SUB):
                    place = jnp.where(mine[g], own_ref[c, g : g + 1, :], place)
                shift = (places[c] - 1).astype(jnp.float32) * domain_edge
                offset.append(place - (value[c] + shift))
            distance = (
                offset[0] * offset[0] + offset[1] * offset[1] + offset[2] * offset[2] + soften
            )
            inverse = lax.rsqrt(distance)
            strength = value[3] * (inverse * inverse * inverse)
            for c in range(3):
                push = offset[c] * strength
                for g in range(SUB):
                    k = c * SUB + g
                    sums[k] = sums[k] + jnp.where(mine[g], push, 0.0)
        return tuple(sums)

    zero = jnp.zeros((SUB, LANES), jnp.float32)
    sums = lax.fori_loop(first, last, step, (zero,) * (3 * SUB))
    for c in range(3):
        total = jnp.concatenate(
            [jnp.sum(sums[c * SUB + g], axis=0, keepdims=True) for g in range(SUB)], axis=0
        )
        force_ref[c] = start_ref[c] + coulomb * own_ref[3] * total


def pair_forces(domains, first, last, ranges, keys, own, packed, scale, start):
    return pl.pallas_call(
        functools.partial(pair_kernel, domains, first, last),
        out_shape=jax.ShapeDtypeStruct((3, SUB, LANES), jnp.float32),
        in_specs=[pl.BlockSpec(memory_space=SMEM)] + [pl.BlockSpec(memory_space=VMEM)] * 5,
        out_specs=pl.BlockSpec(memory_space=VMEM),
        cost_estimate=pl.CostEstimate(
            flops=10**7, bytes_accessed=(last - first) * BATCH * 10**5 * 3, transcendentals=0
        ),
        compiler_params=pltpu.CompilerParams(vmem_limit_bytes=GRANT),
        name="pairs",
    )(ranges, keys, own, packed, scale, start)


def neighbourhood(counts, along_rows):
    reach = [(-1, 0, 1) if n >= 3 else (0, 1) if n == 2 else (0,) for n in counts]
    mine = jnp.stack([along_rows[(-i) % counts[0]] for i in reach[0]])
    columns, layers = counts[1:]
    near = []
    for j in reach[1]:
        for k in reach[2]:
            if (j, k) == (0, 0):
                near.append(mine)
                continue
            pairs = [
                (((c + j) % columns) * layers + (g + k) % layers, c * layers + g)
                for c in range(columns)
                for g in range(layers)
            ]
            near.append(lax.ppermute(mine, ("qc", "grp"), pairs))
    return near


def crossed(value, axis):
    count = lax.axis_size(axis)
    if count & (count - 1):
        return rotated(value, axis), [lambda me, k=k: modulo(me - k, count) for k in range(count)]
    return (
        [value]
        + [lax.ppermute(value, axis, [(i, i ^ k) for i in range(count)]) for k in range(1, count)],
        [lambda me, k=k: me ^ k for k in range(count)],
    )


def per_device(
    kohn_sham, pattern, basis_centers, occupations, atoms, neighbours, emb_atom, emb_dest, emb_block
):
    counts = tuple(lax.axis_size(axis) for axis in ALL)
    layers = counts[2]
    order = kohn_sham.shape[0]
    width = order // layers
    record_count = emb_atom.shape[0]
    own = atoms.reshape(4, SUB, LANES)
    after = lax.optimization_barrier

    left_own, right_own, packet = prepare(width, kohn_sham, own, basis_centers, occupations)
    rights = rotated(right_own, "qr")
    packets = rotated(packet, "qr")
    lefts, places = crossed(left_own, "qc")
    keys, ranges, keep, *records = sorting(
        counts,
        order,
        neighbours[0, 0, 0],
        pattern,
        emb_atom.reshape(1, record_count),
        emb_dest.reshape(1, record_count),
        emb_block.reshape(1, record_count),
    )
    domains = min(3, counts[0]) * min(3, counts[1]) * min(3, counts[2])
    field, embed_force = embedding(order, packets, *records)
    near = neighbourhood(counts, [piece[:4] for piece in packets])

    def from_layers(send):
        if layers == 2:
            return lax.ppermute(send, "grp", [(0, 1), (1, 0)])
        got = lax.all_to_all(
            send.reshape(layers, width, order), "grp", split_axis=0, concat_axis=0, tiled=True
        )
        other = jnp.arange(layers)[:, None, None] != lax.axis_index("grp")
        return jnp.sum(jnp.where(other, got.astype(jnp.float32), 0.0), axis=0)

    blocks = keys.shape[0] // BATCH

    *arrived, keys = after((*rights[1:], keys))
    mine, send, table = product_part(keep, lefts, places, [right_own] + arrived)
    got = from_layers(send)
    field_all = everyone(field, ALL)
    rows, columns = whole_field(field_all)
    product_rows = (mine + got.astype(jnp.float32)).astype(jnp.bfloat16)
    products = rotated(product_rows, "qr")
    packed, scale = packing(near)
    product_rows, packed = after((product_rows, packed))
    force = pair_forces(domains, 0, blocks, ranges, keys, own, packed, scale, embed_force)
    *received, force = after((*products[1:], force))
    products = [products[0]] + received

    mine, send = cube_part(keep, table, rows, columns, products, rights)
    got = from_layers(send)
    sign_step = final_step(mine, got, right_own, columns)
    return (sign_step, force.reshape(3, 1, 1, 1, SUB * LANES))


def solution(mesh):
    in_specs = (
        P("qr", "qc"),
        P("qr", "qc"),
        P(None, "qr"),
        P("qr"),
        P(None, "qr", "qc", "grp", None),
        P("qr", "qc", "grp", None, None, None),
        P(("qr", "qc", "grp")),
        P(("qr", "qc", "grp"), None),
        P(("qr", "qc", "grp")),
    )
    out_specs = (P(("qr", "grp"), "qc"), P(None, "qr", "qc", "grp", None))

    return jax.shard_map(
        per_device, mesh=mesh, in_specs=in_specs, out_specs=out_specs, check_vma=False
    )
```

```python
import functools

import jax
import jax.numpy as jnp
from jax import lax
from jax.experimental import pallas as pl
from jax.experimental.pallas import tpu as pltpu
from jax.sharding import PartitionSpec as P


BLOCK = 64
SUB, LANES = 8, 128

coulomb = 138.935
hartree_nm = 0.0529177
soften = 0.01
domain_edge = 3.4

ALL = ("qr", "qc", "grp")
VMEM = pltpu.MemorySpace.VMEM
GRANT = 16 << 20
SMEM = pltpu.MemorySpace.SMEM

LANE_PICK = lax.GatherDimensionNumbers(
    offset_dims=(),
    collapsed_slice_dims=(1,),
    start_index_map=(1,),
    operand_batching_dims=(0,),
    start_indices_batching_dims=(0,),
)


def pick_lanes(row, lane):
    return lax.gather(
        row, lane[..., None], LANE_PICK, (1, 1), mode=lax.GatherScatterMode.PROMISE_IN_BOUNDS
    )


def everyone(value, axes):
    count = 1
    for axis in (axes,) if isinstance(axes, str) else axes:
        count *= lax.axis_size(axis)
    copies = jnp.broadcast_to(value[None], (count,) + value.shape)
    return lax.all_to_all(copies, axes, split_axis=0, concat_axis=0, tiled=True)


def rotated(value, axis):
    count = lax.axis_size(axis)
    return [value] + [
        lax.ppermute(value, axis, [(i, (i + k) % count) for i in range(count)])
        for k in range(1, count)
    ]


def in_place(*values):
    return [pltpu.with_memory_space_constraint(value, pltpu.MemorySpace.HBM) for value in values]


def thirds(value):
    high = value.astype(jnp.bfloat16)
    rest = value - high.astype(jnp.float32)
    middle = rest.astype(jnp.bfloat16)
    low = (rest - middle.astype(jnp.float32)).astype(jnp.bfloat16)
    return high, middle, low


def prepare_kernel(count, *refs):
    inputs, (left_ref, right_ref, packet_ref), kept, (matrix_buf, centers_buf, weights_buf, sems) = (
        refs[:count],
        refs[count : count + 3],
        refs[count + 3 : -4],
        refs[-4:],
    )
    order, width = left_ref.shape
    layer = lax.axis_index("grp")
    targets = [matrix_buf, packet_ref.at[0:4], centers_buf, weights_buf] + list(kept)
    copies = [
        pltpu.make_async_copy(source, target, sems.at[i])
        for i, (source, target) in enumerate(zip(inputs, targets))
    ]
    for copy in copies:
        copy.start()
    copies[2].wait()
    copies[3].wait()
    lines = order // LANES
    rows = [
        centers_buf[c : c + 1, n * LANES : (n + 1) * LANES] for c in range(3) for n in range(lines)
    ]
    rows = rows + [weights_buf[n * LANES : (n + 1) * LANES].reshape(1, LANES) for n in range(lines)]
    planes = packet_ref.shape[0] - 4
    rows = rows + [jnp.zeros((1, LANES), jnp.float32)] * (planes * SUB - len(rows))
    for n in range(planes):
        packet_ref[4 + n] = jnp.concatenate(rows[n * SUB : (n + 1) * SUB], axis=0)
    copies[0].wait()
    right_ref[...] = matrix_buf[pl.ds(pl.multiple_of(layer * width, width), width), :]
    for i in range(order // width):

        @pl.when(layer == i)
        def _():
            left_ref[...] = matrix_buf[:, i * width : (i + 1) * width]

    for copy in copies[1:2] + copies[4:]:
        copy.wait()


def prepare(width, matrix, atoms, centers, weights, *kept):
    order = matrix.shape[0]
    planes = -(-4 * (order // LANES) // SUB)
    inputs = (matrix, atoms, centers, weights) + kept
    return pl.pallas_call(
        functools.partial(prepare_kernel, len(inputs)),
        out_shape=(
            jax.ShapeDtypeStruct((order, width), matrix.dtype),
            jax.ShapeDtypeStruct((width, order), matrix.dtype),
            jax.ShapeDtypeStruct((4 + planes, SUB, LANES), jnp.float32),
        )
        + tuple(jax.ShapeDtypeStruct(value.shape, value.dtype) for value in kept),
        in_specs=[pl.BlockSpec(memory_space=pltpu.MemorySpace.HBM)] * len(inputs),
        out_specs=(pl.BlockSpec(memory_space=VMEM),) * (3 + len(kept)),
        scratch_shapes=[
            pltpu.VMEM(matrix.shape, matrix.dtype),
            pltpu.VMEM(centers.shape, centers.dtype),
            pltpu.VMEM(weights.shape, weights.dtype),
            pltpu.SemaphoreType.DMA((len(inputs),)),
        ],
        cost_estimate=pl.CostEstimate(flops=10**6, bytes_accessed=10**6, transcendentals=0),
        compiler_params=pltpu.CompilerParams(vmem_limit_bytes=GRANT),
        name="prepare",
    )(*in_place(*inputs))


def records_kernel(extent, lines, *refs):
    packet_refs = refs[:extent]
    pick_ref, dest_ref, block_ref, field_ref, force_ref = refs[extent:]
    count = pick_ref.shape[1]
    here = [lax.axis_index(axis) for axis in ALL]
    anchor = [place.astype(jnp.float32) * domain_edge for place in here]
    pick, dest, block = pick_ref[...], dest_ref[...], block_ref[...]
    lane, group = pick & (LANES - 1), pick >> 7
    behind = here[0] - dest
    behind = jnp.where(behind < 0, behind + extent, behind)
    iota = functools.partial(lax.broadcasted_iota, jnp.int32)
    one_lane = (iota((LANES, count), 0) == lane).astype(jnp.bfloat16)
    in_group = iota((SUB, count), 0) == group
    half = block >> 1
    odd = (block & 1) == 1
    one_line = (iota((extent * lines, count), 0) == behind * lines + half).astype(jnp.bfloat16)
    one_out = (iota((extent * lines, count), 0) == dest * lines + half).astype(jnp.bfloat16)

    def exact(product, value):
        high, middle, low = thirds(value)
        return product(high) + product(middle) + product(low)

    def dot(contract):
        return lambda other: lambda value: lax.dot_general(
            value, other, (contract, ((), ())), preferred_element_type=jnp.float32
        )

    own = packet_refs[0]
    atoms = jnp.concatenate([own[c] for c in range(4)], axis=0)
    spread = exact(dot(((1,), (0,)))(one_lane), atoms)
    taken = [
        jnp.sum(jnp.where(in_group, spread[c * SUB : (c + 1) * SUB], 0.0), axis=0, keepdims=True)
        for c in range(4)
    ]

    def line(k, n):
        return packet_refs[k][4 + n // SUB, n % SUB : n % SUB + 1, :]

    def chosen(c):
        table = jnp.concatenate(
            [line(k, c * lines + n) for k in range(extent) for n in range(lines)], axis=0
        )
        both = exact(dot(((0,), (0,)))(one_line), table)
        return jnp.where(odd, both[BLOCK:], both[:BLOCK])

    charge = taken[3]
    offset = [taken[c] + anchor[c] - chosen(c) for c in range(3)]
    weight = chosen(3)
    distance = offset[0] * offset[0] + offset[1] * offset[1] + offset[2] * offset[2] + soften
    inverse = lax.rsqrt(distance)
    terms = hartree_nm * charge * inverse
    terms = jnp.concatenate([jnp.where(odd, 0.0, terms), jnp.where(odd, terms, 0.0)], axis=0)
    high, middle, low = thirds(terms)
    field = sum(
        lax.dot_general(one_out, piece, (((1,), (1,)), ((), ())), preferred_element_type=jnp.float32)
        for piece in (high, middle, low)
    )
    field_ref[...] = field.astype(field_ref.dtype)
    strength = weight * (inverse * inverse * inverse)
    pushes = [
        coulomb * charge * jnp.sum(strength * offset[c], axis=0, keepdims=True) for c in range(3)
    ]
    pushes = jnp.concatenate([jnp.where(in_group, push, 0.0) for push in pushes], axis=0)
    total = exact(dot(((1,), (1,)))(one_lane), pushes)
    for c in range(3):
        force_ref[c] = total[c * SUB : (c + 1) * SUB]


def embedding(order, packets, pick, dest, block):
    extent, lines = len(packets), order // LANES
    return pl.pallas_call(
        functools.partial(records_kernel, extent, lines),
        out_shape=(
            jax.ShapeDtypeStruct((extent * lines, LANES), jnp.bfloat16),
            jax.ShapeDtypeStruct((3, SUB, LANES), jnp.float32),
        ),
        in_specs=[pl.BlockSpec(memory_space=VMEM)] * (extent + 3),
        out_specs=(pl.BlockSpec(memory_space=VMEM),) * 2,
        cost_estimate=pl.CostEstimate(flops=10**7, bytes_accessed=5 * 10**6, transcendentals=0),
        compiler_params=pltpu.CompilerParams(vmem_limit_bytes=GRANT),
        name="embedding",
    )(*packets, pick, dest, block)


def field_kernel(parts_ref, rows_ref, columns_ref):
    total = parts_ref[0].astype(jnp.float32)
    for k in range(1, parts_ref.shape[0]):
        total = total + parts_ref[k].astype(jnp.float32)
    rows_ref[...] = total
    for n in range(total.shape[0]):
        columns_ref[n * LANES : (n + 1) * LANES, :] = jnp.broadcast_to(
            total[n : n + 1], (LANES, LANES)
        ).T


def whole_field(parts):
    lines = parts.shape[1]
    return pl.pallas_call(
        field_kernel,
        out_shape=(
            jax.ShapeDtypeStruct((lines, LANES), jnp.float32),
            jax.ShapeDtypeStruct((lines * LANES, LANES), jnp.float32),
        ),
        in_specs=[pl.BlockSpec(memory_space=VMEM)],
        out_specs=(pl.BlockSpec(memory_space=VMEM),) * 2,
        cost_estimate=pl.CostEstimate(flops=10**6, bytes_accessed=3 * 10**6, transcendentals=0),
        compiler_params=pltpu.CompilerParams(vmem_limit_bytes=GRANT),
        name="field",
    )(parts)


def modulo(value, count):
    return jnp.where(value < 0, value + count, value)


def keep_pattern(pattern_ref, value):
    order, blocks = value.shape[0], pattern_ref.shape[0]
    member_of = (
        lax.broadcasted_iota(jnp.int32, (order, blocks), 0) // BLOCK
        == lax.broadcasted_iota(jnp.int32, (order, blocks), 1)
    ).astype(jnp.bfloat16)
    marks = (pattern_ref[...] == 1).astype(jnp.float32).astype(jnp.bfloat16)
    wide = jnp.dot(member_of, marks, preferred_element_type=jnp.float32).astype(jnp.bfloat16)
    keep = lax.dot_general(
        wide, member_of, (((1,), (1,)), ((), ())), preferred_element_type=jnp.float32
    )
    return jnp.where(keep > 0.5, value, 0.0)


def part_outputs(layers, value, hold_ref, mine_ref, send_ref):
    width = mine_ref.shape[0]
    layer = lax.axis_index("grp")
    hold_ref[...] = value
    mine_ref[...] = hold_ref[pl.ds(pl.multiple_of(layer * width, width), width), :]
    if layers == 2:
        send_ref[...] = hold_ref[
            pl.ds(pl.multiple_of((1 - layer) * width, width), width), :
        ].astype(send_ref.dtype)
    else:
        send_ref[...] = value.astype(send_ref.dtype)


def product_kernel(places, pattern_ref, *refs):
    extent = len(refs) - 4 - len(places)
    left_refs, right_refs = refs[: len(places)], refs[len(places) : len(places) + extent]
    mine_ref, send_ref, table_ref, hold_ref = refs[len(places) + extent :]
    row, column = lax.axis_index("qr"), lax.axis_index("qc")
    for left_ref, place in zip(left_refs, places):
        table_ref[place(column)] = left_ref[...]
    total = jnp.zeros(hold_ref.shape, jnp.float32)
    for k in range(extent):
        total = total + jnp.dot(
            table_ref[modulo(row - k, extent)],
            right_refs[k][...],
            preferred_element_type=jnp.float32,
        )
    part_outputs(
        hold_ref.shape[0] // mine_ref.shape[0],
        keep_pattern(pattern_ref, total),
        hold_ref,
        mine_ref,
        send_ref,
    )


def part_shapes(order, width):
    rows = width if order == 2 * width else order
    return (
        jax.ShapeDtypeStruct((width, order), jnp.float32),
        jax.ShapeDtypeStruct((rows, order), jnp.bfloat16),
    )


def product_part(pattern, lefts, places, rights):
    order, width = lefts[0].shape
    inputs = len(lefts) + len(rights)
    return pl.pallas_call(
        functools.partial(product_kernel, places),
        out_shape=part_shapes(order, width)
        + (jax.ShapeDtypeStruct((len(lefts), order, width), jnp.bfloat16),),
        in_specs=[pl.BlockSpec(memory_space=VMEM)] * (inputs + 1),
        out_specs=(pl.BlockSpec(memory_space=VMEM),) * 3,
        scratch_shapes=[pltpu.VMEM((order, order), jnp.float32)],
        cost_estimate=pl.CostEstimate(
            flops=2 * order * order * width * len(rights),
            bytes_accessed=3 * 10**6,
            transcendentals=0,
        ),
        compiler_params=pltpu.CompilerParams(vmem_limit_bytes=GRANT),
        name="product",
    )(pattern, *lefts, *rights)


def cube_kernel(pattern_ref, table_ref, rows_ref, columns_ref, *refs):
    extent = (len(refs) - 3) // 2
    product_refs, right_refs = refs[:extent], refs[extent : 2 * extent]
    mine_ref, send_ref, hold_ref = refs[2 * extent :]
    width, order = mine_ref.shape
    lines = order // LANES
    row, column, layer = (lax.axis_index(axis) for axis in ALL)
    first = layer * width
    iota = functools.partial(lax.broadcasted_iota, jnp.int32)
    total = jnp.zeros((order, order), jnp.float32)
    for k in range(extent):
        tile = modulo(row - k, extent)
        down = columns_ref[pl.ds(pl.multiple_of(tile * order + first, width), width), :]
        pieces = []
        for n in range(lines):
            spot = slice(n * LANES, (n + 1) * LANES)
            across = rows_ref[pl.ds(column * lines + n, 1), :]
            matrix = right_refs[k][:, spot].astype(jnp.float32)
            on_diagonal = iota((width, LANES), 0) + first == iota((width, LANES), 1) + n * LANES
            corner = jnp.where(on_diagonal & (tile == column), down * down, 0.0)
            piece = product_refs[k][:, spot].astype(jnp.float32) + matrix * (down + across) + corner
            pieces.append(piece.astype(jnp.bfloat16))
        square = jnp.concatenate(pieces, axis=1)
        operand = table_ref[tile]
        if k == 0:
            own = columns_ref[pl.ds(pl.multiple_of(row * order, order), order), :]
            parts = []
            for start in range(0, width, LANES):
                size = min(LANES, width - start)
                shape = (order, size)
                on_diagonal = iota(shape, 0) == iota(shape, 1) + (first + start)
                parts.append(jnp.where(on_diagonal, own[:, :size], 0.0))
            added = parts[0] if len(parts) == 1 else jnp.concatenate(parts, axis=1)
            operand = (operand.astype(jnp.float32) + added).astype(jnp.bfloat16)
        total = total + jnp.dot(operand, square, preferred_element_type=jnp.float32)
    part_outputs(
        order // width, keep_pattern(pattern_ref, total), hold_ref, mine_ref, send_ref
    )


def cube_part(pattern, table, rows, columns, products, rights):
    _, order, width = table.shape
    inputs = 3 + len(products) + len(rights)
    return pl.pallas_call(
        cube_kernel,
        out_shape=part_shapes(order, width),
        in_specs=[pl.BlockSpec(memory_space=VMEM)] * (inputs + 1),
        out_specs=(pl.BlockSpec(memory_space=VMEM),) * 2,
        scratch_shapes=[pltpu.VMEM((order, order), jnp.float32)],
        cost_estimate=pl.CostEstimate(
            flops=2 * order * order * width * len(rights),
            bytes_accessed=3 * 10**6,
            transcendentals=0,
        ),
        compiler_params=pltpu.CompilerParams(vmem_limit_bytes=GRANT),
        name="cube",
    )(pattern, table, rows, columns, *products, *rights)


def final_kernel(mine_ref, got_ref, right_ref, columns_ref, out_ref):
    width, order = mine_ref.shape
    row, column, layer = (lax.axis_index(axis) for axis in ALL)
    first = layer * width
    down = columns_ref[pl.ds(pl.multiple_of(row * order + first, width), width), :]
    iota = functools.partial(lax.broadcasted_iota, jnp.int32)
    for n in range(order // LANES):
        spot = slice(n * LANES, (n + 1) * LANES)
        on_diagonal = iota((width, LANES), 0) + first == iota((width, LANES), 1) + n * LANES
        added = jnp.where(on_diagonal & (row == column), down, 0.0)
        shifted = (right_ref[:, spot].astype(jnp.float32) + added).astype(jnp.bfloat16)
        cube = mine_ref[:, spot] + got_ref[:, spot].astype(jnp.float32)
        out_ref[:, spot] = (0.5 * (3.0 * shifted.astype(jnp.float32) - cube)).astype(jnp.bfloat16)


def final_step(mine, got, right, columns):
    return pl.pallas_call(
        final_kernel,
        out_shape=jax.ShapeDtypeStruct(mine.shape, jnp.bfloat16),
        in_specs=[pl.BlockSpec(memory_space=VMEM)] * 4,
        out_specs=pl.BlockSpec(memory_space=VMEM),
        cost_estimate=pl.CostEstimate(flops=10**6, bytes_accessed=10**6, transcendentals=0),
        compiler_params=pltpu.CompilerParams(vmem_limit_bytes=GRANT),
        name="final",
    )(mine, got, right, columns)


KEY_BITS = 8
GROUP_BITS = 3
BATCH = 8
CHUNK = 24


def packing_kernel(inner, *refs):
    *near_refs, packed_ref, scale_ref = refs
    picks = [(near_ref, i) for i in range(inner) for near_ref in near_refs]
    domains = len(picks)

    def entry(d, c):
        near_ref, i = picks[d]
        return near_ref[i, c]

    low = [entry(0, c) for c in range(4)]
    high = list(low)
    for d in range(1, domains):
        for c in range(4):
            value = entry(d, c)
            low[c] = jnp.minimum(low[c], value)
            high[c] = jnp.maximum(high[c], value)
    steps = 65535.0
    base, back = [], []
    for c in range(4):
        least = jnp.min(low[c], axis=(0, 1), keepdims=True)
        width = jnp.maximum(jnp.max(high[c], axis=(0, 1), keepdims=True) - least, 1e-30)
        base.append(jnp.broadcast_to(least, (SUB, LANES)))
        back.append(jnp.broadcast_to(steps / width, (SUB, LANES)))
        scale_ref[c] = base[c]
        scale_ref[4 + c] = jnp.broadcast_to(width * (1.0 / steps), (SUB, LANES))
    for d in range(domains):
        code = [
            jnp.clip((entry(d, c) - base[c]) * back[c] + 0.5, 0.0, steps).astype(jnp.int32)
            for c in range(4)
        ]
        start = (SUB - 1) * domains + d * SUB
        packed_ref[0, start : start + SUB, :] = code[0] | (code[1] << 16)
        packed_ref[1, start : start + SUB, :] = code[2] | (code[3] << 16)
    front, size = (SUB - 1) * domains, domains * SUB
    for w in range(2):
        packed_ref[w, :front, :] = jnp.zeros((front, LANES), jnp.int32)
        packed_ref[w, front + size :, :] = jnp.zeros((front + CHUNK, LANES), jnp.int32)


def packing(near):
    domains = len(near) * near[0].shape[0]
    rows = domains * SUB + 2 * (SUB - 1) * domains + CHUNK
    return pl.pallas_call(
        functools.partial(packing_kernel, near[0].shape[0]),
        out_shape=(
            jax.ShapeDtypeStruct((2, rows, LANES), jnp.int32),
            jax.ShapeDtypeStruct((8, SUB, LANES), jnp.float32),
        ),
        in_specs=[pl.BlockSpec(memory_space=VMEM)] * len(near),
        out_specs=(pl.BlockSpec(memory_space=VMEM),) * 2,
        cost_estimate=pl.CostEstimate(flops=10**7, bytes_accessed=5 * 10**6, transcendentals=0),
        compiler_params=pltpu.CompilerParams(vmem_limit_bytes=GRANT),
        name="packing",
    )(*near)


def compact(place, count):
    if count >= 3:
        return place
    if count == 2:
        return jnp.where(place == 1, 0, 1)
    return jnp.zeros_like(place)


def places_of(slot):
    p = (slot * 57) >> 9
    rest = slot - 9 * p
    q = (rest * 11) >> 5
    return p, q, rest - 3 * q


def network(count):
    pairs = []
    p = 1
    while p < count:
        k = p
        while k >= 1:
            for j in range(k % p, count - k, 2 * k):
                for i in range(min(k, count - j - k)):
                    if (i + j) // (2 * p) == (i + j + k) // (2 * p):
                        pairs.append((i + j, i + j + k))
            k //= 2
        p *= 2
    return pairs


def sorting_kernel(counts, lists_hbm, keys_ref, range_ref, spread_ref, lists_ref, sem):
    copy = pltpu.make_async_copy(lists_hbm, lists_ref, sem)
    copy.start()
    copy.wait()
    entries = lists_ref.shape[1]
    distinct = [min(3, count) for count in counts]
    domains = distinct[0] * distinct[1] * distinct[2]
    keys = []
    for b in range(entries // SUB):
        for a in range(SUB):
            slot = lists_ref[0, b * SUB : (b + 1) * SUB, a * LANES : (a + 1) * LANES]
            member = lists_ref[1, b * SUB : (b + 1) * SUB, a * LANES : (a + 1) * LANES]
            p, q, r = places_of(slot)
            domain = (
                compact(p, counts[0]) * distinct[1] + compact(q, counts[1])
            ) * distinct[2] + compact(r, counts[2])
            key = ((domain * (SUB * LANES) + member) << KEY_BITS) + (slot << GROUP_BITS) + a
            keys.append(key.astype(jnp.float32))
    size = len(keys)
    sublane = lax.broadcasted_iota(jnp.int32, (SUB, LANES), 0)

    def turned(values, bit):
        sign = jnp.where((sublane >> bit) & 1 == 1, -1.0, 1.0)
        return [value * sign for value in values]

    def by_sublane(values):
        for v in range(size):
            spread_ref[pl.ds(v, SUB, stride=size), :] = values[v]
        return [spread_ref[n * SUB : (n + 1) * SUB, :] for n in range(size)]

    def by_register(values):
        for n in range(size):
            spread_ref[n * SUB : (n + 1) * SUB, :] = values[n]
        return [spread_ref[pl.ds(v, SUB, stride=size), :] for v in range(size)]

    def exchange(values, i, j, up=True):
        low, high = jnp.minimum(values[i], values[j]), jnp.maximum(values[i], values[j])
        values[i], values[j] = (low, high) if up else (high, low)

    keys = turned(keys, 0)
    for i, j in network(size):
        exchange(keys, i, j)
    keys = turned(keys, 0)
    run = size // SUB
    for level in range(1, 4):
        keys = by_sublane(keys)
        for step in reversed(range(level)):
            for s in range(SUB):
                if not s >> step & 1:
                    for n in range(run):
                        exchange(
                            keys,
                            s * run + n,
                            (s | 1 << step) * run + n,
                            level == 3 or not s >> level & 1,
                        )
        keys = by_register(keys)
        if level < 3:
            keys = turned(keys, level)
        stride = size // 2
        while stride:
            for v in range(size):
                if not v & stride:
                    exchange(keys, v, v | stride)
            stride //= 2
        if level < 3:
            keys = turned(keys, level)

    whole = [key.astype(jnp.int32) for key in keys]
    for v in range(size):
        keys_ref[v] = whole[v]
    base = sublane * domains
    lows = [(whole[v] >> (KEY_BITS + 7)) - base for v in range(0, size, BATCH)]
    highs = [(whole[v + BATCH - 1] >> (KEY_BITS + 7)) - base for v in range(0, size, BATCH)]
    least = jnp.concatenate(
        [jnp.min(low.astype(jnp.float32), axis=0, keepdims=True) for low in lows], axis=0
    )
    most = jnp.concatenate(
        [jnp.max(high.astype(jnp.float32), axis=0, keepdims=True) for high in highs], axis=0
    )
    least = jnp.min(least, axis=1, keepdims=True)
    most = jnp.max(most, axis=1, keepdims=True)
    both = jnp.concatenate([least, most], axis=0).astype(jnp.int32)
    range_ref[...] = jnp.broadcast_to(both, range_ref.shape)


def sorting(counts, lists):
    entries = lists.shape[1]
    return pl.pallas_call(
        functools.partial(sorting_kernel, counts),
        out_shape=(
            jax.ShapeDtypeStruct((entries, SUB, LANES), jnp.int32),
            jax.ShapeDtypeStruct((2 * entries // BATCH, LANES), jnp.int32),
        ),
        in_specs=[pl.BlockSpec(memory_space=pltpu.MemorySpace.HBM)],
        out_specs=(pl.BlockSpec(memory_space=VMEM),) * 2,
        scratch_shapes=[
            pltpu.VMEM((entries * SUB, LANES), jnp.float32),
            pltpu.VMEM(lists.shape, jnp.int32),
            pltpu.SemaphoreType.DMA,
        ],
        cost_estimate=pl.CostEstimate(flops=10**7, bytes_accessed=5 * 10**6, transcendentals=0),
        compiler_params=pltpu.CompilerParams(vmem_limit_bytes=GRANT),
        name="sorting",
    )(*in_place(lists))


def pair_kernel(
    domains, first, last, range_ref, keys_ref, own_ref, packed_ref, scale_ref, start_ref, force_ref
):
    blocks = keys_ref.shape[0] // BATCH
    front = (SUB - 1) * domains
    base = lax.broadcasted_iota(jnp.int32, (SUB, LANES), 0) * domains

    def step(j, sums):
        keys = [keys_ref[j * BATCH + i] for i in range(BATCH)]
        rows = [(key >> (KEY_BITS + 7)) - base for key in keys]
        lanes = [(key >> KEY_BITS) & (LANES - 1) for key in keys]
        low = range_ref[j, 0]
        rounds = (range_ref[blocks + j, 0] - low) // CHUNK + 1

        def scan(i, words):
            words = list(words)
            start = low + i * CHUNK
            for m in range(BATCH):
                for u in range(CHUNK):
                    here = rows[m] == start + u
                    for w in range(2):
                        lines = packed_ref[w, pl.ds(front + start + u, SUB, stride=domains), :]
                        k = 2 * m + w
                        words[k] = jnp.where(here, pick_lanes(lines, lanes[m]), words[k])
            return tuple(words)

        zero = jnp.zeros((SUB, LANES), jnp.int32)
        words = lax.fori_loop(0, rounds, scan, (zero,) * (2 * BATCH))
        sums = list(sums)
        for m in range(BATCH):
            group = keys[m] & ((1 << GROUP_BITS) - 1)
            places = places_of((keys[m] >> GROUP_BITS) & 31)
            mine = [group == g for g in range(SUB)]
            one, two = words[2 * m], words[2 * m + 1]
            code = [one & 0xFFFF, (one >> 16) & 0xFFFF, two & 0xFFFF, (two >> 16) & 0xFFFF]
            value = [code[c].astype(jnp.float32) * scale_ref[4 + c] + scale_ref[c] for c in range(4)]
            offset = []
            for c in range(3):
                place = own_ref[c, 0:1, :]
                for g in range(1, SUB):
                    place = jnp.where(mine[g], own_ref[c, g : g + 1, :], place)
                shift = (places[c] - 1).astype(jnp.float32) * domain_edge
                offset.append(place - (value[c] + shift))
            distance = (
                offset[0] * offset[0] + offset[1] * offset[1] + offset[2] * offset[2] + soften
            )
            inverse = lax.rsqrt(distance)
            strength = value[3] * (inverse * inverse * inverse)
            for c in range(3):
                push = offset[c] * strength
                for g in range(SUB):
                    k = c * SUB + g
                    sums[k] = sums[k] + jnp.where(mine[g], push, 0.0)
        return tuple(sums)

    zero = jnp.zeros((SUB, LANES), jnp.float32)
    sums = lax.fori_loop(first, last, step, (zero,) * (3 * SUB))
    for c in range(3):
        total = jnp.concatenate(
            [jnp.sum(sums[c * SUB + g], axis=0, keepdims=True) for g in range(SUB)], axis=0
        )
        force_ref[c] = start_ref[c] + coulomb * own_ref[3] * total


def pair_forces(first, last, ranges, keys, own, packed, scale, start):
    return pl.pallas_call(
        functools.partial(pair_kernel, (packed.shape[1] - CHUNK) // (3 * SUB - 2), first, last),
        out_shape=jax.ShapeDtypeStruct((3, SUB, LANES), jnp.float32),
        in_specs=[pl.BlockSpec(memory_space=SMEM)] + [pl.BlockSpec(memory_space=VMEM)] * 5,
        out_specs=pl.BlockSpec(memory_space=VMEM),
        cost_estimate=pl.CostEstimate(
            flops=10**7, bytes_accessed=(last - first) * BATCH * 10**5 * 3, transcendentals=0
        ),
        compiler_params=pltpu.CompilerParams(vmem_limit_bytes=GRANT),
        name="pairs",
    )(ranges, keys, own, packed, scale, start)


def neighbourhood(counts, along_rows):
    reach = [(-1, 0, 1) if n >= 3 else (0, 1) if n == 2 else (0,) for n in counts]
    mine = jnp.stack([along_rows[(-i) % counts[0]] for i in reach[0]])
    columns, layers = counts[1:]
    near = []
    for j in reach[1]:
        for k in reach[2]:
            if (j, k) == (0, 0):
                near.append(mine)
                continue
            pairs = [
                (((c + j) % columns) * layers + (g + k) % layers, c * layers + g)
                for c in range(columns)
                for g in range(layers)
            ]
            near.append(lax.ppermute(mine, ("qc", "grp"), pairs))
    return near


def crossed(value, axis):
    count = lax.axis_size(axis)
    if count & (count - 1):
        return rotated(value, axis), [lambda me, k=k: modulo(me - k, count) for k in range(count)]
    return (
        [value]
        + [lax.ppermute(value, axis, [(i, i ^ k) for i in range(count)]) for k in range(1, count)],
        [lambda me, k=k: me ^ k for k in range(count)],
    )


def per_device(
    kohn_sham, pattern, basis_centers, occupations, atoms, neighbours, emb_atom, emb_dest, emb_block
):
    counts = tuple(lax.axis_size(axis) for axis in ALL)
    layers = counts[2]
    order = kohn_sham.shape[0]
    width = order // layers
    record_count = emb_atom.shape[0]
    own = atoms.reshape(4, SUB, LANES)
    after = lax.optimization_barrier

    left_own, right_own, packet, pattern, *records = prepare(
        width,
        kohn_sham,
        own,
        basis_centers,
        occupations,
        pattern,
        emb_atom.reshape(1, record_count),
        emb_dest.reshape(1, record_count),
        emb_block.reshape(1, record_count),
    )
    packets = rotated(packet, "qr")
    rights = rotated(right_own, "qr")
    lefts, places = crossed(left_own, "qc")
    field, embed_force = embedding(order, packets, *records)
    field_all = everyone(field, ALL)
    near = neighbourhood(counts, [piece[:4] for piece in packets])

    def from_layers(send):
        if layers == 2:
            return lax.ppermute(send, "grp", [(0, 1), (1, 0)])
        got = lax.all_to_all(
            send.reshape(layers, width, order), "grp", split_axis=0, concat_axis=0, tiled=True
        )
        other = jnp.arange(layers)[:, None, None] != lax.axis_index("grp")
        return jnp.sum(jnp.where(other, got.astype(jnp.float32), 0.0), axis=0)

    mine, send, table = product_part(pattern, lefts, places, rights)
    got = from_layers(send)
    lists, mine = after((neighbours[0, 0, 0], mine))
    keys, ranges = sorting(counts, lists)
    blocks = keys.shape[0] // BATCH
    got, keys = after((got, keys))
    rows, columns = whole_field(field_all)
    product_rows = (mine + got.astype(jnp.float32)).astype(jnp.bfloat16)
    products = rotated(product_rows, "qr")
    packed, scale = packing(near)
    product_rows, packed = after((product_rows, packed))
    force = pair_forces(0, blocks // 2, ranges, keys, own, packed, scale, embed_force)
    *received, force = after((*products[1:], force))
    products = [products[0]] + received

    mine, send = cube_part(pattern, table, rows, columns, products, rights)
    got = from_layers(send)
    mine, force = after((mine, force))
    force = pair_forces(blocks // 2, blocks, ranges, keys, own, packed, scale, force)
    got, force = after((got, force))
    sign_step = final_step(mine, got, right_own, columns)
    return (sign_step, force.reshape(3, 1, 1, 1, SUB * LANES))


def solution(mesh):
    in_specs = (
        P("qr", "qc"),
        P("qr", "qc"),
        P(None, "qr"),
        P("qr"),
        P(None, "qr", "qc", "grp", None),
        P("qr", "qc", "grp", None, None, None),
        P(("qr", "qc", "grp")),
        P(("qr", "qc", "grp"), None),
        P(("qr", "qc", "grp")),
    )
    out_specs = (P(("qr", "grp"), "qc"), P(None, "qr", "qc", "grp", None))

    return jax.shard_map(
        per_device, mesh=mesh, in_specs=in_specs, out_specs=out_specs, check_vma=False
    )
```

```python
import functools

import jax
import jax.numpy as jnp
from jax import lax
from jax.experimental import pallas as pl
from jax.experimental.pallas import tpu as pltpu
from jax.sharding import PartitionSpec as P


BLOCK = 64
SUB, LANES = 8, 128

coulomb = 138.935
hartree_nm = 0.0529177
soften = 0.01
domain_edge = 3.4

ALL = ("qr", "qc", "grp")
VMEM = pltpu.MemorySpace.VMEM
GRANT = 16 << 20
SMEM = pltpu.MemorySpace.SMEM

LANE_PICK = lax.GatherDimensionNumbers(
    offset_dims=(),
    collapsed_slice_dims=(1,),
    start_index_map=(1,),
    operand_batching_dims=(0,),
    start_indices_batching_dims=(0,),
)


def pick_lanes(row, lane):
    return lax.gather(
        row, lane[..., None], LANE_PICK, (1, 1), mode=lax.GatherScatterMode.PROMISE_IN_BOUNDS
    )


def rotated(value, axis):
    count = lax.axis_size(axis)
    of = value if callable(value) else lambda k: value
    return [of(0)] + [
        lax.ppermute(of(k), axis, [(i, (i + k) % count) for i in range(count)])
        for k in range(1, count)
    ]


def in_place(*values):
    return [pltpu.with_memory_space_constraint(value, pltpu.MemorySpace.HBM) for value in values]


def thirds(value):
    high = value.astype(jnp.bfloat16)
    rest = value - high.astype(jnp.float32)
    middle = rest.astype(jnp.bfloat16)
    low = (rest - middle.astype(jnp.float32)).astype(jnp.bfloat16)
    return high, middle, low


def prepare_kernel(count, *refs):
    inputs, (left_ref, right_ref, packet_ref, basis_ref), kept, buffers = (
        refs[:count],
        refs[count : count + 4],
        refs[count + 4 : -4],
        refs[-4:],
    )
    matrix_buf, centers_buf, weights_buf, sems = buffers
    order, width = left_ref.shape
    layer = lax.axis_index("grp")
    targets = [matrix_buf, packet_ref.at[0:4], centers_buf, weights_buf] + list(kept)
    copies = [
        pltpu.make_async_copy(source, target, sems.at[i])
        for i, (source, target) in enumerate(zip(inputs, targets))
    ]
    for copy in copies:
        copy.start()
    copies[2].wait()
    copies[3].wait()
    lines = order // LANES
    rows = [
        centers_buf[c : c + 1, n * LANES : (n + 1) * LANES] for c in range(3) for n in range(lines)
    ]
    rows = rows + [weights_buf[n * LANES : (n + 1) * LANES].reshape(1, LANES) for n in range(lines)]
    planes = packet_ref.shape[0] - 4
    rows = rows + [jnp.zeros((1, LANES), jnp.float32)] * (planes * SUB - len(rows))
    for n in range(planes):
        basis = jnp.concatenate(rows[n * SUB : (n + 1) * SUB], axis=0)
        packet_ref[4 + n] = basis
        basis_ref[n] = basis
    copies[0].wait()
    right_ref[...] = matrix_buf[pl.ds(pl.multiple_of(layer * width, width), width), :]
    for i in range(order // width):

        @pl.when(layer == i)
        def _():
            left_ref[...] = matrix_buf[:, i * width : (i + 1) * width]

    for copy in copies[1:2] + copies[4:]:
        copy.wait()


def prepare(width, matrix, atoms, centers, weights, *kept):
    order = matrix.shape[0]
    planes = -(-4 * (order // LANES) // SUB)
    inputs = (matrix, atoms, centers, weights) + kept
    return pl.pallas_call(
        functools.partial(prepare_kernel, len(inputs)),
        out_shape=(
            jax.ShapeDtypeStruct((order, width), matrix.dtype),
            jax.ShapeDtypeStruct((width, order), matrix.dtype),
            jax.ShapeDtypeStruct((4 + planes, SUB, LANES), jnp.float32),
            jax.ShapeDtypeStruct((planes, SUB, LANES), jnp.float32),
        )
        + tuple(jax.ShapeDtypeStruct(value.shape, value.dtype) for value in kept),
        in_specs=[pl.BlockSpec(memory_space=pltpu.MemorySpace.HBM)] * len(inputs),
        out_specs=(pl.BlockSpec(memory_space=VMEM),) * (4 + len(kept)),
        scratch_shapes=[
            pltpu.VMEM(matrix.shape, matrix.dtype),
            pltpu.VMEM(centers.shape, centers.dtype),
            pltpu.VMEM(weights.shape, weights.dtype),
            pltpu.SemaphoreType.DMA((len(inputs),)),
        ],
        cost_estimate=pl.CostEstimate(flops=10**6, bytes_accessed=10**6, transcendentals=0),
        compiler_params=pltpu.CompilerParams(vmem_limit_bytes=GRANT),
        name="prepare",
    )(*in_place(*inputs))


def records_kernel(extent, lines, offsets, *refs):
    packet_refs = refs[:extent]
    pick_ref, dest_ref, block_ref, field_ref, force_ref = refs[extent:]
    count = pick_ref.shape[1]
    here = [lax.axis_index(axis) for axis in ALL]
    anchor = [place.astype(jnp.float32) * domain_edge for place in here]
    pick, dest, block = pick_ref[...], dest_ref[...], block_ref[...]
    lane, group = pick & (LANES - 1), pick >> 7
    behind = here[0] - dest
    behind = jnp.where(behind < 0, behind + extent, behind)
    iota = functools.partial(lax.broadcasted_iota, jnp.int32)
    one_lane = (iota((LANES, count), 0) == lane).astype(jnp.bfloat16)
    in_group = iota((SUB, count), 0) == group
    half = block >> 1
    odd = (block & 1) == 1
    one_line = (iota((extent * lines, count), 0) == behind * lines + half).astype(jnp.bfloat16)
    one_out = (iota((extent * lines, count), 0) == dest * lines + half).astype(jnp.bfloat16)

    def exact(product, value):
        high, middle, low = thirds(value)
        return product(high) + product(middle) + product(low)

    def dot(contract):
        return lambda other: lambda value: lax.dot_general(
            value, other, (contract, ((), ())), preferred_element_type=jnp.float32
        )

    own = packet_refs[0]
    atoms = jnp.concatenate([own[c] for c in range(4)], axis=0)
    spread = exact(dot(((1,), (0,)))(one_lane), atoms)
    taken = [
        jnp.sum(jnp.where(in_group, spread[c * SUB : (c + 1) * SUB], 0.0), axis=0, keepdims=True)
        for c in range(4)
    ]

    def line(k, n):
        return packet_refs[k][offsets[k] + n // SUB, n % SUB : n % SUB + 1, :]

    def chosen(c):
        table = jnp.concatenate(
            [line(k, c * lines + n) for k in range(extent) for n in range(lines)], axis=0
        )
        both = exact(dot(((0,), (0,)))(one_line), table)
        return jnp.where(odd, both[BLOCK:], both[:BLOCK])

    charge = taken[3]
    offset = [taken[c] + anchor[c] - chosen(c) for c in range(3)]
    weight = chosen(3)
    distance = offset[0] * offset[0] + offset[1] * offset[1] + offset[2] * offset[2] + soften
    inverse = lax.rsqrt(distance)
    terms = hartree_nm * charge * inverse
    terms = jnp.concatenate([jnp.where(odd, 0.0, terms), jnp.where(odd, terms, 0.0)], axis=0)
    high, middle, low = thirds(terms)
    field = sum(
        lax.dot_general(one_out, piece, (((1,), (1,)), ((), ())), preferred_element_type=jnp.float32)
        for piece in (high, middle, low)
    )
    field = jnp.concatenate(
        [
            jnp.concatenate([field[r * lines + n : r * lines + n + 1] for n in range(lines)], axis=1)
            for r in range(extent)
        ],
        axis=0,
    ).astype(field_ref.dtype)
    for device in range(field_ref.shape[0]):
        field_ref[device] = field
    strength = weight * (inverse * inverse * inverse)
    pushes = [
        coulomb * charge * jnp.sum(strength * offset[c], axis=0, keepdims=True) for c in range(3)
    ]
    pushes = jnp.concatenate([jnp.where(in_group, push, 0.0) for push in pushes], axis=0)
    total = exact(dot(((1,), (1,)))(one_lane), pushes)
    for c in range(3):
        force_ref[c] = total[c * SUB : (c + 1) * SUB]


def embedding(order, devices, packets, offsets, pick, dest, block):
    extent, lines = len(packets), order // LANES
    return in_vmem(
        functools.partial(records_kernel, extent, lines, offsets),
        (
            jax.ShapeDtypeStruct((devices, extent, order), jnp.bfloat16),
            jax.ShapeDtypeStruct((3, SUB, LANES), jnp.float32),
        ),
        *packets,
        pick,
        dest,
        block,
    )


def field_kernel(parts_ref, rows_ref, columns_ref):
    devices, extent, order = parts_ref.shape
    total = parts_ref[0].astype(jnp.float32)
    for k in range(1, devices):
        total = total + parts_ref[k].astype(jnp.float32)
    lines = order // LANES
    for r in range(extent):
        for n in range(lines):
            line = total[r : r + 1, n * LANES : (n + 1) * LANES]
            k = r * lines + n
            rows_ref[k : k + 1, :] = line
            columns_ref[k * LANES : (k + 1) * LANES, :] = jnp.broadcast_to(line, (LANES, LANES)).T


def whole_field(parts):
    _, extent, order = parts.shape
    size = extent * order
    return in_vmem(
        field_kernel,
        (
            jax.ShapeDtypeStruct((size // LANES, LANES), jnp.float32),
            jax.ShapeDtypeStruct((size, LANES), jnp.float32),
        ),
        parts,
    )


def modulo(value, count):
    return jnp.where(value < 0, value + count, value)


def keep_pattern(pattern_ref, first, value):
    rows, order, blocks = value.shape[0], value.shape[1], pattern_ref.shape[0]
    row_block = lax.broadcasted_iota(jnp.int32, (rows, blocks), 0) + first
    below = (
        row_block // BLOCK == lax.broadcasted_iota(jnp.int32, (rows, blocks), 1)
    ).astype(jnp.bfloat16)
    across = (
        lax.broadcasted_iota(jnp.int32, (order, blocks), 0) // BLOCK
        == lax.broadcasted_iota(jnp.int32, (order, blocks), 1)
    ).astype(jnp.bfloat16)
    marks = (pattern_ref[...] == 1).astype(jnp.float32).astype(jnp.bfloat16)
    wide = jnp.dot(below, marks, preferred_element_type=jnp.float32).astype(jnp.bfloat16)
    keep = lax.dot_general(wide, across, (((1,), (1,)), ((), ())), preferred_element_type=jnp.float32)
    return jnp.where(keep > 0.5, value, 0.0)


def sent_rows(order, width):
    return width if order == 2 * width else order


def first_row(order, width, sent):
    layer = lax.axis_index("grp")
    if not sent:
        return pl.multiple_of(layer * width, width)
    return pl.multiple_of((1 - layer) * width, width) if order == 2 * width else 0


def row_product(table_ref, tiles, right_refs, first, rows):
    total = jnp.zeros((rows, right_refs[0].shape[-1]), jnp.float32)
    for tile, right_ref in zip(tiles, right_refs):
        total = total + jnp.dot(
            table_ref[tile, pl.ds(first, rows), :],
            right_ref[...],
            preferred_element_type=jnp.float32,
        )
    return total


def tiles_behind(extent):
    row = lax.axis_index("qr")
    return [modulo(row - k, extent) for k in range(extent)]


def product_send_kernel(places, pattern_ref, *refs):
    left_refs, right_refs, (send_ref, table_ref) = refs[: len(places)], refs[len(places) : -2], refs[-2:]
    column = lax.axis_index("qc")
    for left_ref, place in zip(left_refs, places):
        table_ref[place(column)] = left_ref[...]
    _, order, width = table_ref.shape
    rows = sent_rows(order, width)
    first = first_row(order, width, True)
    value = row_product(table_ref, tiles_behind(len(right_refs)), right_refs, first, rows)
    send_ref[...] = keep_pattern(pattern_ref, first, value).astype(send_ref.dtype)


def product_own_kernel(pattern_ref, table_ref, *refs):
    right_refs, own_ref = refs[:-1], refs[-1]
    _, order, width = table_ref.shape
    first = first_row(order, width, False)
    value = row_product(table_ref, tiles_behind(len(right_refs)), right_refs, first, width)
    own_ref[...] = keep_pattern(pattern_ref, first, value)


def in_vmem(kernel, out_shape, *values, work=10**6):
    return pl.pallas_call(
        kernel,
        out_shape=out_shape,
        in_specs=[pl.BlockSpec(memory_space=VMEM)] * len(values),
        out_specs=jax.tree.map(lambda _: pl.BlockSpec(memory_space=VMEM), out_shape),
        cost_estimate=pl.CostEstimate(flops=work, bytes_accessed=work, transcendentals=0),
        compiler_params=pltpu.CompilerParams(vmem_limit_bytes=GRANT),
    )(*values)


def product_send(pattern, lefts, places, rights):
    order, width = lefts[0].shape
    return in_vmem(
        functools.partial(product_send_kernel, places),
        (
            jax.ShapeDtypeStruct((sent_rows(order, width), order), jnp.bfloat16),
            jax.ShapeDtypeStruct((len(lefts), order, width), jnp.bfloat16),
        ),
        pattern,
        *lefts,
        *rights,
    )


def product_own(pattern, table, rights):
    _, order, width = table.shape
    out = jax.ShapeDtypeStruct((width, order), jnp.float32)
    return in_vmem(product_own_kernel, out, pattern, table, *rights)


def cube_send_kernel(pattern_ref, table_ref, rows_ref, columns_ref, *refs):
    extent = (len(refs) - 2) // 2
    product_refs, right_refs = refs[:extent], refs[extent : 2 * extent]
    send_ref, square_ref = refs[2 * extent :]
    _, order, width = table_ref.shape
    lines = order // LANES
    column, layer = lax.axis_index("qc"), lax.axis_index("grp")
    start = layer * width
    iota = functools.partial(lax.broadcasted_iota, jnp.int32)
    tiles = tiles_behind(extent)
    for k, tile in enumerate(tiles):
        down = columns_ref[pl.ds(pl.multiple_of(tile * order + start, width), width), :]
        for n in range(lines):
            spot = slice(n * LANES, (n + 1) * LANES)
            across = rows_ref[pl.ds(column * lines + n, 1), :]
            matrix = right_refs[k][:, spot].astype(jnp.float32)
            on_diagonal = iota((width, LANES), 0) + start == iota((width, LANES), 1) + n * LANES
            corner = jnp.where(on_diagonal & (tile == column), down * down, 0.0)
            piece = product_refs[k][:, spot].astype(jnp.float32) + matrix * (down + across) + corner
            square_ref[k, :, spot] = piece.astype(jnp.bfloat16)
    rows = sent_rows(order, width)
    first = first_row(order, width, True)
    squares = [square_ref.at[k] for k in range(extent)]
    value = row_product(table_ref, tiles, squares, first, rows)
    send_ref[...] = keep_pattern(pattern_ref, first, value).astype(send_ref.dtype)


def cube_send(pattern, table, rows, columns, products, rights):
    extent, (_, order, width) = len(rights), table.shape
    return in_vmem(
        cube_send_kernel,
        (
            jax.ShapeDtypeStruct((sent_rows(order, width), order), jnp.bfloat16),
            jax.ShapeDtypeStruct((extent, width, order), jnp.bfloat16),
        ),
        pattern,
        table,
        rows,
        columns,
        *products,
        *rights,
    )


def cube_own_kernel(pattern_ref, table_ref, square_ref, columns_ref, right_ref, out_ref):
    extent, width, order = square_ref.shape
    row, column = lax.axis_index("qr"), lax.axis_index("qc")
    first = first_row(order, width, False)
    down = columns_ref[pl.ds(pl.multiple_of(row * order + first, width), width), :]
    iota = functools.partial(lax.broadcasted_iota, jnp.int32)
    parts = []
    for start in range(0, width, LANES):
        size = min(LANES, width - start)
        on_diagonal = iota((width, size), 0) == iota((width, size), 1) + start
        parts.append(jnp.where(on_diagonal, down[:, :size], 0.0))
    added = parts[0] if len(parts) == 1 else jnp.concatenate(parts, axis=1)
    value = jnp.zeros((width, order), jnp.float32)
    for k, tile in enumerate(tiles_behind(extent)):
        operand = table_ref[tile, pl.ds(first, width), :]
        if k == 0:
            operand = (operand.astype(jnp.float32) + added).astype(jnp.bfloat16)
        value = value + jnp.dot(operand, square_ref[k], preferred_element_type=jnp.float32)
    value = keep_pattern(pattern_ref, first, value)
    for n in range(order // LANES):
        spot = slice(n * LANES, (n + 1) * LANES)
        on_diagonal = iota((width, LANES), 0) + first == iota((width, LANES), 1) + n * LANES
        diagonal = jnp.where(on_diagonal & (row == column), down, 0.0)
        shifted = (right_ref[:, spot].astype(jnp.float32) + diagonal).astype(jnp.bfloat16)
        out_ref[:, spot] = 0.5 * (3.0 * shifted.astype(jnp.float32) - value[:, spot])


def cube_own(pattern, table, squares, columns, right):
    _, width, order = squares.shape
    out = jax.ShapeDtypeStruct((width, order), jnp.float32)
    return in_vmem(cube_own_kernel, out, pattern, table, squares, columns, right)


def final_kernel(own_ref, got_ref, out_ref):
    out_ref[...] = (own_ref[...] - 0.5 * got_ref[...].astype(jnp.float32)).astype(out_ref.dtype)


def final_step(own, got):
    return in_vmem(final_kernel, jax.ShapeDtypeStruct(own.shape, jnp.bfloat16), own, got)


KEY_BITS = 8
GROUP_BITS = 3
BATCH = 8
CHUNK = 24


def packing_kernel(inner, *refs):
    *near_refs, packed_ref, scale_ref = refs
    picks = [(near_ref, i) for i in range(inner) for near_ref in near_refs]
    domains = len(picks)

    def entry(d, c):
        near_ref, i = picks[d]
        return near_ref[i, c]

    low = [entry(0, c) for c in range(4)]
    high = list(low)
    for d in range(1, domains):
        for c in range(4):
            value = entry(d, c)
            low[c] = jnp.minimum(low[c], value)
            high[c] = jnp.maximum(high[c], value)
    steps = 65535.0
    base, back = [], []
    for c in range(4):
        least = jnp.min(low[c], axis=(0, 1), keepdims=True)
        width = jnp.maximum(jnp.max(high[c], axis=(0, 1), keepdims=True) - least, 1e-30)
        base.append(jnp.broadcast_to(least, (SUB, LANES)))
        back.append(jnp.broadcast_to(steps / width, (SUB, LANES)))
        scale_ref[c] = base[c]
        scale_ref[4 + c] = jnp.broadcast_to(width * (1.0 / steps), (SUB, LANES))
    for d in range(domains):
        code = [
            jnp.clip((entry(d, c) - base[c]) * back[c] + 0.5, 0.0, steps).astype(jnp.int32)
            for c in range(4)
        ]
        start = (SUB - 1) * domains + d * SUB
        packed_ref[0, start : start + SUB, :] = code[0] | (code[1] << 16)
        packed_ref[1, start : start + SUB, :] = code[2] | (code[3] << 16)
    front, size = (SUB - 1) * domains, domains * SUB
    for w in range(2):
        packed_ref[w, :front, :] = jnp.zeros((front, LANES), jnp.int32)
        packed_ref[w, front + size :, :] = jnp.zeros((front + CHUNK, LANES), jnp.int32)


def packing(near):
    domains = len(near) * near[0].shape[0]
    rows = domains * SUB + 2 * (SUB - 1) * domains + CHUNK
    return pl.pallas_call(
        functools.partial(packing_kernel, near[0].shape[0]),
        out_shape=(
            jax.ShapeDtypeStruct((2, rows, LANES), jnp.int32),
            jax.ShapeDtypeStruct((8, SUB, LANES), jnp.float32),
        ),
        in_specs=[pl.BlockSpec(memory_space=VMEM)] * len(near),
        out_specs=(pl.BlockSpec(memory_space=VMEM),) * 2,
        cost_estimate=pl.CostEstimate(flops=10**7, bytes_accessed=5 * 10**6, transcendentals=0),
        compiler_params=pltpu.CompilerParams(vmem_limit_bytes=GRANT),
        name="packing",
    )(*near)


def compact(place, count):
    if count >= 3:
        return place
    if count == 2:
        return jnp.where(place == 1, 0, 1)
    return jnp.zeros_like(place)


def places_of(slot):
    p = (slot * 57) >> 9
    rest = slot - 9 * p
    q = (rest * 11) >> 5
    return p, q, rest - 3 * q


def network(count):
    pairs = []
    p = 1
    while p < count:
        k = p
        while k >= 1:
            for j in range(k % p, count - k, 2 * k):
                for i in range(min(k, count - j - k)):
                    if (i + j) // (2 * p) == (i + j + k) // (2 * p):
                        pairs.append((i + j, i + j + k))
            k //= 2
        p *= 2
    return pairs


def sorting_kernel(counts, lists_hbm, keys_ref, range_ref, spread_ref, lists_ref, sem):
    copy = pltpu.make_async_copy(lists_hbm, lists_ref, sem)
    copy.start()
    copy.wait()
    entries = lists_ref.shape[1]
    distinct = [min(3, count) for count in counts]
    domains = distinct[0] * distinct[1] * distinct[2]
    keys = []
    for b in range(entries // SUB):
        for a in range(SUB):
            slot = lists_ref[0, b * SUB : (b + 1) * SUB, a * LANES : (a + 1) * LANES]
            member = lists_ref[1, b * SUB : (b + 1) * SUB, a * LANES : (a + 1) * LANES]
            p, q, r = places_of(slot)
            domain = (
                compact(p, counts[0]) * distinct[1] + compact(q, counts[1])
            ) * distinct[2] + compact(r, counts[2])
            key = ((domain * (SUB * LANES) + member) << KEY_BITS) + (slot << GROUP_BITS) + a
            keys.append(key.astype(jnp.float32))
    size = len(keys)
    sublane = lax.broadcasted_iota(jnp.int32, (SUB, LANES), 0)

    def turned(values, bit):
        sign = jnp.where((sublane >> bit) & 1 == 1, -1.0, 1.0)
        return [value * sign for value in values]

    def by_sublane(values):
        for v in range(size):
            spread_ref[pl.ds(v, SUB, stride=size), :] = values[v]
        return [spread_ref[n * SUB : (n + 1) * SUB, :] for n in range(size)]

    def by_register(values):
        for n in range(size):
            spread_ref[n * SUB : (n + 1) * SUB, :] = values[n]
        return [spread_ref[pl.ds(v, SUB, stride=size), :] for v in range(size)]

    def exchange(values, i, j, up=True):
        low, high = jnp.minimum(values[i], values[j]), jnp.maximum(values[i], values[j])
        values[i], values[j] = (low, high) if up else (high, low)

    keys = turned(keys, 0)
    for i, j in network(size):
        exchange(keys, i, j)
    keys = turned(keys, 0)
    run = size // SUB
    for level in range(1, 4):
        keys = by_sublane(keys)
        for step in reversed(range(level)):
            for s in range(SUB):
                if not s >> step & 1:
                    for n in range(run):
                        exchange(
                            keys,
                            s * run + n,
                            (s | 1 << step) * run + n,
                            level == 3 or not s >> level & 1,
                        )
        keys = by_register(keys)
        if level < 3:
            keys = turned(keys, level)
        stride = size // 2
        while stride:
            for v in range(size):
                if not v & stride:
                    exchange(keys, v, v | stride)
            stride //= 2
        if level < 3:
            keys = turned(keys, level)

    whole = [key.astype(jnp.int32) for key in keys]
    for v in range(size):
        keys_ref[v] = whole[v]
    base = sublane * domains
    lows = [(whole[v] >> (KEY_BITS + 7)) - base for v in range(0, size, BATCH)]
    highs = [(whole[v + BATCH - 1] >> (KEY_BITS + 7)) - base for v in range(0, size, BATCH)]
    least = jnp.concatenate(
        [jnp.min(low.astype(jnp.float32), axis=0, keepdims=True) for low in lows], axis=0
    )
    most = jnp.concatenate(
        [jnp.max(high.astype(jnp.float32), axis=0, keepdims=True) for high in highs], axis=0
    )
    least = jnp.min(least, axis=1, keepdims=True)
    most = jnp.max(most, axis=1, keepdims=True)
    both = jnp.concatenate([least, most], axis=0).astype(jnp.int32)
    range_ref[...] = jnp.broadcast_to(both, range_ref.shape)


def sorting(counts, lists):
    entries = lists.shape[1]
    return pl.pallas_call(
        functools.partial(sorting_kernel, counts),
        out_shape=(
            jax.ShapeDtypeStruct((entries, SUB, LANES), jnp.int32),
            jax.ShapeDtypeStruct((2 * entries // BATCH, LANES), jnp.int32),
        ),
        in_specs=[pl.BlockSpec(memory_space=pltpu.MemorySpace.HBM)],
        out_specs=(pl.BlockSpec(memory_space=VMEM),) * 2,
        scratch_shapes=[
            pltpu.VMEM((entries * SUB, LANES), jnp.float32),
            pltpu.VMEM(lists.shape, jnp.int32),
            pltpu.SemaphoreType.DMA,
        ],
        cost_estimate=pl.CostEstimate(flops=10**7, bytes_accessed=5 * 10**6, transcendentals=0),
        compiler_params=pltpu.CompilerParams(vmem_limit_bytes=GRANT),
        name="sorting",
    )(*in_place(lists))


def pair_kernel(
    domains, first, last, range_ref, keys_ref, own_ref, packed_ref, scale_ref, start_ref, force_ref
):
    blocks = keys_ref.shape[0] // BATCH
    front = (SUB - 1) * domains
    base = lax.broadcasted_iota(jnp.int32, (SUB, LANES), 0) * domains

    def step(j, sums):
        keys = [keys_ref[j * BATCH + i] for i in range(BATCH)]
        rows = [(key >> (KEY_BITS + 7)) - base for key in keys]
        lanes = [(key >> KEY_BITS) & (LANES - 1) for key in keys]
        low = range_ref[j, 0]
        rounds = (range_ref[blocks + j, 0] - low) // CHUNK + 1

        def scan(i, words):
            words = list(words)
            start = low + i * CHUNK
            for m in range(BATCH):
                for u in range(CHUNK):
                    here = rows[m] == start + u
                    for w in range(2):
                        lines = packed_ref[w, pl.ds(front + start + u, SUB, stride=domains), :]
                        k = 2 * m + w
                        words[k] = jnp.where(here, pick_lanes(lines, lanes[m]), words[k])
            return tuple(words)

        zero = jnp.zeros((SUB, LANES), jnp.int32)
        words = lax.fori_loop(0, rounds, scan, (zero,) * (2 * BATCH))
        sums = list(sums)
        for m in range(BATCH):
            group = keys[m] & ((1 << GROUP_BITS) - 1)
            places = places_of((keys[m] >> GROUP_BITS) & 31)
            mine = [group == g for g in range(SUB)]
            one, two = words[2 * m], words[2 * m + 1]
            code = [one & 0xFFFF, (one >> 16) & 0xFFFF, two & 0xFFFF, (two >> 16) & 0xFFFF]
            value = [code[c].astype(jnp.float32) * scale_ref[4 + c] + scale_ref[c] for c in range(4)]
            offset = []
            for c in range(3):
                place = own_ref[c, 0:1, :]
                for g in range(1, SUB):
                    place = jnp.where(mine[g], own_ref[c, g : g + 1, :], place)
                shift = (places[c] - 1).astype(jnp.float32) * domain_edge
                offset.append(place - (value[c] + shift))
            distance = (
                offset[0] * offset[0] + offset[1] * offset[1] + offset[2] * offset[2] + soften
            )
            inverse = lax.rsqrt(distance)
            strength = value[3] * (inverse * inverse * inverse)
            for c in range(3):
                push = offset[c] * strength
                for g in range(SUB):
                    k = c * SUB + g
                    sums[k] = sums[k] + jnp.where(mine[g], push, 0.0)
        return tuple(sums)

    zero = jnp.zeros((SUB, LANES), jnp.float32)
    sums = lax.fori_loop(first, last, step, (zero,) * (3 * SUB))
    for c in range(3):
        total = jnp.concatenate(
            [jnp.sum(sums[c * SUB + g], axis=0, keepdims=True) for g in range(SUB)], axis=0
        )
        force_ref[c] = start_ref[c] + coulomb * own_ref[3] * total


def pair_forces(first, last, ranges, keys, own, packed, scale, start):
    return pl.pallas_call(
        functools.partial(pair_kernel, (packed.shape[1] - CHUNK) // (3 * SUB - 2), first, last),
        out_shape=jax.ShapeDtypeStruct((3, SUB, LANES), jnp.float32),
        in_specs=[pl.BlockSpec(memory_space=SMEM)] + [pl.BlockSpec(memory_space=VMEM)] * 5,
        out_specs=pl.BlockSpec(memory_space=VMEM),
        cost_estimate=pl.CostEstimate(
            flops=10**7, bytes_accessed=(last - first) * BATCH * 10**5 * 3, transcendentals=0
        ),
        compiler_params=pltpu.CompilerParams(vmem_limit_bytes=GRANT),
        name="pairs",
    )(ranges, keys, own, packed, scale, start)


def neighbourhood(counts, along_rows):
    reach = [(-1, 0, 1) if n >= 3 else (0, 1) if n == 2 else (0,) for n in counts]
    mine = jnp.stack([along_rows[(-i) % counts[0]] for i in reach[0]])
    columns, layers = counts[1:]
    near = []
    for j in reach[1]:
        for k in reach[2]:
            if (j, k) == (0, 0):
                near.append(mine)
                continue
            pairs = [
                (((c + j) % columns) * layers + (g + k) % layers, c * layers + g)
                for c in range(columns)
                for g in range(layers)
            ]
            near.append(lax.ppermute(mine, ("qc", "grp"), pairs))
    return near


def crossed(value, axis):
    count = lax.axis_size(axis)
    if count & (count - 1):
        return rotated(value, axis), [lambda me, k=k: modulo(me - k, count) for k in range(count)]
    return (
        [value]
        + [lax.ppermute(value, axis, [(i, i ^ k) for i in range(count)]) for k in range(1, count)],
        [lambda me, k=k: me ^ k for k in range(count)],
    )


def per_device(
    kohn_sham, pattern, basis_centers, occupations, atoms, neighbours, emb_atom, emb_dest, emb_block
):
    counts = tuple(lax.axis_size(axis) for axis in ALL)
    layers = counts[2]
    order = kohn_sham.shape[0]
    width = order // layers
    record_count = emb_atom.shape[0]
    own = atoms.reshape(4, SUB, LANES)
    after = lax.optimization_barrier

    left_own, right_own, packet, basis, pattern, *records = prepare(
        width,
        kohn_sham,
        own,
        basis_centers,
        occupations,
        pattern,
        emb_atom.reshape(1, record_count),
        emb_dest.reshape(1, record_count),
        emb_block.reshape(1, record_count),
    )
    near_row = [min(k, counts[0] - k) <= 1 for k in range(counts[0])]
    packets = rotated(lambda k: packet if near_row[k] else basis, "qr")
    rights = rotated(right_own, "qr")
    lefts, places = crossed(left_own, "qc")
    field, embed_force = embedding(
        order,
        counts[0] * counts[1] * counts[2],
        packets,
        [4 if close else 0 for close in near_row],
        *records,
    )
    field_all = lax.all_to_all(field, ALL, split_axis=0, concat_axis=0, tiled=True)
    near = neighbourhood(counts, [piece[:4] for piece in packets])

    def from_layers(send):
        if layers == 2:
            return lax.ppermute(send, "grp", [(0, 1), (1, 0)])
        got = lax.all_to_all(
            send.reshape(layers, width, order), "grp", split_axis=0, concat_axis=0, tiled=True
        )
        other = jnp.arange(layers)[:, None, None] != lax.axis_index("grp")
        return jnp.sum(jnp.where(other, got.astype(jnp.float32), 0.0), axis=0)

    send, table = product_send(pattern, lefts, places, rights)
    got = from_layers(send)
    mine = product_own(pattern, table, rights)
    lists, mine = after((neighbours[0, 0, 0], mine))
    keys, ranges = sorting(counts, lists)
    blocks = keys.shape[0] // BATCH
    got, keys = after((got, keys))
    rows, columns = whole_field(field_all)
    product_rows = (mine + got.astype(jnp.float32)).astype(jnp.bfloat16)
    products = rotated(product_rows, "qr")
    packed, scale = packing(near)
    product_rows, packed = after((product_rows, packed))
    cut = (blocks + 1) // 2
    force = pair_forces(0, cut, ranges, keys, own, packed, scale, embed_force)
    *received, force = after((*products[1:], force))
    products = [products[0]] + received

    send, squares = cube_send(pattern, table, rows, columns, products, rights)
    got = from_layers(send)
    squares, force = after((squares, force))
    result = cube_own(pattern, table, squares, columns, right_own)
    force = pair_forces(cut, blocks, ranges, keys, own, packed, scale, force)
    got, force, result = after((got, force, result))
    sign_step = final_step(result, got)
    return (sign_step, force.reshape(3, 1, 1, 1, SUB * LANES))


def solution(mesh):
    in_specs = (
        P("qr", "qc"),
        P("qr", "qc"),
        P(None, "qr"),
        P("qr"),
        P(None, "qr", "qc", "grp", None),
        P("qr", "qc", "grp", None, None, None),
        P(("qr", "qc", "grp")),
        P(("qr", "qc", "grp"), None),
        P(("qr", "qc", "grp")),
    )
    out_specs = (P(("qr", "grp"), "qc"), P(None, "qr", "qc", "grp", None))

    return jax.shard_map(
        per_device, mesh=mesh, in_specs=in_specs, out_specs=out_specs, check_vma=False
    )
```

```python
import functools

import jax
import jax.numpy as jnp
from jax import lax
from jax.experimental import pallas as pl
from jax.experimental.pallas import tpu as pltpu
from jax.sharding import PartitionSpec as P


BLOCK = 64
SUB, LANES = 8, 128

coulomb = 138.935
hartree_nm = 0.0529177
soften = 0.01
domain_edge = 3.4

ALL = ("qr", "qc", "grp")
VMEM = pltpu.MemorySpace.VMEM
GRANT = 16 << 20
SMEM = pltpu.MemorySpace.SMEM

LANE_PICK = lax.GatherDimensionNumbers(
    offset_dims=(),
    collapsed_slice_dims=(1,),
    start_index_map=(1,),
    operand_batching_dims=(0,),
    start_indices_batching_dims=(0,),
)


def pick_lanes(row, lane):
    return lax.gather(
        row, lane[..., None], LANE_PICK, (1, 1), mode=lax.GatherScatterMode.PROMISE_IN_BOUNDS
    )


def rotated(value, axis):
    count = lax.axis_size(axis)
    of = value if callable(value) else lambda k: value
    return [of(0)] + [
        lax.ppermute(of(k), axis, [(i, (i + k) % count) for i in range(count)])
        for k in range(1, count)
    ]


def in_place(*values):
    return [pltpu.with_memory_space_constraint(value, pltpu.MemorySpace.HBM) for value in values]


def thirds(value):
    high = value.astype(jnp.bfloat16)
    rest = value - high.astype(jnp.float32)
    middle = rest.astype(jnp.bfloat16)
    low = (rest - middle.astype(jnp.float32)).astype(jnp.bfloat16)
    return high, middle, low


def prepare_kernel(count, *refs):
    inputs, (left_ref, right_ref, packet_ref, basis_ref), kept, buffers = (
        refs[:count],
        refs[count : count + 4],
        refs[count + 4 : -4],
        refs[-4:],
    )
    matrix_buf, centers_buf, weights_buf, sems = buffers
    order, width = left_ref.shape
    layer = lax.axis_index("grp")
    targets = [matrix_buf, packet_ref.at[0:4], centers_buf, weights_buf] + list(kept)
    copies = [
        pltpu.make_async_copy(source, target, sems.at[i])
        for i, (source, target) in enumerate(zip(inputs, targets))
    ]
    for copy in copies:
        copy.start()
    copies[2].wait()
    copies[3].wait()
    lines = order // LANES
    rows = [
        centers_buf[c : c + 1, n * LANES : (n + 1) * LANES] for c in range(3) for n in range(lines)
    ]
    rows = rows + [weights_buf[n * LANES : (n + 1) * LANES].reshape(1, LANES) for n in range(lines)]
    planes = packet_ref.shape[0] - 4
    rows = rows + [jnp.zeros((1, LANES), jnp.float32)] * (planes * SUB - len(rows))
    for n in range(planes):
        basis = jnp.concatenate(rows[n * SUB : (n + 1) * SUB], axis=0)
        packet_ref[4 + n] = basis
        basis_ref[n] = basis
    copies[0].wait()
    right_ref[...] = matrix_buf[pl.ds(pl.multiple_of(layer * width, width), width), :]
    for i in range(order // width):

        @pl.when(layer == i)
        def _():
            left_ref[...] = matrix_buf[:, i * width : (i + 1) * width]

    for copy in copies[1:2] + copies[4:]:
        copy.wait()


def prepare(width, matrix, atoms, centers, weights, *kept):
    order = matrix.shape[0]
    planes = -(-4 * (order // LANES) // SUB)
    inputs = (matrix, atoms, centers, weights) + kept
    return pl.pallas_call(
        functools.partial(prepare_kernel, len(inputs)),
        out_shape=(
            jax.ShapeDtypeStruct((order, width), matrix.dtype),
            jax.ShapeDtypeStruct((width, order), matrix.dtype),
            jax.ShapeDtypeStruct((4 + planes, SUB, LANES), jnp.float32),
            jax.ShapeDtypeStruct((planes, SUB, LANES), jnp.float32),
        )
        + tuple(jax.ShapeDtypeStruct(value.shape, value.dtype) for value in kept),
        in_specs=[pl.BlockSpec(memory_space=pltpu.MemorySpace.HBM)] * len(inputs),
        out_specs=(pl.BlockSpec(memory_space=VMEM),) * (4 + len(kept)),
        scratch_shapes=[
            pltpu.VMEM(matrix.shape, matrix.dtype),
            pltpu.VMEM(centers.shape, centers.dtype),
            pltpu.VMEM(weights.shape, weights.dtype),
            pltpu.SemaphoreType.DMA((len(inputs),)),
        ],
        cost_estimate=pl.CostEstimate(flops=10**6, bytes_accessed=10**6, transcendentals=0),
        compiler_params=pltpu.CompilerParams(vmem_limit_bytes=GRANT),
        name="prepare",
    )(*in_place(*inputs))


def records_kernel(extent, lines, offsets, *refs):
    packet_refs = refs[:extent]
    pick_ref, dest_ref, block_ref, field_ref, force_ref = refs[extent:]
    count = pick_ref.shape[1]
    here = [lax.axis_index(axis) for axis in ALL]
    anchor = [place.astype(jnp.float32) * domain_edge for place in here]
    pick, dest, block = pick_ref[...], dest_ref[...], block_ref[...]
    lane, group = pick & (LANES - 1), pick >> 7
    behind = here[0] - dest
    behind = jnp.where(behind < 0, behind + extent, behind)
    iota = functools.partial(lax.broadcasted_iota, jnp.int32)
    one_lane = (iota((LANES, count), 0) == lane).astype(jnp.bfloat16)
    in_group = iota((SUB, count), 0) == group
    half = block >> 1
    odd = (block & 1) == 1
    one_line = (iota((extent * lines, count), 0) == behind * lines + half).astype(jnp.bfloat16)
    one_out = (iota((extent * lines, count), 0) == dest * lines + half).astype(jnp.bfloat16)

    def exact(product, value):
        high, middle, low = thirds(value)
        return product(high) + product(middle) + product(low)

    def dot(contract):
        return lambda other: lambda value: lax.dot_general(
            value, other, (contract, ((), ())), preferred_element_type=jnp.float32
        )

    own = packet_refs[0]
    atoms = jnp.concatenate([own[c] for c in range(4)], axis=0)
    spread = exact(dot(((1,), (0,)))(one_lane), atoms)
    taken = [
        jnp.sum(jnp.where(in_group, spread[c * SUB : (c + 1) * SUB], 0.0), axis=0, keepdims=True)
        for c in range(4)
    ]

    def line(k, n):
        return packet_refs[k][offsets[k] + n // SUB, n % SUB : n % SUB + 1, :]

    def chosen(c):
        table = jnp.concatenate(
            [line(k, c * lines + n) for k in range(extent) for n in range(lines)], axis=0
        )
        both = exact(dot(((0,), (0,)))(one_line), table)
        return jnp.where(odd, both[BLOCK:], both[:BLOCK])

    charge = taken[3]
    offset = [taken[c] + anchor[c] - chosen(c) for c in range(3)]
    weight = chosen(3)
    distance = offset[0] * offset[0] + offset[1] * offset[1] + offset[2] * offset[2] + soften
    inverse = lax.rsqrt(distance)
    terms = hartree_nm * charge * inverse
    terms = jnp.concatenate([jnp.where(odd, 0.0, terms), jnp.where(odd, terms, 0.0)], axis=0)
    high, middle, low = thirds(terms)
    field = sum(
        lax.dot_general(one_out, piece, (((1,), (1,)), ((), ())), preferred_element_type=jnp.float32)
        for piece in (high, middle, low)
    )
    field = jnp.concatenate(
        [
            jnp.concatenate([field[r * lines + n : r * lines + n + 1] for n in range(lines)], axis=1)
            for r in range(extent)
        ],
        axis=0,
    ).astype(field_ref.dtype)
    for device in range(field_ref.shape[0]):
        field_ref[device] = field
    strength = weight * (inverse * inverse * inverse)
    pushes = [
        coulomb * charge * jnp.sum(strength * offset[c], axis=0, keepdims=True) for c in range(3)
    ]
    pushes = jnp.concatenate([jnp.where(in_group, push, 0.0) for push in pushes], axis=0)
    total = exact(dot(((1,), (1,)))(one_lane), pushes)
    for c in range(3):
        force_ref[c] = total[c * SUB : (c + 1) * SUB]


def embedding(order, devices, packets, offsets, pick, dest, block):
    extent, lines = len(packets), order // LANES
    return in_vmem(
        functools.partial(records_kernel, extent, lines, offsets),
        (
            jax.ShapeDtypeStruct((devices, extent, order), jnp.bfloat16),
            jax.ShapeDtypeStruct((3, SUB, LANES), jnp.float32),
        ),
        *packets,
        pick,
        dest,
        block,
    )


def field_kernel(parts_ref, rows_ref, columns_ref):
    devices, extent, order = parts_ref.shape
    total = parts_ref[0].astype(jnp.float32)
    for k in range(1, devices):
        total = total + parts_ref[k].astype(jnp.float32)
    lines = order // LANES
    for r in range(extent):
        for n in range(lines):
            line = total[r : r + 1, n * LANES : (n + 1) * LANES]
            k = r * lines + n
            rows_ref[k : k + 1, :] = line
            columns_ref[k * LANES : (k + 1) * LANES, :] = jnp.broadcast_to(line, (LANES, LANES)).T


def whole_field(parts):
    _, extent, order = parts.shape
    size = extent * order
    return in_vmem(
        field_kernel,
        (
            jax.ShapeDtypeStruct((size // LANES, LANES), jnp.float32),
            jax.ShapeDtypeStruct((size, LANES), jnp.float32),
        ),
        parts,
    )


def modulo(value, count):
    return jnp.where(value < 0, value + count, value)


def keep_pattern(pattern_ref, first, value):
    rows, order, blocks = value.shape[0], value.shape[1], pattern_ref.shape[0]
    row_block = lax.broadcasted_iota(jnp.int32, (rows, blocks), 0) + first
    below = (
        row_block // BLOCK == lax.broadcasted_iota(jnp.int32, (rows, blocks), 1)
    ).astype(jnp.bfloat16)
    across = (
        lax.broadcasted_iota(jnp.int32, (order, blocks), 0) // BLOCK
        == lax.broadcasted_iota(jnp.int32, (order, blocks), 1)
    ).astype(jnp.bfloat16)
    marks = (pattern_ref[...] == 1).astype(jnp.float32).astype(jnp.bfloat16)
    wide = jnp.dot(below, marks, preferred_element_type=jnp.float32).astype(jnp.bfloat16)
    keep = lax.dot_general(wide, across, (((1,), (1,)), ((), ())), preferred_element_type=jnp.float32)
    return jnp.where(keep > 0.5, value, 0.0)


def sent_rows(order, width):
    return width if order == 2 * width else order


def first_row(order, width, sent):
    layer = lax.axis_index("grp")
    if not sent:
        return pl.multiple_of(layer * width, width)
    return pl.multiple_of((1 - layer) * width, width) if order == 2 * width else 0


def row_product(table_ref, tiles, right_refs, first, rows):
    total = jnp.zeros((rows, right_refs[0].shape[-1]), jnp.float32)
    for tile, right_ref in zip(tiles, right_refs):
        total = total + jnp.dot(
            table_ref[tile, pl.ds(first, rows), :],
            right_ref[...],
            preferred_element_type=jnp.float32,
        )
    return total


def tiles_behind(extent):
    row = lax.axis_index("qr")
    return [modulo(row - k, extent) for k in range(extent)]


def product_send_kernel(places, pattern_ref, *refs):
    left_refs, right_refs, (send_ref, table_ref) = refs[: len(places)], refs[len(places) : -2], refs[-2:]
    column = lax.axis_index("qc")
    for left_ref, place in zip(left_refs, places):
        table_ref[place(column)] = left_ref[...]
    _, order, width = table_ref.shape
    rows = sent_rows(order, width)
    first = first_row(order, width, True)
    value = row_product(table_ref, tiles_behind(len(right_refs)), right_refs, first, rows)
    send_ref[...] = keep_pattern(pattern_ref, first, value).astype(send_ref.dtype)


def product_own_kernel(pattern_ref, table_ref, *refs):
    right_refs, own_ref = refs[:-1], refs[-1]
    _, order, width = table_ref.shape
    first = first_row(order, width, False)
    value = row_product(table_ref, tiles_behind(len(right_refs)), right_refs, first, width)
    own_ref[...] = keep_pattern(pattern_ref, first, value)


def in_vmem(kernel, out_shape, *values, work=10**6):
    return pl.pallas_call(
        kernel,
        out_shape=out_shape,
        in_specs=[pl.BlockSpec(memory_space=VMEM)] * len(values),
        out_specs=jax.tree.map(lambda _: pl.BlockSpec(memory_space=VMEM), out_shape),
        cost_estimate=pl.CostEstimate(flops=work, bytes_accessed=work, transcendentals=0),
        compiler_params=pltpu.CompilerParams(vmem_limit_bytes=GRANT),
    )(*values)


def product_send(pattern, lefts, places, rights):
    order, width = lefts[0].shape
    return in_vmem(
        functools.partial(product_send_kernel, places),
        (
            jax.ShapeDtypeStruct((sent_rows(order, width), order), jnp.bfloat16),
            jax.ShapeDtypeStruct((len(lefts), order, width), jnp.bfloat16),
        ),
        pattern,
        *lefts,
        *rights,
    )


def product_own(pattern, table, rights):
    _, order, width = table.shape
    out = jax.ShapeDtypeStruct((width, order), jnp.float32)
    return in_vmem(product_own_kernel, out, pattern, table, *rights)


def cube_send_kernel(pattern_ref, table_ref, rows_ref, columns_ref, *refs):
    extent = (len(refs) - 2) // 2
    product_refs, right_refs = refs[:extent], refs[extent : 2 * extent]
    send_ref, square_ref = refs[2 * extent :]
    _, order, width = table_ref.shape
    lines = order // LANES
    column, layer = lax.axis_index("qc"), lax.axis_index("grp")
    start = layer * width
    iota = functools.partial(lax.broadcasted_iota, jnp.int32)
    tiles = tiles_behind(extent)
    for k, tile in enumerate(tiles):
        down = columns_ref[pl.ds(pl.multiple_of(tile * order + start, width), width), :]
        for n in range(lines):
            spot = slice(n * LANES, (n + 1) * LANES)
            across = rows_ref[pl.ds(column * lines + n, 1), :]
            matrix = right_refs[k][:, spot].astype(jnp.float32)
            on_diagonal = iota((width, LANES), 0) + start == iota((width, LANES), 1) + n * LANES
            corner = jnp.where(on_diagonal & (tile == column), down * down, 0.0)
            piece = product_refs[k][:, spot].astype(jnp.float32) + matrix * (down + across) + corner
            square_ref[k, :, spot] = piece.astype(jnp.bfloat16)
    rows = sent_rows(order, width)
    first = first_row(order, width, True)
    squares = [square_ref.at[k] for k in range(extent)]
    value = row_product(table_ref, tiles, squares, first, rows)
    send_ref[...] = keep_pattern(pattern_ref, first, value).astype(send_ref.dtype)


def cube_send(pattern, table, rows, columns, products, rights):
    extent, (_, order, width) = len(rights), table.shape
    return in_vmem(
        cube_send_kernel,
        (
            jax.ShapeDtypeStruct((sent_rows(order, width), order), jnp.bfloat16),
            jax.ShapeDtypeStruct((extent, width, order), jnp.bfloat16),
        ),
        pattern,
        table,
        rows,
        columns,
        *products,
        *rights,
    )


def cube_own_kernel(pattern_ref, table_ref, square_ref, columns_ref, right_ref, out_ref):
    extent, width, order = square_ref.shape
    row, column = lax.axis_index("qr"), lax.axis_index("qc")
    first = first_row(order, width, False)
    down = columns_ref[pl.ds(pl.multiple_of(row * order + first, width), width), :]
    iota = functools.partial(lax.broadcasted_iota, jnp.int32)
    parts = []
    for start in range(0, width, LANES):
        size = min(LANES, width - start)
        on_diagonal = iota((width, size), 0) == iota((width, size), 1) + start
        parts.append(jnp.where(on_diagonal, down[:, :size], 0.0))
    added = parts[0] if len(parts) == 1 else jnp.concatenate(parts, axis=1)
    value = jnp.zeros((width, order), jnp.float32)
    for k, tile in enumerate(tiles_behind(extent)):
        operand = table_ref[tile, pl.ds(first, width), :]
        if k == 0:
            operand = (operand.astype(jnp.float32) + added).astype(jnp.bfloat16)
        value = value + jnp.dot(operand, square_ref[k], preferred_element_type=jnp.float32)
    value = keep_pattern(pattern_ref, first, value)
    for n in range(order // LANES):
        spot = slice(n * LANES, (n + 1) * LANES)
        on_diagonal = iota((width, LANES), 0) + first == iota((width, LANES), 1) + n * LANES
        diagonal = jnp.where(on_diagonal & (row == column), down, 0.0)
        shifted = (right_ref[:, spot].astype(jnp.float32) + diagonal).astype(jnp.bfloat16)
        out_ref[:, spot] = 0.5 * (3.0 * shifted.astype(jnp.float32) - value[:, spot])


def cube_own(pattern, table, squares, columns, right):
    _, width, order = squares.shape
    out = jax.ShapeDtypeStruct((width, order), jnp.float32)
    return in_vmem(cube_own_kernel, out, pattern, table, squares, columns, right)


def final_kernel(own_ref, got_ref, out_ref):
    out_ref[...] = (own_ref[...] - 0.5 * got_ref[...].astype(jnp.float32)).astype(out_ref.dtype)


def final_step(own, got):
    return in_vmem(final_kernel, jax.ShapeDtypeStruct(own.shape, jnp.bfloat16), own, got)


KEY_BITS = 8
GROUP_BITS = 3
BATCH = 8
CHUNK = 24


def packing_kernel(inner, *refs):
    *near_refs, packed_ref, scale_ref = refs
    picks = [(near_ref, i) for i in range(inner) for near_ref in near_refs]
    domains = len(picks)

    def entry(d, c):
        near_ref, i = picks[d]
        return near_ref[i, c]

    low = [entry(0, c) for c in range(4)]
    high = list(low)
    for d in range(1, domains):
        for c in range(4):
            value = entry(d, c)
            low[c] = jnp.minimum(low[c], value)
            high[c] = jnp.maximum(high[c], value)
    steps = 65535.0
    base, back = [], []
    for c in range(4):
        least = jnp.min(low[c], axis=(0, 1), keepdims=True)
        width = jnp.maximum(jnp.max(high[c], axis=(0, 1), keepdims=True) - least, 1e-30)
        base.append(jnp.broadcast_to(least, (SUB, LANES)))
        back.append(jnp.broadcast_to(steps / width, (SUB, LANES)))
        scale_ref[c] = base[c]
        scale_ref[4 + c] = jnp.broadcast_to(width * (1.0 / steps), (SUB, LANES))
    for d in range(domains):
        code = [
            jnp.clip((entry(d, c) - base[c]) * back[c] + 0.5, 0.0, steps).astype(jnp.int32)
            for c in range(4)
        ]
        start = (SUB - 1) * domains + d * SUB
        packed_ref[0, start : start + SUB, :] = code[0] | (code[1] << 16)
        packed_ref[1, start : start + SUB, :] = code[2] | (code[3] << 16)
    front, size = (SUB - 1) * domains, domains * SUB
    for w in range(2):
        packed_ref[w, :front, :] = jnp.zeros((front, LANES), jnp.int32)
        packed_ref[w, front + size :, :] = jnp.zeros((front + CHUNK, LANES), jnp.int32)


def packing(near):
    domains = len(near) * near[0].shape[0]
    rows = domains * SUB + 2 * (SUB - 1) * domains + CHUNK
    return pl.pallas_call(
        functools.partial(packing_kernel, near[0].shape[0]),
        out_shape=(
            jax.ShapeDtypeStruct((2, rows, LANES), jnp.int32),
            jax.ShapeDtypeStruct((8, SUB, LANES), jnp.float32),
        ),
        in_specs=[pl.BlockSpec(memory_space=VMEM)] * len(near),
        out_specs=(pl.BlockSpec(memory_space=VMEM),) * 2,
        cost_estimate=pl.CostEstimate(flops=10**7, bytes_accessed=5 * 10**6, transcendentals=0),
        compiler_params=pltpu.CompilerParams(vmem_limit_bytes=GRANT),
        name="packing",
    )(*near)


def compact(place, count):
    if count >= 3:
        return place
    if count == 2:
        return jnp.where(place == 1, 0, 1)
    return jnp.zeros_like(place)


def places_of(slot):
    p = (slot * 57) >> 9
    rest = slot - 9 * p
    q = (rest * 11) >> 5
    return p, q, rest - 3 * q


def network(count):
    pairs = []
    p = 1
    while p < count:
        k = p
        while k >= 1:
            for j in range(k % p, count - k, 2 * k):
                for i in range(min(k, count - j - k)):
                    if (i + j) // (2 * p) == (i + j + k) // (2 * p):
                        pairs.append((i + j, i + j + k))
            k //= 2
        p *= 2
    return pairs


def sorting_kernel(counts, lists_hbm, keys_ref, range_ref, spread_ref, lists_ref, sem):
    copy = pltpu.make_async_copy(lists_hbm, lists_ref, sem)
    copy.start()
    copy.wait()
    entries = lists_ref.shape[1]
    distinct = [min(3, count) for count in counts]
    domains = distinct[0] * distinct[1] * distinct[2]
    keys = []
    for b in range(entries // SUB):
        for a in range(SUB):
            slot = lists_ref[0, b * SUB : (b + 1) * SUB, a * LANES : (a + 1) * LANES]
            member = lists_ref[1, b * SUB : (b + 1) * SUB, a * LANES : (a + 1) * LANES]
            p, q, r = places_of(slot)
            domain = (
                compact(p, counts[0]) * distinct[1] + compact(q, counts[1])
            ) * distinct[2] + compact(r, counts[2])
            key = ((domain * (SUB * LANES) + member) << KEY_BITS) + (slot << GROUP_BITS) + a
            keys.append(key.astype(jnp.float32))
    size = len(keys)
    sublane = lax.broadcasted_iota(jnp.int32, (SUB, LANES), 0)

    def turned(values, bit):
        sign = jnp.where((sublane >> bit) & 1 == 1, -1.0, 1.0)
        return [value * sign for value in values]

    def by_sublane(values):
        for v in range(size):
            spread_ref[pl.ds(v, SUB, stride=size), :] = values[v]
        return [spread_ref[n * SUB : (n + 1) * SUB, :] for n in range(size)]

    def by_register(values):
        for n in range(size):
            spread_ref[n * SUB : (n + 1) * SUB, :] = values[n]
        return [spread_ref[pl.ds(v, SUB, stride=size), :] for v in range(size)]

    def exchange(values, i, j, up=True):
        low, high = jnp.minimum(values[i], values[j]), jnp.maximum(values[i], values[j])
        values[i], values[j] = (low, high) if up else (high, low)

    keys = turned(keys, 0)
    for i, j in network(size):
        exchange(keys, i, j)
    keys = turned(keys, 0)
    run = size // SUB
    for level in range(1, 4):
        keys = by_sublane(keys)
        for step in reversed(range(level)):
            for s in range(SUB):
                if not s >> step & 1:
                    for n in range(run):
                        exchange(
                            keys,
                            s * run + n,
                            (s | 1 << step) * run + n,
                            level == 3 or not s >> level & 1,
                        )
        keys = by_register(keys)
        if level < 3:
            keys = turned(keys, level)
        stride = size // 2
        while stride:
            for v in range(size):
                if not v & stride:
                    exchange(keys, v, v | stride)
            stride //= 2
        if level < 3:
            keys = turned(keys, level)

    whole = [key.astype(jnp.int32) for key in keys]
    for v in range(size):
        keys_ref[v] = whole[v]
    base = sublane * domains
    lows = [(whole[v] >> (KEY_BITS + 7)) - base for v in range(0, size, BATCH)]
    highs = [(whole[v + BATCH - 1] >> (KEY_BITS + 7)) - base for v in range(0, size, BATCH)]
    least = jnp.concatenate(
        [jnp.min(low.astype(jnp.float32), axis=0, keepdims=True) for low in lows], axis=0
    )
    most = jnp.concatenate(
        [jnp.max(high.astype(jnp.float32), axis=0, keepdims=True) for high in highs], axis=0
    )
    least = jnp.min(least, axis=1, keepdims=True)
    most = jnp.max(most, axis=1, keepdims=True)
    both = jnp.concatenate([least, most], axis=0).astype(jnp.int32)
    range_ref[...] = jnp.broadcast_to(both, range_ref.shape)


def sorting(counts, lists):
    entries = lists.shape[1]
    return pl.pallas_call(
        functools.partial(sorting_kernel, counts),
        out_shape=(
            jax.ShapeDtypeStruct((entries, SUB, LANES), jnp.int32),
            jax.ShapeDtypeStruct((2 * entries // BATCH, LANES), jnp.int32),
        ),
        in_specs=[pl.BlockSpec(memory_space=pltpu.MemorySpace.HBM)],
        out_specs=(pl.BlockSpec(memory_space=VMEM),) * 2,
        scratch_shapes=[
            pltpu.VMEM((entries * SUB, LANES), jnp.float32),
            pltpu.VMEM(lists.shape, jnp.int32),
            pltpu.SemaphoreType.DMA,
        ],
        cost_estimate=pl.CostEstimate(flops=10**7, bytes_accessed=5 * 10**6, transcendentals=0),
        compiler_params=pltpu.CompilerParams(vmem_limit_bytes=GRANT),
        name="sorting",
    )(*in_place(lists))


def pair_kernel(
    domains, first, last, range_ref, keys_ref, own_ref, packed_ref, scale_ref, start_ref, force_ref
):
    blocks = keys_ref.shape[0] // BATCH
    front = (SUB - 1) * domains
    base = lax.broadcasted_iota(jnp.int32, (SUB, LANES), 0) * domains

    def step(j, sums):
        keys = [keys_ref[j * BATCH + i] for i in range(BATCH)]
        rows = [(key >> (KEY_BITS + 7)) - base for key in keys]
        lanes = [(key >> KEY_BITS) & (LANES - 1) for key in keys]
        low = range_ref[j, 0]
        rounds = (range_ref[blocks + j, 0] - low) // CHUNK + 1

        def scan(i, words):
            words = list(words)
            start = low + i * CHUNK
            for m in range(BATCH):
                for u in range(CHUNK):
                    here = rows[m] == start + u
                    for w in range(2):
                        lines = packed_ref[w, pl.ds(front + start + u, SUB, stride=domains), :]
                        k = 2 * m + w
                        words[k] = jnp.where(here, pick_lanes(lines, lanes[m]), words[k])
            return tuple(words)

        zero = jnp.zeros((SUB, LANES), jnp.int32)
        words = lax.fori_loop(0, rounds, scan, (zero,) * (2 * BATCH))
        sums = list(sums)
        for m in range(BATCH):
            group = keys[m] & ((1 << GROUP_BITS) - 1)
            places = places_of((keys[m] >> GROUP_BITS) & 31)
            mine = [group == g for g in range(SUB)]
            one, two = words[2 * m], words[2 * m + 1]
            code = [one & 0xFFFF, (one >> 16) & 0xFFFF, two & 0xFFFF, (two >> 16) & 0xFFFF]
            value = [code[c].astype(jnp.float32) * scale_ref[4 + c] + scale_ref[c] for c in range(4)]
            offset = []
            for c in range(3):
                place = own_ref[c, 0:1, :]
                for g in range(1, SUB):
                    place = jnp.where(mine[g], own_ref[c, g : g + 1, :], place)
                shift = (places[c] - 1).astype(jnp.float32) * domain_edge
                offset.append(place - (value[c] + shift))
            distance = (
                offset[0] * offset[0] + offset[1] * offset[1] + offset[2] * offset[2] + soften
            )
            inverse = lax.rsqrt(distance)
            strength = value[3] * (inverse * inverse * inverse)
            for c in range(3):
                push = offset[c] * strength
                for g in range(SUB):
                    k = c * SUB + g
                    sums[k] = sums[k] + jnp.where(mine[g], push, 0.0)
        return tuple(sums)

    zero = jnp.zeros((SUB, LANES), jnp.float32)
    sums = lax.fori_loop(first, last, step, (zero,) * (3 * SUB))
    for c in range(3):
        total = jnp.concatenate(
            [jnp.sum(sums[c * SUB + g], axis=0, keepdims=True) for g in range(SUB)], axis=0
        )
        force_ref[c] = start_ref[c] + coulomb * own_ref[3] * total


def pair_forces(first, last, ranges, keys, own, packed, scale, start):
    return pl.pallas_call(
        functools.partial(pair_kernel, (packed.shape[1] - CHUNK) // (3 * SUB - 2), first, last),
        out_shape=jax.ShapeDtypeStruct((3, SUB, LANES), jnp.float32),
        in_specs=[pl.BlockSpec(memory_space=SMEM)] + [pl.BlockSpec(memory_space=VMEM)] * 5,
        out_specs=pl.BlockSpec(memory_space=VMEM),
        cost_estimate=pl.CostEstimate(
            flops=10**7, bytes_accessed=(last - first) * BATCH * 10**5 * 3, transcendentals=0
        ),
        compiler_params=pltpu.CompilerParams(vmem_limit_bytes=GRANT),
        name="pairs",
    )(ranges, keys, own, packed, scale, start)


def neighbourhood(counts, along_rows):
    reach = [(-1, 0, 1) if n >= 3 else (0, 1) if n == 2 else (0,) for n in counts]
    mine = jnp.stack([along_rows[(-i) % counts[0]] for i in reach[0]])
    columns, layers = counts[1:]
    near = []
    for j in reach[1]:
        for k in reach[2]:
            if (j, k) == (0, 0):
                near.append(mine)
                continue
            pairs = [
                (((c + j) % columns) * layers + (g + k) % layers, c * layers + g)
                for c in range(columns)
                for g in range(layers)
            ]
            near.append(lax.ppermute(mine, ("qc", "grp"), pairs))
    return near


def crossed(value, axis):
    count = lax.axis_size(axis)
    if count & (count - 1):
        return rotated(value, axis), [lambda me, k=k: modulo(me - k, count) for k in range(count)]
    return (
        [value]
        + [lax.ppermute(value, axis, [(i, i ^ k) for i in range(count)]) for k in range(1, count)],
        [lambda me, k=k: me ^ k for k in range(count)],
    )


def per_device(
    kohn_sham, pattern, basis_centers, occupations, atoms, neighbours, emb_atom, emb_dest, emb_block
):
    counts = tuple(lax.axis_size(axis) for axis in ALL)
    layers = counts[2]
    order = kohn_sham.shape[0]
    width = order // layers
    record_count = emb_atom.shape[0]
    own = atoms.reshape(4, SUB, LANES)
    after = lax.optimization_barrier

    left_own, right_own, packet, basis, pattern, *records = prepare(
        width,
        kohn_sham,
        own,
        basis_centers,
        occupations,
        pattern,
        emb_atom.reshape(1, record_count),
        emb_dest.reshape(1, record_count),
        emb_block.reshape(1, record_count),
    )
    near_row = [min(k, counts[0] - k) <= 1 for k in range(counts[0])]
    packets = rotated(lambda k: packet if near_row[k] else basis, "qr")
    rights = rotated(right_own, "qr")
    lefts, places = crossed(left_own, "qc")
    field, embed_force = embedding(
        order,
        counts[0] * counts[1] * counts[2],
        packets,
        [4 if close else 0 for close in near_row],
        *records,
    )
    field_all = lax.all_to_all(field, ALL, split_axis=0, concat_axis=0, tiled=True)
    near = neighbourhood(counts, [piece[:4] for piece in packets])

    def from_layers(send):
        if layers == 2:
            return lax.ppermute(send, "grp", [(0, 1), (1, 0)])
        got = lax.all_to_all(
            send.reshape(layers, width, order), "grp", split_axis=0, concat_axis=0, tiled=True
        )
        other = jnp.arange(layers)[:, None, None] != lax.axis_index("grp")
        return jnp.sum(jnp.where(other, got.astype(jnp.float32), 0.0), axis=0)

    send, table = product_send(pattern, lefts, places, rights)
    got = from_layers(send)
    mine = product_own(pattern, table, rights)
    rows, columns = whole_field(field_all)
    product_rows = (mine + got.astype(jnp.float32)).astype(jnp.bfloat16)
    products = rotated(product_rows, "qr")
    lists, product_rows = after((neighbours[0, 0, 0], product_rows))
    keys, ranges = sorting(counts, lists)
    blocks = keys.shape[0] // BATCH
    packed, scale = packing(near)
    product_rows, packed = after((product_rows, packed))
    cut = (5 * blocks + 7) // 8
    force = pair_forces(0, cut, ranges, keys, own, packed, scale, embed_force)
    *received, force = after((*products[1:], force))
    products = [products[0]] + received

    send, squares = cube_send(pattern, table, rows, columns, products, rights)
    got = from_layers(send)
    squares, force = after((squares, force))
    result = cube_own(pattern, table, squares, columns, right_own)
    force = pair_forces(cut, blocks, ranges, keys, own, packed, scale, force)
    got, force, result = after((got, force, result))
    sign_step = final_step(result, got)
    return (sign_step, force.reshape(3, 1, 1, 1, SUB * LANES))


def solution(mesh):
    in_specs = (
        P("qr", "qc"),
        P("qr", "qc"),
        P(None, "qr"),
        P("qr"),
        P(None, "qr", "qc", "grp", None),
        P("qr", "qc", "grp", None, None, None),
        P(("qr", "qc", "grp")),
        P(("qr", "qc", "grp"), None),
        P(("qr", "qc", "grp")),
    )
    out_specs = (P(("qr", "grp"), "qc"), P(None, "qr", "qc", "grp", None))

    return jax.shard_map(
        per_device, mesh=mesh, in_specs=in_specs, out_specs=out_specs, check_vma=False
    )
```

```python
import functools

import jax
import jax.numpy as jnp
from jax import lax
from jax.experimental import pallas as pl
from jax.experimental.pallas import tpu as pltpu
from jax.sharding import PartitionSpec as P


BLOCK = 64
SUB, LANES = 8, 128

coulomb = 138.935
hartree_nm = 0.0529177
soften = 0.01
domain_edge = 3.4

ALL = ("qr", "qc", "grp")
VMEM = pltpu.MemorySpace.VMEM
GRANT = 16 << 20
SMEM = pltpu.MemorySpace.SMEM

LANE_PICK = lax.GatherDimensionNumbers(
    offset_dims=(),
    collapsed_slice_dims=(1,),
    start_index_map=(1,),
    operand_batching_dims=(0,),
    start_indices_batching_dims=(0,),
)


def pick_lanes(row, lane):
    return lax.gather(
        row, lane[..., None], LANE_PICK, (1, 1), mode=lax.GatherScatterMode.PROMISE_IN_BOUNDS
    )


def rotated(value, axis):
    count = lax.axis_size(axis)
    of = value if callable(value) else lambda k: value
    return [of(0)] + [
        lax.ppermute(of(k), axis, [(i, (i + k) % count) for i in range(count)])
        for k in range(1, count)
    ]


def in_place(*values):
    return [pltpu.with_memory_space_constraint(value, pltpu.MemorySpace.HBM) for value in values]


def thirds(value):
    high = value.astype(jnp.bfloat16)
    rest = value - high.astype(jnp.float32)
    middle = rest.astype(jnp.bfloat16)
    low = (rest - middle.astype(jnp.float32)).astype(jnp.bfloat16)
    return high, middle, low


def prepare_kernel(count, *refs):
    inputs, (left_ref, right_ref, packet_ref, basis_ref), kept, buffers = (
        refs[:count],
        refs[count : count + 4],
        refs[count + 4 : -4],
        refs[-4:],
    )
    matrix_buf, centers_buf, weights_buf, sems = buffers
    order, width = left_ref.shape
    layer = lax.axis_index("grp")
    targets = [matrix_buf, packet_ref.at[0:4], centers_buf, weights_buf] + list(kept)
    copies = [
        pltpu.make_async_copy(source, target, sems.at[i])
        for i, (source, target) in enumerate(zip(inputs, targets))
    ]
    for copy in copies:
        copy.start()
    copies[2].wait()
    copies[3].wait()
    lines = order // LANES
    rows = [
        centers_buf[c : c + 1, n * LANES : (n + 1) * LANES] for c in range(3) for n in range(lines)
    ]
    rows = rows + [weights_buf[n * LANES : (n + 1) * LANES].reshape(1, LANES) for n in range(lines)]
    planes = packet_ref.shape[0] - 4
    rows = rows + [jnp.zeros((1, LANES), jnp.float32)] * (planes * SUB - len(rows))
    for n in range(planes):
        basis = jnp.concatenate(rows[n * SUB : (n + 1) * SUB], axis=0)
        packet_ref[4 + n] = basis
        basis_ref[n] = basis
    copies[0].wait()
    right_ref[...] = matrix_buf[pl.ds(pl.multiple_of(layer * width, width), width), :]
    for i in range(order // width):

        @pl.when(layer == i)
        def _():
            left_ref[...] = matrix_buf[:, i * width : (i + 1) * width]

    for copy in copies[1:2] + copies[4:]:
        copy.wait()


def prepare(width, matrix, atoms, centers, weights, *kept):
    order = matrix.shape[0]
    planes = -(-4 * (order // LANES) // SUB)
    inputs = (matrix, atoms, centers, weights) + kept
    return pl.pallas_call(
        functools.partial(prepare_kernel, len(inputs)),
        out_shape=(
            jax.ShapeDtypeStruct((order, width), matrix.dtype),
            jax.ShapeDtypeStruct((width, order), matrix.dtype),
            jax.ShapeDtypeStruct((4 + planes, SUB, LANES), jnp.float32),
            jax.ShapeDtypeStruct((planes, SUB, LANES), jnp.float32),
        )
        + tuple(jax.ShapeDtypeStruct(value.shape, value.dtype) for value in kept),
        in_specs=[pl.BlockSpec(memory_space=pltpu.MemorySpace.HBM)] * len(inputs),
        out_specs=(pl.BlockSpec(memory_space=VMEM),) * (4 + len(kept)),
        scratch_shapes=[
            pltpu.VMEM(matrix.shape, matrix.dtype),
            pltpu.VMEM(centers.shape, centers.dtype),
            pltpu.VMEM(weights.shape, weights.dtype),
            pltpu.SemaphoreType.DMA((len(inputs),)),
        ],
        cost_estimate=pl.CostEstimate(flops=10**6, bytes_accessed=10**6, transcendentals=0),
        compiler_params=pltpu.CompilerParams(vmem_limit_bytes=GRANT),
        name="prepare",
    )(*in_place(*inputs))


def records_kernel(extent, lines, offsets, *refs):
    packet_refs = refs[:extent]
    pick_ref, dest_ref, block_ref, field_ref, force_ref = refs[extent:]
    count = pick_ref.shape[1]
    here = [lax.axis_index(axis) for axis in ALL]
    anchor = [place.astype(jnp.float32) * domain_edge for place in here]
    pick, dest, block = pick_ref[...], dest_ref[...], block_ref[...]
    lane, group = pick & (LANES - 1), pick >> 7
    behind = here[0] - dest
    behind = jnp.where(behind < 0, behind + extent, behind)
    iota = functools.partial(lax.broadcasted_iota, jnp.int32)
    one_lane = (iota((LANES, count), 0) == lane).astype(jnp.bfloat16)
    in_group = iota((SUB, count), 0) == group
    half = block >> 1
    odd = (block & 1) == 1
    one_line = (iota((extent * lines, count), 0) == behind * lines + half).astype(jnp.bfloat16)
    one_out = (iota((extent * lines, count), 0) == dest * lines + half).astype(jnp.bfloat16)

    def exact(product, value):
        high, middle, low = thirds(value)
        return product(high) + product(middle) + product(low)

    def dot(contract):
        return lambda other: lambda value: lax.dot_general(
            value, other, (contract, ((), ())), preferred_element_type=jnp.float32
        )

    own = packet_refs[0]
    atoms = jnp.concatenate([own[c] for c in range(4)], axis=0)
    spread = exact(dot(((1,), (0,)))(one_lane), atoms)
    taken = [
        jnp.sum(jnp.where(in_group, spread[c * SUB : (c + 1) * SUB], 0.0), axis=0, keepdims=True)
        for c in range(4)
    ]

    def line(k, n):
        return packet_refs[k][offsets[k] + n // SUB, n % SUB : n % SUB + 1, :]

    def chosen(c):
        table = jnp.concatenate(
            [line(k, c * lines + n) for k in range(extent) for n in range(lines)], axis=0
        )
        both = exact(dot(((0,), (0,)))(one_line), table)
        return jnp.where(odd, both[BLOCK:], both[:BLOCK])

    charge = taken[3]
    offset = [taken[c] + anchor[c] - chosen(c) for c in range(3)]
    weight = chosen(3)
    distance = offset[0] * offset[0] + offset[1] * offset[1] + offset[2] * offset[2] + soften
    inverse = lax.rsqrt(distance)
    terms = hartree_nm * charge * inverse
    terms = jnp.concatenate([jnp.where(odd, 0.0, terms), jnp.where(odd, terms, 0.0)], axis=0)
    high, middle, low = thirds(terms)
    field = sum(
        lax.dot_general(one_out, piece, (((1,), (1,)), ((), ())), preferred_element_type=jnp.float32)
        for piece in (high, middle, low)
    )
    field = jnp.concatenate(
        [
            jnp.concatenate([field[r * lines + n : r * lines + n + 1] for n in range(lines)], axis=1)
            for r in range(extent)
        ],
        axis=0,
    ).astype(field_ref.dtype)
    for device in range(field_ref.shape[0]):
        field_ref[device] = field
    strength = weight * (inverse * inverse * inverse)
    pushes = [
        coulomb * charge * jnp.sum(strength * offset[c], axis=0, keepdims=True) for c in range(3)
    ]
    pushes = jnp.concatenate([jnp.where(in_group, push, 0.0) for push in pushes], axis=0)
    total = exact(dot(((1,), (1,)))(one_lane), pushes)
    for c in range(3):
        force_ref[c] = total[c * SUB : (c + 1) * SUB]


def embedding(order, devices, packets, offsets, pick, dest, block):
    extent, lines = len(packets), order // LANES
    return in_vmem(
        functools.partial(records_kernel, extent, lines, offsets),
        (
            jax.ShapeDtypeStruct((devices, extent, order), jnp.bfloat16),
            jax.ShapeDtypeStruct((3, SUB, LANES), jnp.float32),
        ),
        *packets,
        pick,
        dest,
        block,
    )


def field_kernel(parts_ref, rows_ref, columns_ref):
    devices, extent, order = parts_ref.shape
    total = parts_ref[0].astype(jnp.float32)
    for k in range(1, devices):
        total = total + parts_ref[k].astype(jnp.float32)
    lines = order // LANES
    for r in range(extent):
        for n in range(lines):
            line = total[r : r + 1, n * LANES : (n + 1) * LANES]
            k = r * lines + n
            rows_ref[k : k + 1, :] = line
            columns_ref[k * LANES : (k + 1) * LANES, :] = jnp.broadcast_to(line, (LANES, LANES)).T


def whole_field(parts):
    _, extent, order = parts.shape
    size = extent * order
    return in_vmem(
        field_kernel,
        (
            jax.ShapeDtypeStruct((size // LANES, LANES), jnp.float32),
            jax.ShapeDtypeStruct((size, LANES), jnp.float32),
        ),
        parts,
    )


def modulo(value, count):
    return jnp.where(value < 0, value + count, value)


def keep_pattern(pattern_ref, first, value):
    rows, order, blocks = value.shape[0], value.shape[1], pattern_ref.shape[0]
    row_block = lax.broadcasted_iota(jnp.int32, (rows, blocks), 0) + first
    below = (
        row_block // BLOCK == lax.broadcasted_iota(jnp.int32, (rows, blocks), 1)
    ).astype(jnp.bfloat16)
    across = (
        lax.broadcasted_iota(jnp.int32, (order, blocks), 0) // BLOCK
        == lax.broadcasted_iota(jnp.int32, (order, blocks), 1)
    ).astype(jnp.bfloat16)
    marks = (pattern_ref[...] == 1).astype(jnp.float32).astype(jnp.bfloat16)
    wide = jnp.dot(below, marks, preferred_element_type=jnp.float32).astype(jnp.bfloat16)
    keep = lax.dot_general(wide, across, (((1,), (1,)), ((), ())), preferred_element_type=jnp.float32)
    return jnp.where(keep > 0.5, value, 0.0)


def sent_rows(order, width):
    return width if order == 2 * width else order


def first_row(order, width, sent):
    layer = lax.axis_index("grp")
    if not sent:
        return pl.multiple_of(layer * width, width)
    return pl.multiple_of((1 - layer) * width, width) if order == 2 * width else 0


def row_product(table_ref, tiles, right_refs, first, rows):
    total = jnp.zeros((rows, right_refs[0].shape[-1]), jnp.float32)
    for tile, right_ref in zip(tiles, right_refs):
        total = total + jnp.dot(
            table_ref[tile, pl.ds(first, rows), :],
            right_ref[...],
            preferred_element_type=jnp.float32,
        )
    return total


def tiles_behind(extent):
    row = lax.axis_index("qr")
    return [modulo(row - k, extent) for k in range(extent)]


def product_send_kernel(places, pattern_ref, *refs):
    left_refs, right_refs, (send_ref, table_ref) = refs[: len(places)], refs[len(places) : -2], refs[-2:]
    column = lax.axis_index("qc")
    for left_ref, place in zip(left_refs, places):
        table_ref[place(column)] = left_ref[...]
    _, order, width = table_ref.shape
    rows = sent_rows(order, width)
    first = first_row(order, width, True)
    value = row_product(table_ref, tiles_behind(len(right_refs)), right_refs, first, rows)
    send_ref[...] = keep_pattern(pattern_ref, first, value).astype(send_ref.dtype)


def product_own_kernel(pattern_ref, table_ref, *refs):
    right_refs, own_ref = refs[:-1], refs[-1]
    _, order, width = table_ref.shape
    first = first_row(order, width, False)
    value = row_product(table_ref, tiles_behind(len(right_refs)), right_refs, first, width)
    own_ref[...] = keep_pattern(pattern_ref, first, value)


def in_vmem(kernel, out_shape, *values, work=10**6):
    return pl.pallas_call(
        kernel,
        out_shape=out_shape,
        in_specs=[pl.BlockSpec(memory_space=VMEM)] * len(values),
        out_specs=jax.tree.map(lambda _: pl.BlockSpec(memory_space=VMEM), out_shape),
        cost_estimate=pl.CostEstimate(flops=work, bytes_accessed=work, transcendentals=0),
        compiler_params=pltpu.CompilerParams(vmem_limit_bytes=GRANT),
    )(*values)


def product_send(pattern, lefts, places, rights):
    order, width = lefts[0].shape
    return in_vmem(
        functools.partial(product_send_kernel, places),
        (
            jax.ShapeDtypeStruct((sent_rows(order, width), order), jnp.bfloat16),
            jax.ShapeDtypeStruct((len(lefts), order, width), jnp.bfloat16),
        ),
        pattern,
        *lefts,
        *rights,
    )


def product_own(pattern, table, rights):
    _, order, width = table.shape
    out = jax.ShapeDtypeStruct((width, order), jnp.float32)
    return in_vmem(product_own_kernel, out, pattern, table, *rights)


def cube_send_kernel(pattern_ref, table_ref, rows_ref, columns_ref, *refs):
    extent = (len(refs) - 2) // 2
    product_refs, right_refs = refs[:extent], refs[extent : 2 * extent]
    send_ref, square_ref = refs[2 * extent :]
    _, order, width = table_ref.shape
    lines = order // LANES
    column, layer = lax.axis_index("qc"), lax.axis_index("grp")
    start = layer * width
    iota = functools.partial(lax.broadcasted_iota, jnp.int32)
    tiles = tiles_behind(extent)
    for k, tile in enumerate(tiles):
        down = columns_ref[pl.ds(pl.multiple_of(tile * order + start, width), width), :]
        for n in range(lines):
            spot = slice(n * LANES, (n + 1) * LANES)
            across = rows_ref[pl.ds(column * lines + n, 1), :]
            matrix = right_refs[k][:, spot].astype(jnp.float32)
            on_diagonal = iota((width, LANES), 0) + start == iota((width, LANES), 1) + n * LANES
            corner = jnp.where(on_diagonal & (tile == column), down * down, 0.0)
            piece = product_refs[k][:, spot].astype(jnp.float32) + matrix * (down + across) + corner
            square_ref[k, :, spot] = piece.astype(jnp.bfloat16)
    rows = sent_rows(order, width)
    first = first_row(order, width, True)
    squares = [square_ref.at[k] for k in range(extent)]
    value = row_product(table_ref, tiles, squares, first, rows)
    send_ref[...] = keep_pattern(pattern_ref, first, value).astype(send_ref.dtype)


def cube_send(pattern, table, rows, columns, products, rights):
    extent, (_, order, width) = len(rights), table.shape
    return in_vmem(
        cube_send_kernel,
        (
            jax.ShapeDtypeStruct((sent_rows(order, width), order), jnp.bfloat16),
            jax.ShapeDtypeStruct((extent, width, order), jnp.bfloat16),
        ),
        pattern,
        table,
        rows,
        columns,
        *products,
        *rights,
    )


def cube_own_kernel(pattern_ref, table_ref, square_ref, columns_ref, right_ref, out_ref):
    extent, width, order = square_ref.shape
    row, column = lax.axis_index("qr"), lax.axis_index("qc")
    first = first_row(order, width, False)
    down = columns_ref[pl.ds(pl.multiple_of(row * order + first, width), width), :]
    iota = functools.partial(lax.broadcasted_iota, jnp.int32)
    parts = []
    for start in range(0, width, LANES):
        size = min(LANES, width - start)
        on_diagonal = iota((width, size), 0) == iota((width, size), 1) + start
        parts.append(jnp.where(on_diagonal, down[:, :size], 0.0))
    added = parts[0] if len(parts) == 1 else jnp.concatenate(parts, axis=1)
    value = jnp.zeros((width, order), jnp.float32)
    for k, tile in enumerate(tiles_behind(extent)):
        operand = table_ref[tile, pl.ds(first, width), :]
        if k == 0:
            operand = (operand.astype(jnp.float32) + added).astype(jnp.bfloat16)
        value = value + jnp.dot(operand, square_ref[k], preferred_element_type=jnp.float32)
    value = keep_pattern(pattern_ref, first, value)
    for n in range(order // LANES):
        spot = slice(n * LANES, (n + 1) * LANES)
        on_diagonal = iota((width, LANES), 0) + first == iota((width, LANES), 1) + n * LANES
        diagonal = jnp.where(on_diagonal & (row == column), down, 0.0)
        shifted = (right_ref[:, spot].astype(jnp.float32) + diagonal).astype(jnp.bfloat16)
        out_ref[:, spot] = 0.5 * (3.0 * shifted.astype(jnp.float32) - value[:, spot])


def cube_own(pattern, table, squares, columns, right):
    _, width, order = squares.shape
    out = jax.ShapeDtypeStruct((width, order), jnp.float32)
    return in_vmem(cube_own_kernel, out, pattern, table, squares, columns, right)


def final_kernel(own_ref, got_ref, out_ref):
    out_ref[...] = (own_ref[...] - 0.5 * got_ref[...].astype(jnp.float32)).astype(out_ref.dtype)


def final_step(own, got):
    return in_vmem(final_kernel, jax.ShapeDtypeStruct(own.shape, jnp.bfloat16), own, got)


KEY_BITS = 8
GROUP_BITS = 3
BATCH = 4
CHUNK = 24


def packing_kernel(layers, inner, *refs):
    *near_refs, packed_ref, scale_ref = refs
    picks = [
        (near_ref, k, i) for i in range(inner) for near_ref in near_refs for k in range(layers)
    ]
    domains = len(picks)

    def entry(d, c):
        near_ref, k, i = picks[d]
        return near_ref[k, i, c]

    low = [entry(0, c) for c in range(4)]
    high = list(low)
    for d in range(1, domains):
        for c in range(4):
            value = entry(d, c)
            low[c] = jnp.minimum(low[c], value)
            high[c] = jnp.maximum(high[c], value)
    steps = 65535.0
    base, back = [], []
    for c in range(4):
        least = jnp.min(low[c], axis=(0, 1), keepdims=True)
        width = jnp.maximum(jnp.max(high[c], axis=(0, 1), keepdims=True) - least, 1e-30)
        base.append(jnp.broadcast_to(least, (SUB, LANES)))
        back.append(jnp.broadcast_to(steps / width, (SUB, LANES)))
        scale_ref[c] = base[c]
        scale_ref[4 + c] = jnp.broadcast_to(width * (1.0 / steps), (SUB, LANES))
    for d in range(domains):
        code = [
            jnp.clip((entry(d, c) - base[c]) * back[c] + 0.5, 0.0, steps).astype(jnp.int32)
            for c in range(4)
        ]
        start = (SUB - 1) * domains + d * SUB
        packed_ref[0, start : start + SUB, :] = code[0] | (code[1] << 16)
        packed_ref[1, start : start + SUB, :] = code[2] | (code[3] << 16)
    front, size = (SUB - 1) * domains, domains * SUB
    for w in range(2):
        packed_ref[w, :front, :] = jnp.zeros((front, LANES), jnp.int32)
        packed_ref[w, front + size :, :] = jnp.zeros((front + CHUNK, LANES), jnp.int32)


def packing(near):
    layers, inner = near[0].shape[:2]
    domains = len(near) * layers * inner
    rows = domains * SUB + 2 * (SUB - 1) * domains + CHUNK
    return pl.pallas_call(
        functools.partial(packing_kernel, layers, inner),
        out_shape=(
            jax.ShapeDtypeStruct((2, rows, LANES), jnp.int32),
            jax.ShapeDtypeStruct((8, SUB, LANES), jnp.float32),
        ),
        in_specs=[pl.BlockSpec(memory_space=VMEM)] * len(near),
        out_specs=(pl.BlockSpec(memory_space=VMEM),) * 2,
        cost_estimate=pl.CostEstimate(flops=10**7, bytes_accessed=5 * 10**6, transcendentals=0),
        compiler_params=pltpu.CompilerParams(vmem_limit_bytes=GRANT),
        name="packing",
    )(*near)


def compact(place, count):
    if count >= 3:
        return place
    if count == 2:
        return jnp.where(place == 1, 0, 1)
    return jnp.zeros_like(place)


def places_of(slot):
    p = (slot * 57) >> 9
    rest = slot - 9 * p
    q = (rest * 11) >> 5
    return p, q, rest - 3 * q


def network(count):
    pairs = []
    p = 1
    while p < count:
        k = p
        while k >= 1:
            for j in range(k % p, count - k, 2 * k):
                for i in range(min(k, count - j - k)):
                    if (i + j) // (2 * p) == (i + j + k) // (2 * p):
                        pairs.append((i + j, i + j + k))
            k //= 2
        p *= 2
    return pairs


def sorting_kernel(counts, lists_hbm, keys_ref, range_ref, spread_ref, lists_ref, sem):
    copy = pltpu.make_async_copy(lists_hbm, lists_ref, sem)
    copy.start()
    copy.wait()
    entries = lists_ref.shape[1]
    distinct = [min(3, count) for count in counts]
    domains = distinct[0] * distinct[1] * distinct[2]
    keys = []
    for b in range(entries // SUB):
        for a in range(SUB):
            slot = lists_ref[0, b * SUB : (b + 1) * SUB, a * LANES : (a + 1) * LANES]
            member = lists_ref[1, b * SUB : (b + 1) * SUB, a * LANES : (a + 1) * LANES]
            p, q, r = places_of(slot)
            domain = (
                compact(p, counts[0]) * distinct[1] + compact(q, counts[1])
            ) * distinct[2] + compact(r, counts[2])
            key = ((domain * (SUB * LANES) + member) << KEY_BITS) + (slot << GROUP_BITS) + a
            keys.append(key.astype(jnp.float32))
    size = len(keys)
    sublane = lax.broadcasted_iota(jnp.int32, (SUB, LANES), 0)

    def turned(values, bit):
        sign = jnp.where((sublane >> bit) & 1 == 1, -1.0, 1.0)
        return [value * sign for value in values]

    def by_sublane(values):
        for v in range(size):
            spread_ref[pl.ds(v, SUB, stride=size), :] = values[v]
        return [spread_ref[n * SUB : (n + 1) * SUB, :] for n in range(size)]

    def by_register(values):
        for n in range(size):
            spread_ref[n * SUB : (n + 1) * SUB, :] = values[n]
        return [spread_ref[pl.ds(v, SUB, stride=size), :] for v in range(size)]

    def exchange(values, i, j, up=True):
        low, high = jnp.minimum(values[i], values[j]), jnp.maximum(values[i], values[j])
        values[i], values[j] = (low, high) if up else (high, low)

    keys = turned(keys, 0)
    for i, j in network(size):
        exchange(keys, i, j)
    keys = turned(keys, 0)
    run = size // SUB
    for level in range(1, 4):
        keys = by_sublane(keys)
        for step in reversed(range(level)):
            for s in range(SUB):
                if not s >> step & 1:
                    for n in range(run):
                        exchange(
                            keys,
                            s * run + n,
                            (s | 1 << step) * run + n,
                            level == 3 or not s >> level & 1,
                        )
        keys = by_register(keys)
        if level < 3:
            keys = turned(keys, level)
        stride = size // 2
        while stride:
            for v in range(size):
                if not v & stride:
                    exchange(keys, v, v | stride)
            stride //= 2
        if level < 3:
            keys = turned(keys, level)

    whole = [key.astype(jnp.int32) for key in keys]
    for v in range(size):
        keys_ref[v] = whole[v]
    base = sublane * domains
    lows = [(whole[v] >> (KEY_BITS + 7)) - base for v in range(0, size, BATCH)]
    highs = [(whole[v + BATCH - 1] >> (KEY_BITS + 7)) - base for v in range(0, size, BATCH)]
    least = jnp.concatenate(
        [jnp.min(low.astype(jnp.float32), axis=0, keepdims=True) for low in lows], axis=0
    )
    most = jnp.concatenate(
        [jnp.max(high.astype(jnp.float32), axis=0, keepdims=True) for high in highs], axis=0
    )
    least = jnp.min(least, axis=1, keepdims=True)
    most = jnp.max(most, axis=1, keepdims=True)
    both = jnp.concatenate([least, most], axis=0).astype(jnp.int32)
    range_ref[...] = jnp.broadcast_to(both, range_ref.shape)


def sorting(counts, lists):
    entries = lists.shape[1]
    return pl.pallas_call(
        functools.partial(sorting_kernel, counts),
        out_shape=(
            jax.ShapeDtypeStruct((entries, SUB, LANES), jnp.int32),
            jax.ShapeDtypeStruct((2 * entries // BATCH, LANES), jnp.int32),
        ),
        in_specs=[pl.BlockSpec(memory_space=pltpu.MemorySpace.HBM)],
        out_specs=(pl.BlockSpec(memory_space=VMEM),) * 2,
        scratch_shapes=[
            pltpu.VMEM((entries * SUB, LANES), jnp.float32),
            pltpu.VMEM(lists.shape, jnp.int32),
            pltpu.SemaphoreType.DMA,
        ],
        cost_estimate=pl.CostEstimate(flops=10**7, bytes_accessed=5 * 10**6, transcendentals=0),
        compiler_params=pltpu.CompilerParams(vmem_limit_bytes=GRANT),
        name="sorting",
    )(*in_place(lists))


def pair_kernel(
    domains, first, last, range_ref, keys_ref, own_ref, packed_ref, scale_ref, start_ref, force_ref
):
    blocks = keys_ref.shape[0] // BATCH
    front = (SUB - 1) * domains
    base = lax.broadcasted_iota(jnp.int32, (SUB, LANES), 0) * domains

    def step(j, sums):
        keys = [keys_ref[j * BATCH + i] for i in range(BATCH)]
        rows = [(key >> (KEY_BITS + 7)) - base for key in keys]
        lanes = [(key >> KEY_BITS) & (LANES - 1) for key in keys]
        low = range_ref[j, 0]
        rounds = (range_ref[blocks + j, 0] - low) // CHUNK + 1

        def scan(i, words):
            words = list(words)
            start = low + i * CHUNK
            for m in range(BATCH):
                for u in range(CHUNK):
                    here = rows[m] == start + u
                    for w in range(2):
                        lines = packed_ref[w, pl.ds(front + start + u, SUB, stride=domains), :]
                        k = 2 * m + w
                        words[k] = jnp.where(here, pick_lanes(lines, lanes[m]), words[k])
            return tuple(words)

        zero = jnp.zeros((SUB, LANES), jnp.int32)
        words = lax.fori_loop(0, rounds, scan, (zero,) * (2 * BATCH))
        sums = list(sums)
        for m in range(BATCH):
            group = keys[m] & ((1 << GROUP_BITS) - 1)
            places = places_of((keys[m] >> GROUP_BITS) & 31)
            mine = [group == g for g in range(SUB)]
            one, two = words[2 * m], words[2 * m + 1]
            code = [one & 0xFFFF, (one >> 16) & 0xFFFF, two & 0xFFFF, (two >> 16) & 0xFFFF]
            value = [code[c].astype(jnp.float32) * scale_ref[4 + c] + scale_ref[c] for c in range(4)]
            offset = []
            for c in range(3):
                place = own_ref[c, 0:1, :]
                for g in range(1, SUB):
                    place = jnp.where(mine[g], own_ref[c, g : g + 1, :], place)
                shift = (places[c] - 1).astype(jnp.float32) * domain_edge
                offset.append(place - (value[c] + shift))
            distance = (
                offset[0] * offset[0] + offset[1] * offset[1] + offset[2] * offset[2] + soften
            )
            inverse = lax.rsqrt(distance)
            strength = value[3] * (inverse * inverse * inverse)
            for c in range(3):
                push = offset[c] * strength
                for g in range(SUB):
                    k = c * SUB + g
                    sums[k] = sums[k] + jnp.where(mine[g], push, 0.0)
        return tuple(sums)

    zero = jnp.zeros((SUB, LANES), jnp.float32)
    sums = lax.fori_loop(first, last, step, (zero,) * (3 * SUB))
    for c in range(3):
        total = jnp.concatenate(
            [jnp.sum(sums[c * SUB + g], axis=0, keepdims=True) for g in range(SUB)], axis=0
        )
        force_ref[c] = start_ref[c] + coulomb * own_ref[3] * total


def pair_forces(first, last, ranges, keys, own, packed, scale, start):
    return pl.pallas_call(
        functools.partial(pair_kernel, (packed.shape[1] - CHUNK) // (3 * SUB - 2), first, last),
        out_shape=jax.ShapeDtypeStruct((3, SUB, LANES), jnp.float32),
        in_specs=[pl.BlockSpec(memory_space=SMEM)] + [pl.BlockSpec(memory_space=VMEM)] * 5,
        out_specs=pl.BlockSpec(memory_space=VMEM),
        cost_estimate=pl.CostEstimate(
            flops=10**7, bytes_accessed=(last - first) * BATCH * 10**5 * 3, transcendentals=0
        ),
        compiler_params=pltpu.CompilerParams(vmem_limit_bytes=GRANT),
        name="pairs",
    )(ranges, keys, own, packed, scale, start)


def widened(value, axis):
    count = lax.axis_size(axis)
    steps = (-1, 0, 1) if count >= 3 else (0, 1) if count == 2 else (0,)
    return [
        lax.ppermute(value, axis, [((a + step) % count, a) for a in range(count)])
        if step
        else value
        for step in steps
    ]


def neighbourhood(counts, along_rows):
    steps = (-1, 0, 1) if counts[0] >= 3 else (0, 1) if counts[0] == 2 else (0,)
    mine = jnp.stack([along_rows[(-i) % counts[0]] for i in steps])
    return widened(jnp.stack(widened(mine, "grp")), "qc")


def crossed(value, axis):
    count = lax.axis_size(axis)
    if count & (count - 1):
        return rotated(value, axis), [lambda me, k=k: modulo(me - k, count) for k in range(count)]
    return (
        [value]
        + [lax.ppermute(value, axis, [(i, i ^ k) for i in range(count)]) for k in range(1, count)],
        [lambda me, k=k: me ^ k for k in range(count)],
    )


def per_device(
    kohn_sham, pattern, basis_centers, occupations, atoms, neighbours, emb_atom, emb_dest, emb_block
):
    counts = tuple(lax.axis_size(axis) for axis in ALL)
    layers = counts[2]
    order = kohn_sham.shape[0]
    width = order // layers
    record_count = emb_atom.shape[0]
    own = atoms.reshape(4, SUB, LANES)
    after = lax.optimization_barrier

    left_own, right_own, packet, basis, pattern, *records = prepare(
        width,
        kohn_sham,
        own,
        basis_centers,
        occupations,
        pattern,
        emb_atom.reshape(1, record_count),
        emb_dest.reshape(1, record_count),
        emb_block.reshape(1, record_count),
    )
    near_row = [min(k, counts[0] - k) <= 1 for k in range(counts[0])]
    packets = rotated(lambda k: packet if near_row[k] else basis, "qr")
    rights = rotated(right_own, "qr")
    lefts, places = crossed(left_own, "qc")
    field, embed_force = embedding(
        order,
        counts[0] * counts[1] * counts[2],
        packets,
        [4 if close else 0 for close in near_row],
        *records,
    )
    field_all = lax.all_to_all(field, ALL, split_axis=0, concat_axis=0, tiled=True)
    near = neighbourhood(counts, [piece[:4] for piece in packets])

    def from_layers(send):
        if layers == 2:
            return lax.ppermute(send, "grp", [(0, 1), (1, 0)])
        got = lax.all_to_all(
            send.reshape(layers, width, order), "grp", split_axis=0, concat_axis=0, tiled=True
        )
        other = jnp.arange(layers)[:, None, None] != lax.axis_index("grp")
        return jnp.sum(jnp.where(other, got.astype(jnp.float32), 0.0), axis=0)

    send, table = product_send(pattern, lefts, places, rights)
    got = from_layers(send)
    mine = product_own(pattern, table, rights)
    rows, columns = whole_field(field_all)
    product_rows = (mine + got.astype(jnp.float32)).astype(jnp.bfloat16)
    products = rotated(product_rows, "qr")
    lists, product_rows = after((neighbours[0, 0, 0], product_rows))
    keys, ranges = sorting(counts, lists)
    blocks = keys.shape[0] // BATCH
    packed, scale = packing(near)
    product_rows, packed = after((product_rows, packed))
    cut = (5 * blocks + 7) // 8
    force = pair_forces(0, cut, ranges, keys, own, packed, scale, embed_force)
    *received, force = after((*products[1:], force))
    products = [products[0]] + received

    send, squares = cube_send(pattern, table, rows, columns, products, rights)
    got = from_layers(send)
    squares, force = after((squares, force))
    result = cube_own(pattern, table, squares, columns, right_own)
    force = pair_forces(cut, blocks, ranges, keys, own, packed, scale, force)
    got, force, result = after((got, force, result))
    sign_step = final_step(result, got)
    return (sign_step, force.reshape(3, 1, 1, 1, SUB * LANES))


def solution(mesh):
    in_specs = (
        P("qr", "qc"),
        P("qr", "qc"),
        P(None, "qr"),
        P("qr"),
        P(None, "qr", "qc", "grp", None),
        P("qr", "qc", "grp", None, None, None),
        P(("qr", "qc", "grp")),
        P(("qr", "qc", "grp"), None),
        P(("qr", "qc", "grp")),
    )
    out_specs = (P(("qr", "grp"), "qc"), P(None, "qr", "qc", "grp", None))

    return jax.shard_map(
        per_device, mesh=mesh, in_specs=in_specs, out_specs=out_specs, check_vma=False
    )
```
